512 devices in a mesh: row: 32 (over z, y_lo), col: 16 (over y_hi, x, core).
Axes of the slice: x: 4, y: 4 (y_hi: 2, y_lo: 2; y = y_hi * 2 + y_lo), z: 16, core: 2. Of those that a mesh axis runs over, the one named last changes fastest.
Arguments:
- coords: int32 [3, 65536], P(None, ('row', 'col')), may hold values from 0 to 60809, as said below
- mode_shapes: bfloat16 [256, 65536], P(None, ('row', 'col')), as said below
- output_shapes: bfloat16 [1048576, 256], P(('row', 'col')), may hold values from -0.375 to 0.375
- response_gain: float32 [2, 256], replicated, may hold values from -4 to 4
Outputs:
- response_power: float32 [1048576], P(('row', 'col'))
- modal_csd: float32 [256, 256], replicated
The draws below stay inside these ranges and needn't reach their ends.
Inputs may be any that keep to these rules, and one draw needn't show every extreme that they name: `coords`: positions of points on an aircraft's skin, numbered in no spatial order. `mode_shapes`: entries are of order 1 / sqrt(65536); each mode has a share of one sign over all nodes.
All inputs are finite; a program needn't handle non-finite values.
Results may differ from the reference program's by a relative error of at most 0.002.
Values may be sent and summed in bfloat16 or wider, within the bound.
A program may use at most 64 MiB of HBM per device.

```python
import math
import jax
import jax.numpy as jnp
import numpy as np
from jax import lax

M = 256
NODES = 65536
CYCLE_NODES = 128
DOFS = 1048576


def draw_mode_shapes(key, part):
    offset_key, noise_key = jax.random.split(key, 2)
    offset = jax.random.uniform(offset_key, (M, 1), jnp.float32, -0.5, 0.5)
    noise_draw = jnp.clip(jax.random.normal(noise_key, (M, NODES), jnp.float32), -4.0, 4.0)
    values = (offset + noise_draw) / jnp.sqrt(jnp.float32(NODES))
    return values.astype(jnp.bfloat16)


def draw_coords(key, part):
    cycle_size = CYCLE_NODES
    cycle_count = NODES // cycle_size
    fine_steps = 16
    step_count = cycle_size * fine_steps
    axial_pitch = 119
    angles = 2.0 * np.pi * np.arange(step_count) / step_count
    outline = 1.0 + 0.06 * np.cos(2.0 * angles) + 0.02 * np.cos(3.0 * angles)
    radius = axial_pitch * cycle_size / (2.0 * np.pi)
    across_table = np.floor(radius * outline * np.cos(angles) + 0.5).astype(np.int32)
    upward_table = np.floor(radius * outline * np.sin(angles) + 0.5).astype(np.int32)
    cycle_place = np.arange(cycle_count) / max(cycle_count - 1, 1)
    taper_shape = 1.0 - 0.25 * np.clip((cycle_place - 0.6) / 0.4, 0.0, 1.0) ** 2
    taper_table = np.floor(4096.0 * taper_shape + 0.5).astype(np.int32)
    offset_ticks = int(np.ceil(1.1 * radius))
    jitter_key, order_key = jax.random.split(key)
    node_index = jnp.arange(NODES, dtype=jnp.int32)
    frame_index = node_index // cycle_size
    slot_index = node_index - frame_index * cycle_size
    jitter = jax.random.randint(jitter_key, (NODES,), -5, 6, jnp.int32)
    position = (slot_index * fine_steps + jitter + step_count) % step_count
    taper_scale = jnp.asarray(taper_table)[frame_index]
    across_x = jnp.asarray(across_table)[position] * taper_scale // 4096 + offset_ticks
    across_y = jnp.asarray(upward_table)[position] * taper_scale // 4096 + offset_ticks
    axial_ticks = frame_index * axial_pitch
    placed = jnp.stack([across_x, across_y, axial_ticks]).astype(jnp.int32)
    node_order = jax.random.permutation(order_key, NODES)
    return placed[:, node_order]


def level_of(stream_key, dims, cuts, smallest, largest):
    loudness, own = 1.0, jax.random.fold_in(stream_key, 6)
    for dim, parts in cuts:
        steps = jnp.exp(jax.random.uniform(jax.random.fold_in(own, dim), (parts,), jnp.float32, smallest / len(cuts), largest / len(cuts)))
        loudness = loudness * jnp.repeat(steps, dims[dim] // parts).reshape([-1 if axis == dim else 1 for axis in range(len(dims))])
    return loudness


def bell_draw(key, shape, width, reach, cuts=(), kind=jnp.bfloat16):
    result = jax.random.normal(key, shape, jnp.float32) * width
    if len(cuts) > 0:
        result = level_of(key, shape, cuts, -0.22, 0.18) * result
    return jnp.clip(result, min=-reach, max=reach).astype(kind)


def setup_inputs(seed: int = 0) -> dict:
    key_list = jax.random.split(jax.random.key(seed), 5)
    coords = draw_coords(jax.random.fold_in(key_list[4], 71), 0)
    mode_shapes = draw_mode_shapes(jax.random.fold_in(key_list[4], 71), 0)
    output_shapes = bell_draw(key_list[2], (DOFS, M), M ** -0.5, 0.375, ((0, 512),))
    response_gain = bell_draw(key_list[3], (2, M), 1.0, 4.0, (), jnp.float32)
    return {"coords": coords, "mode_shapes": mode_shapes, "output_shapes": output_shapes, "response_gain": response_gain}


wave_scale = 0.35 / 64.0

def coherence(left_points, right_points):
    difference = (left_points[:, :, None] - right_points[:, None, :]).astype(jnp.float32)
    squared = lax.optimization_barrier(jnp.sum(difference * difference, axis=0))
    return jnp.sinc(wave_scale * jnp.sqrt(squared)).astype(jnp.bfloat16)

def reference(coords, mode_shapes, output_shapes, response_gain):
    node_total = coords.shape[1]
    mode_count = mode_shapes.shape[0]
    block_size = math.gcd(node_total, 512)
    block_count = node_total // block_size
    shapes_wide = mode_shapes.astype(jnp.float32)

    def one_block(block_start):
        block_points = lax.dynamic_slice_in_dim(coords, block_start, block_size, 1)
        coherence_tile = coherence(coords, block_points).astype(jnp.float32)
        return jnp.dot(shapes_wide, coherence_tile, precision=lax.Precision.HIGHEST)
    block_starts = (jnp.arange(block_count) * block_size).astype(jnp.int32)
    blocks = lax.map(one_block, block_starts)
    projection = jnp.transpose(blocks, (1, 0, 2)).reshape(mode_count, node_total)
    modal_csd = lax.dot_general(shapes_wide, projection, (((1,), (1,)), ((), ())), precision=lax.Precision.HIGHEST)
    real_part = response_gain[0]
    imag_part = response_gain[1]
    weighted = (real_part[:, None] * real_part[None, :] + imag_part[:, None] * imag_part[None, :]) * modal_csd
    outputs_wide = output_shapes.astype(jnp.float32)
    mapped = jnp.dot(outputs_wide, weighted, precision=lax.Precision.HIGHEST)
    response_power = lax.optimization_barrier(jnp.sum(mapped * outputs_wide, axis=1))
    return (response_power, modal_csd)
```

```python
import jax
import jax.numpy as jnp
from jax import lax
from jax.sharding import PartitionSpec as P

wave_scale = 0.35 / 64.0


def coherence(left_points, right_points):
    difference = left_points[:, :, None] - right_points[:, None, :]
    squared = jnp.sum(difference * difference, axis=0)
    return jnp.sinc(wave_scale * jnp.sqrt(squared)).astype(jnp.bfloat16)


def split_parts(matrix):
    high_part = matrix.astype(jnp.bfloat16)
    low_part = (matrix - high_part.astype(jnp.float32)).astype(jnp.bfloat16)
    return (high_part, low_part)


def pack_block(coords, mode_shapes):
    wide = coords.astype(jnp.float32)
    high = jnp.floor(wide * (1.0 / 256.0))
    low = wide - 256.0 * high
    pad = jnp.zeros((2, wide.shape[1]), jnp.float32)
    extra = jnp.concatenate([high, low, pad], axis=0).astype(jnp.bfloat16)
    return jnp.concatenate([mode_shapes, extra], axis=0)


def unpack_points(packed, mode_count):
    high = packed[..., mode_count:mode_count + 3, :].astype(jnp.float32)
    low = packed[..., mode_count + 3:mode_count + 6, :].astype(jnp.float32)
    return high * 256.0 + low


def gather_all(block, axis, count):
    spread = jnp.broadcast_to(block[None], (count,) + block.shape)
    return lax.all_to_all(spread, axis, 0, 0, tiled=True)


def all_reduce(matrix, rows, cols):
    flat = matrix.reshape(cols, -1)
    part = lax.all_to_all(flat, "col", 0, 0, tiled=True).reshape(cols, -1).sum(0)
    part = part.reshape(rows, -1)
    part = lax.all_to_all(part, "row", 0, 0, tiled=True).reshape(rows, -1).sum(0)
    whole = gather_all(part, "row", rows).reshape(-1)
    whole = gather_all(whole, "col", cols).reshape(-1)
    return whole.reshape(matrix.shape)


def local(coords, mode_shapes, output_shapes, response_gain):
    rows = lax.axis_size("row")
    cols = lax.axis_size("col")
    mode_count, block_nodes = mode_shapes.shape
    packed = pack_block(coords, mode_shapes)
    row_packed = gather_all(packed, "col", cols)
    col_packed = gather_all(packed, "row", rows)
    row_shapes = jnp.transpose(row_packed[:, :mode_count, :], (1, 0, 2)).reshape(mode_count, -1)
    row_points = jnp.transpose(unpack_points(row_packed, mode_count), (1, 0, 2)).reshape(3, -1)

    half = rows // 2
    me = lax.axis_index("row")
    order = (me + jnp.arange(half + 1)) % rows
    chosen = jnp.take(col_packed, order, axis=0)
    weights = jnp.where((jnp.arange(half + 1) == 0) | (jnp.arange(half + 1) == half), 0.5, 1.0)
    piece_shapes = (chosen[:, :mode_count, :] * weights[:, None, None].astype(jnp.bfloat16))
    piece_points = unpack_points(chosen, mode_count)

    def add_block(loop_index, running_sum):
        part_shapes = lax.dynamic_index_in_dim(piece_shapes, loop_index, 0, keepdims=False)
        part_points = lax.dynamic_index_in_dim(piece_points, loop_index, 0, keepdims=False)
        coherence_tile = coherence(part_points, row_points)
        return running_sum + jnp.dot(part_shapes, coherence_tile, preferred_element_type=jnp.float32)

    zero_block = jnp.zeros((mode_count, row_points.shape[1]), jnp.float32)
    projection = lax.fori_loop(0, half + 1, add_block, zero_block)
    high_part, low_part = split_parts(projection)
    dims = (((1,), (1,)), ((), ()))
    partial = lax.dot_general(row_shapes, high_part, dims, preferred_element_type=jnp.float32)
    partial = partial + lax.dot_general(row_shapes, low_part, dims, preferred_element_type=jnp.float32)
    total = all_reduce(partial, rows, cols)
    modal_csd = total + total.T
    real_part = response_gain[0]
    imag_part = response_gain[1]
    weighted = (
        real_part[:, None] * real_part[None, :] + imag_part[:, None] * imag_part[None, :]
    ) * modal_csd
    weighted_high, weighted_low = split_parts(weighted)
    mapped = jnp.dot(output_shapes, weighted_high, preferred_element_type=jnp.float32)
    mapped = mapped + jnp.dot(output_shapes, weighted_low, preferred_element_type=jnp.float32)
    response_power = jnp.sum(mapped * output_shapes.astype(jnp.float32), axis=1)
    return (response_power, modal_csd)


def solution(mesh):
    in_specs = (P(None, ("row", "col")), P(None, ("row", "col")), P(("row", "col"), None), P())
    out_specs = (P(("row", "col")), P())
    return jax.shard_map(local, mesh=mesh, in_specs=in_specs, out_specs=out_specs, check_vma=False)
```

```python
import jax
import jax.numpy as jnp
from jax import lax
from jax.sharding import PartitionSpec as P

wave_scale = 0.35 / 64.0


def coherence(left_points, right_points):
    difference = left_points[:, :, None] - right_points[:, None, :]
    squared = jnp.sum(difference * difference, axis=0)
    return jnp.sinc(wave_scale * jnp.sqrt(squared)).astype(jnp.bfloat16)


def split_parts(matrix):
    high_part = matrix.astype(jnp.bfloat16)
    low_part = (matrix - high_part.astype(jnp.float32)).astype(jnp.bfloat16)
    return (high_part, low_part)


def pack_block(coords, mode_shapes):
    wide = coords.astype(jnp.float32)
    high = jnp.floor(wide * (1.0 / 256.0))
    low = wide - 256.0 * high
    pad = jnp.zeros((2, wide.shape[1]), jnp.float32)
    extra = jnp.concatenate([high, low, pad], axis=0).astype(jnp.bfloat16)
    return jnp.concatenate([mode_shapes, extra], axis=0)


def unpack_points(packed, mode_count):
    high = packed[..., mode_count:mode_count + 3, :].astype(jnp.float32)
    low = packed[..., mode_count + 3:mode_count + 6, :].astype(jnp.float32)
    return high * 256.0 + low


def gather_all(block, axis, count):
    spread = jnp.broadcast_to(block[None], (count,) + block.shape)
    return lax.all_to_all(spread, axis, 0, 0, tiled=True)


def all_reduce(matrix, rows, cols):
    flat = matrix.reshape(cols, -1)
    part = lax.all_to_all(flat, "col", 0, 0, tiled=True).reshape(cols, -1).sum(0)
    part = part.reshape(rows, -1)
    part = lax.all_to_all(part, "row", 0, 0, tiled=True).reshape(rows, -1).sum(0)
    whole = gather_all(part, "row", rows).reshape(-1)
    whole = gather_all(whole, "col", cols).reshape(-1)
    return whole.reshape(matrix.shape)


def local(coords, mode_shapes, output_shapes, response_gain):
    rows = lax.axis_size("row")
    cols = lax.axis_size("col")
    mode_count, block_nodes = mode_shapes.shape
    packed = pack_block(coords, mode_shapes)
    row_packed = gather_all(packed, "col", cols)
    row_shapes = jnp.transpose(row_packed[:, :mode_count, :], (1, 0, 2)).reshape(mode_count, -1)
    row_points = jnp.transpose(unpack_points(row_packed, mode_count), (1, 0, 2)).reshape(3, -1)

    half = rows // 2
    shifts = [0] + [d if d % 2 else rows - d for d in range(1, half)] + [half]
    projection = jnp.zeros((mode_count, row_points.shape[1]), jnp.float32)
    for shift in shifts:
        if shift == 0:
            block = packed
        else:
            pairs = [(j, (j - shift) % rows) for j in range(rows)]
            block = lax.ppermute(packed, "row", pairs)
        part_shapes = block[:mode_count, :]
        if shift in (0, half):
            part_shapes = part_shapes * jnp.bfloat16(0.5)
        part_points = unpack_points(block, mode_count)
        coherence_tile = coherence(part_points, row_points)
        projection = projection + jnp.dot(part_shapes, coherence_tile, preferred_element_type=jnp.float32)
    high_part, low_part = split_parts(projection)
    dims = (((1,), (1,)), ((), ()))
    partial = lax.dot_general(row_shapes, high_part, dims, preferred_element_type=jnp.float32)
    partial = partial + lax.dot_general(row_shapes, low_part, dims, preferred_element_type=jnp.float32)
    total = all_reduce(partial, rows, cols)
    modal_csd = total + total.T
    real_part = response_gain[0]
    imag_part = response_gain[1]
    weighted = (
        real_part[:, None] * real_part[None, :] + imag_part[:, None] * imag_part[None, :]
    ) * modal_csd
    weighted_high, weighted_low = split_parts(weighted)
    mapped = jnp.dot(output_shapes, weighted_high, preferred_element_type=jnp.float32)
    mapped = mapped + jnp.dot(output_shapes, weighted_low, preferred_element_type=jnp.float32)
    response_power = jnp.sum(mapped * output_shapes.astype(jnp.float32), axis=1)
    return (response_power, modal_csd)


def solution(mesh):
    in_specs = (P(None, ("row", "col")), P(None, ("row", "col")), P(("row", "col"), None), P())
    out_specs = (P(("row", "col")), P())
    return jax.shard_map(local, mesh=mesh, in_specs=in_specs, out_specs=out_specs, check_vma=False)
```

```python
import functools
import math

import jax
import jax.numpy as jnp
from jax import lax
from jax.experimental import pallas as pl
from jax.experimental.pallas import tpu as pltpu
from jax.sharding import PartitionSpec as P

wave_scale = 0.35 / 64.0


def coherence(left_points, right_points):
    difference = left_points[:, :, None] - right_points[:, None, :]
    squared = jnp.sum(difference * difference, axis=0)
    return jnp.sinc(wave_scale * jnp.sqrt(squared)).astype(jnp.bfloat16)


def split_parts(matrix):
    high_part = matrix.astype(jnp.bfloat16)
    low_part = (matrix - high_part.astype(jnp.float32)).astype(jnp.bfloat16)
    return (high_part, low_part)


def pack_block(coords, mode_shapes):
    wide = coords.astype(jnp.float32)
    high = jnp.floor(wide * (1.0 / 256.0))
    low = wide - 256.0 * high
    pad = jnp.zeros((10, wide.shape[1]), jnp.float32)
    extra = jnp.concatenate([high, low, pad], axis=0).astype(jnp.bfloat16)
    return jnp.concatenate([mode_shapes, extra], axis=0)


def unpack_points(packed, mode_count):
    high = packed[..., mode_count:mode_count + 3, :].astype(jnp.float32)
    low = packed[..., mode_count + 3:mode_count + 6, :].astype(jnp.float32)
    return high * 256.0 + low


CHUNK = 32
SIN_TERMS = [math.pi * (-1) ** k * math.pi ** (2 * k) / math.factorial(2 * k + 1) for k in range(6)]


def coherence_chunk(dx, dy, dz):
    squared = dx * dx + dy * dy + dz * dz
    safe = jnp.maximum(squared, 1e-30)
    root_inv = lax.rsqrt(safe)
    root_inv = root_inv * (1.5 - 0.5 * safe * root_inv * root_inv)
    x = squared * root_inv * wave_scale
    n = jnp.floor(x + 0.5)
    f = x - n
    h = n * 0.5
    sign = 1.0 - 4.0 * (h - jnp.floor(h))
    f2 = f * f
    q = SIN_TERMS[5]
    for term in SIN_TERMS[4::-1]:
        q = q * f2 + term
    scale = jnp.where(n == 0.0, 1.0 / math.pi, f * root_inv * (1.0 / (math.pi * wave_scale)))
    return sign * q * scale


def block_points(slot_ref, mode_count):
    tail = slot_ref[mode_count:mode_count + 16, :].astype(jnp.float32)
    return [tail[k:k + 1, :] * 256.0 + tail[k + 3:k + 4, :] for k in range(3)]


def accumulate_block(slot_ref, weight, rowpts_ref, out_ref, tile_ref, mode_count):
    bx, by, bz = block_points(slot_ref, mode_count)
    length = tile_ref.shape[0]

    def chunk(c, carry):
        r0 = pl.multiple_of(c * CHUNK, CHUNK)
        dx = rowpts_ref[0, pl.ds(r0, CHUNK), :] - bx
        dy = rowpts_ref[1, pl.ds(r0, CHUNK), :] - by
        dz = rowpts_ref[2, pl.ds(r0, CHUNK), :] - bz
        tile_ref[pl.ds(r0, CHUNK), :] = coherence_chunk(dx, dy, dz).astype(jnp.bfloat16)
        return carry

    lax.fori_loop(0, length // CHUNK, chunk, 0)
    shapes = slot_ref[0:mode_count, :]
    product = lax.dot_general(
        tile_ref[...], shapes, (((1,), (1,)), ((), ())), preferred_element_type=jnp.float32
    )
    out_ref[...] += weight * product


def shift_of(j, rows):
    odd = j % 2
    return odd * j + (1 - odd) * (rows - j)


def row_kernel(rows, mode_count, packed_ref, rowpts_ref, out_ref, recv, tile_ref, send_sems, recv_sems):
    me = lax.axis_index("row")
    col = lax.axis_index("col")
    half = rows // 2
    barrier = pltpu.get_barrier_semaphore()
    for p in range(1, rows):
        pl.semaphore_signal(
            barrier, 1, device_id=(lax.rem(me + p, rows), col), device_id_type=pl.DeviceIdType.MESH
        )
    pl.semaphore_wait(barrier, rows - 1)

    def transfer(k):
        target = lax.rem(me + rows - shift_of(k + 1, rows), rows)
        return pltpu.make_async_remote_copy(
            src_ref=packed_ref,
            dst_ref=recv.at[k],
            send_sem=send_sems.at[k],
            recv_sem=recv_sems.at[k],
            device_id=(target, col),
            device_id_type=pl.DeviceIdType.MESH,
        )

    for k in range(half):
        transfer(k).start()
    out_ref[...] = jnp.zeros_like(out_ref)
    accumulate_block(packed_ref, 0.5, rowpts_ref, out_ref, tile_ref, mode_count)

    def step(k, carry):
        transfer(k).wait_recv()
        weight = jnp.where(k == half - 1, 0.5, 1.0).astype(jnp.float32)
        accumulate_block(recv.at[k], weight, rowpts_ref, out_ref, tile_ref, mode_count)
        return carry

    lax.fori_loop(0, half, step, 0)
    for k in range(half):
        transfer(k).wait_send()


def row_exchange(packed, rowpts, rows, mode_count):
    length = rowpts.shape[1]
    half = rows // 2
    vmem = pltpu.MemorySpace.VMEM
    flops = 2 * (half + 1) * length * packed.shape[1] * mode_count
    return pl.pallas_call(
        functools.partial(row_kernel, rows, mode_count),
        out_shape=jax.ShapeDtypeStruct((length, mode_count), jnp.float32),
        in_specs=[pl.BlockSpec(memory_space=vmem)] * 2,
        out_specs=pl.BlockSpec(memory_space=vmem),
        scratch_shapes=[
            pltpu.VMEM((half,) + packed.shape, packed.dtype),
            pltpu.VMEM((length, packed.shape[1]), jnp.bfloat16),
            pltpu.SemaphoreType.DMA((half,)),
            pltpu.SemaphoreType.DMA((half,)),
        ],
        compiler_params=pltpu.CompilerParams(
            collective_id=0, has_side_effects=True, vmem_limit_bytes=48 * 1024 * 1024
        ),
        cost_estimate=pl.CostEstimate(
            flops=flops, transcendentals=(half + 1) * length * packed.shape[1], bytes_accessed=8 * 1024 * 1024
        ),
    )(packed, rowpts)


def gather_all(block, axis, count):
    spread = jnp.broadcast_to(block[None], (count,) + block.shape)
    return lax.all_to_all(spread, axis, 0, 0, tiled=True)


def all_reduce(matrix, rows, cols):
    flat = matrix.reshape(cols, -1)
    part = lax.all_to_all(flat, "col", 0, 0, tiled=True).reshape(cols, -1).sum(0)
    part = part.reshape(rows, -1)
    part = lax.all_to_all(part, "row", 0, 0, tiled=True).reshape(rows, -1).sum(0)
    whole = gather_all(part, "row", rows).reshape(-1)
    whole = gather_all(whole, "col", cols).reshape(-1)
    return whole.reshape(matrix.shape)


def local(coords, mode_shapes, output_shapes, response_gain):
    rows = lax.axis_size("row")
    cols = lax.axis_size("col")
    mode_count, block_nodes = mode_shapes.shape
    packed = pack_block(coords, mode_shapes)
    row_packed = gather_all(packed, "col", cols)
    row_shapes = jnp.transpose(row_packed[:, :mode_count, :], (1, 0, 2)).reshape(mode_count, -1)
    row_points = jnp.transpose(unpack_points(row_packed, mode_count), (1, 0, 2)).reshape(3, -1)

    rowpts = jnp.broadcast_to(row_points[:, :, None], row_points.shape + (block_nodes,))
    projection_t = row_exchange(packed, rowpts, rows, mode_count)
    high_part, low_part = split_parts(projection_t)
    partial = jnp.dot(row_shapes, high_part, preferred_element_type=jnp.float32)
    partial = partial + jnp.dot(row_shapes, low_part, preferred_element_type=jnp.float32)
    total = all_reduce(partial, rows, cols)
    modal_csd = total + total.T
    real_part = response_gain[0]
    imag_part = response_gain[1]
    weighted = (
        real_part[:, None] * real_part[None, :] + imag_part[:, None] * imag_part[None, :]
    ) * modal_csd
    weighted_high, weighted_low = split_parts(weighted)
    mapped = jnp.dot(output_shapes, weighted_high, preferred_element_type=jnp.float32)
    mapped = mapped + jnp.dot(output_shapes, weighted_low, preferred_element_type=jnp.float32)
    response_power = jnp.sum(mapped * output_shapes.astype(jnp.float32), axis=1)
    return (response_power, modal_csd)


def solution(mesh):
    in_specs = (P(None, ("row", "col")), P(None, ("row", "col")), P(("row", "col"), None), P())
    out_specs = (P(("row", "col")), P())
    return jax.shard_map(local, mesh=mesh, in_specs=in_specs, out_specs=out_specs, check_vma=False)
```

```python
import functools
import math

import jax
import jax.numpy as jnp
from jax import lax
from jax.experimental import pallas as pl
from jax.experimental.pallas import tpu as pltpu
from jax.sharding import PartitionSpec as P

wave_scale = 0.35 / 64.0


def coherence(left_points, right_points):
    difference = left_points[:, :, None] - right_points[:, None, :]
    squared = jnp.sum(difference * difference, axis=0)
    return jnp.sinc(wave_scale * jnp.sqrt(squared)).astype(jnp.bfloat16)


def split_parts(matrix):
    high_part = matrix.astype(jnp.bfloat16)
    low_part = (matrix - high_part.astype(jnp.float32)).astype(jnp.bfloat16)
    return (high_part, low_part)


def pack_block(coords, mode_shapes):
    wide = coords.astype(jnp.float32)
    high = jnp.floor(wide * (1.0 / 256.0))
    low = wide - 256.0 * high
    pad = jnp.zeros((10, wide.shape[1]), jnp.float32)
    extra = jnp.concatenate([high, low, pad], axis=0).astype(jnp.bfloat16)
    return jnp.concatenate([mode_shapes, extra], axis=0)


def unpack_points(packed, mode_count):
    high = packed[..., mode_count:mode_count + 3, :].astype(jnp.float32)
    low = packed[..., mode_count + 3:mode_count + 6, :].astype(jnp.float32)
    return high * 256.0 + low


CHUNK = 32
SIN_TERMS = [math.pi * (-1) ** k * math.pi ** (2 * k) / math.factorial(2 * k + 1) for k in range(6)]


def coherence_chunk(dx, dy, dz):
    squared = dx * dx + dy * dy + dz * dz
    safe = jnp.maximum(squared, 1e-30)
    root_inv = lax.rsqrt(safe)
    root_inv = root_inv * (1.5 - 0.5 * safe * root_inv * root_inv)
    x = squared * root_inv * wave_scale
    n = jnp.floor(x + 0.5)
    f = x - n
    h = n * 0.5
    sign = 1.0 - 4.0 * (h - jnp.floor(h))
    f2 = f * f
    q = SIN_TERMS[5]
    for term in SIN_TERMS[4::-1]:
        q = q * f2 + term
    scale = jnp.where(n == 0.0, 1.0 / math.pi, f * root_inv * (1.0 / (math.pi * wave_scale)))
    return sign * q * scale


def block_points(slot_ref, mode_count):
    tail = slot_ref[mode_count:mode_count + 16, :].astype(jnp.float32)
    return [tail[k:k + 1, :] * 256.0 + tail[k + 3:k + 4, :] for k in range(3)]


def accumulate_block(slot_ref, weight, rowpts_ref, out_ref, tile_ref, mode_count):
    bx, by, bz = block_points(slot_ref, mode_count)
    length = tile_ref.shape[0]

    def chunk(c, carry):
        r0 = pl.multiple_of(c * CHUNK, CHUNK)
        dx = rowpts_ref[0, pl.ds(r0, CHUNK), :] - bx
        dy = rowpts_ref[1, pl.ds(r0, CHUNK), :] - by
        dz = rowpts_ref[2, pl.ds(r0, CHUNK), :] - bz
        tile_ref[pl.ds(r0, CHUNK), :] = coherence_chunk(dx, dy, dz).astype(jnp.bfloat16)
        return carry

    lax.fori_loop(0, length // CHUNK, chunk, 0)
    shapes = slot_ref[0:mode_count, :]
    product = lax.dot_general(
        tile_ref[...], shapes, (((1,), (1,)), ((), ())), preferred_element_type=jnp.float32
    )
    out_ref[...] += weight * product


def shift_of(j, rows):
    odd = j % 2
    return odd * j + (1 - odd) * (rows - j)


def row_kernel(rows, mode_count, packed_ref, rowpts_ref, out_ref, recv, tile_ref, send_sems, recv_sems):
    me = lax.axis_index("row")
    col = lax.axis_index("col")
    half = rows // 2
    barrier = pltpu.get_barrier_semaphore()
    for p in range(1, rows):
        pl.semaphore_signal(
            barrier, 1, device_id=(lax.rem(me + p, rows), col), device_id_type=pl.DeviceIdType.MESH
        )
    pl.semaphore_wait(barrier, rows - 1)

    def transfer(k):
        target = lax.rem(me + rows - shift_of(k + 1, rows), rows)
        return pltpu.make_async_remote_copy(
            src_ref=packed_ref,
            dst_ref=recv.at[k],
            send_sem=send_sems.at[k],
            recv_sem=recv_sems.at[k],
            device_id=(target, col),
            device_id_type=pl.DeviceIdType.MESH,
        )

    for k in range(half):
        transfer(k).start()
    out_ref[...] = jnp.zeros_like(out_ref)
    accumulate_block(packed_ref, 0.5, rowpts_ref, out_ref, tile_ref, mode_count)

    def step(k, carry):
        transfer(k).wait_recv()
        weight = jnp.where(k == half - 1, 0.5, 1.0).astype(jnp.float32)
        accumulate_block(recv.at[k], weight, rowpts_ref, out_ref, tile_ref, mode_count)
        return carry

    lax.fori_loop(0, half, step, 0)
    for k in range(half):
        transfer(k).wait_send()


def row_exchange(packed, rowpts, rows, mode_count):
    length = rowpts.shape[1]
    half = rows // 2
    vmem = pltpu.MemorySpace.VMEM
    flops = 2 * (half + 1) * length * packed.shape[1] * mode_count
    return pl.pallas_call(
        functools.partial(row_kernel, rows, mode_count),
        out_shape=jax.ShapeDtypeStruct((length, mode_count), jnp.float32),
        in_specs=[pl.BlockSpec(memory_space=vmem)] * 2,
        out_specs=pl.BlockSpec(memory_space=vmem),
        scratch_shapes=[
            pltpu.VMEM((half,) + packed.shape, packed.dtype),
            pltpu.VMEM((length, packed.shape[1]), jnp.bfloat16),
            pltpu.SemaphoreType.DMA((half,)),
            pltpu.SemaphoreType.DMA((half,)),
        ],
        compiler_params=pltpu.CompilerParams(
            collective_id=0, has_side_effects=True, vmem_limit_bytes=48 * 1024 * 1024
        ),
        cost_estimate=pl.CostEstimate(
            flops=flops, transcendentals=(half + 1) * length * packed.shape[1], bytes_accessed=8 * 1024 * 1024
        ),
    )(packed, rowpts)


def gather_all(block, axis, count):
    spread = jnp.broadcast_to(block[None], (count,) + block.shape)
    return lax.all_to_all(spread, axis, 0, 0, tiled=True)


def ar_kernel(rows, cols, y_ref, out_ref, buf_a, buf_b, buf_c, red_a, red_b, sa, ra, sb, rb, sc, rc):
    me_r = lax.axis_index("row")
    me_c = lax.axis_index("col")
    buf_a[...] = jnp.zeros_like(buf_a)
    buf_b[...] = jnp.zeros_like(buf_b)
    buf_c[...] = jnp.zeros_like(buf_c)
    barrier = pltpu.get_barrier_semaphore()
    for p in range(1, cols):
        pl.semaphore_signal(
            barrier, 1, device_id=(me_r, lax.rem(me_c + p, cols)), device_id_type=pl.DeviceIdType.MESH
        )
    for p in range(1, rows):
        pl.semaphore_signal(
            barrier, 1, device_id=(lax.rem(me_r + p, rows), me_c), device_id_type=pl.DeviceIdType.MESH
        )
    pl.semaphore_wait(barrier, cols - 1 + rows - 1)

    def copy(src, buf, slot, send, recv, sem_index, peer):
        return pltpu.make_async_remote_copy(
            src_ref=src,
            dst_ref=buf.at[slot],
            send_sem=send.at[sem_index],
            recv_sem=recv.at[slot],
            device_id=peer,
            device_id_type=pl.DeviceIdType.MESH,
        )

    def exchange(src_of, buf, send, recv, count, me, peer_of):
        for s in range(count):
            @pl.when(s != me)
            def _():
                copy(src_of(s), buf, me, send, recv, s, peer_of(s)).start()
        for s in range(count):
            @pl.when(s != me)
            def _():
                copy(src_of(s), buf, s, send, recv, s, peer_of(s)).wait_recv()

    def finish(src_of, buf, send, recv, count, me, peer_of):
        for s in range(count):
            @pl.when(s != me)
            def _():
                copy(src_of(s), buf, me, send, recv, s, peer_of(s)).wait_send()

    col_peer = lambda s: (me_r, s)
    row_peer = lambda s: (s, me_c)
    exchange(lambda s: y_ref.at[s], buf_a, sa, ra, cols, me_c, col_peer)
    chunk = y_ref[me_c]
    for s in range(cols):
        chunk = chunk + buf_a[s]
    red_a[...] = chunk
    exchange(lambda s: red_a, buf_b, sb, rb, rows, me_r, row_peer)
    total = jnp.zeros_like(chunk)
    for s in range(rows):
        total = total + jnp.where(s == me_r, chunk, buf_b[s])
    red_b[...] = total
    exchange(lambda s: red_b, buf_c, sc, rc, cols, me_c, col_peer)
    for s in range(cols):
        out_ref[s] = jnp.where(s == me_c, total, buf_c[s])
    finish(lambda s: y_ref.at[s], buf_a, sa, ra, cols, me_c, col_peer)
    finish(lambda s: red_a, buf_b, sb, rb, rows, me_r, row_peer)
    finish(lambda s: red_b, buf_c, sc, rc, cols, me_c, col_peer)


def all_reduce(matrix, rows, cols):
    pieces = matrix.reshape(cols, -1, 128)
    shape = pieces.shape
    vmem = pltpu.MemorySpace.VMEM
    total = pl.pallas_call(
        functools.partial(ar_kernel, rows, cols),
        out_shape=jax.ShapeDtypeStruct(shape, jnp.float32),
        in_specs=[pl.BlockSpec(memory_space=vmem)],
        out_specs=pl.BlockSpec(memory_space=vmem),
        scratch_shapes=[
            pltpu.VMEM(shape, jnp.float32),
            pltpu.VMEM((rows,) + shape[1:], jnp.float32),
            pltpu.VMEM(shape, jnp.float32),
            pltpu.VMEM(shape[1:], jnp.float32),
            pltpu.VMEM(shape[1:], jnp.float32),
            pltpu.SemaphoreType.DMA((cols,)),
            pltpu.SemaphoreType.DMA((cols,)),
            pltpu.SemaphoreType.DMA((rows,)),
            pltpu.SemaphoreType.DMA((rows,)),
            pltpu.SemaphoreType.DMA((cols,)),
            pltpu.SemaphoreType.DMA((cols,)),
        ],
        compiler_params=pltpu.CompilerParams(collective_id=1, has_side_effects=True),
    )(pieces)
    return total.reshape(matrix.shape)


def local(coords, mode_shapes, output_shapes, response_gain):
    rows = lax.axis_size("row")
    cols = lax.axis_size("col")
    mode_count, block_nodes = mode_shapes.shape
    packed = pack_block(coords, mode_shapes)
    row_packed = gather_all(packed, "col", cols)
    row_shapes = jnp.transpose(row_packed[:, :mode_count, :], (1, 0, 2)).reshape(mode_count, -1)
    row_points = jnp.transpose(unpack_points(row_packed, mode_count), (1, 0, 2)).reshape(3, -1)

    rowpts = jnp.broadcast_to(row_points[:, :, None], row_points.shape + (block_nodes,))
    projection_t = row_exchange(packed, rowpts, rows, mode_count)
    high_part, low_part = split_parts(projection_t)
    partial = jnp.dot(row_shapes, high_part, preferred_element_type=jnp.float32)
    partial = partial + jnp.dot(row_shapes, low_part, preferred_element_type=jnp.float32)
    total = all_reduce(partial, rows, cols)
    modal_csd = total + total.T
    real_part = response_gain[0]
    imag_part = response_gain[1]
    weighted = (
        real_part[:, None] * real_part[None, :] + imag_part[:, None] * imag_part[None, :]
    ) * modal_csd
    weighted_high, weighted_low = split_parts(weighted)
    mapped = jnp.dot(output_shapes, weighted_high, preferred_element_type=jnp.float32)
    mapped = mapped + jnp.dot(output_shapes, weighted_low, preferred_element_type=jnp.float32)
    response_power = jnp.sum(mapped * output_shapes.astype(jnp.float32), axis=1)
    return (response_power, modal_csd)


def solution(mesh):
    in_specs = (P(None, ("row", "col")), P(None, ("row", "col")), P(("row", "col"), None), P())
    out_specs = (P(("row", "col")), P())
    return jax.shard_map(local, mesh=mesh, in_specs=in_specs, out_specs=out_specs, check_vma=False)
```

```python
import functools
import math

import jax
import jax.numpy as jnp
from jax import lax
from jax.experimental import pallas as pl
from jax.experimental.pallas import tpu as pltpu
from jax.sharding import PartitionSpec as P

wave_scale = 0.35 / 64.0


def coherence(left_points, right_points):
    difference = left_points[:, :, None] - right_points[:, None, :]
    squared = jnp.sum(difference * difference, axis=0)
    return jnp.sinc(wave_scale * jnp.sqrt(squared)).astype(jnp.bfloat16)


def split_parts(matrix):
    high_part = matrix.astype(jnp.bfloat16)
    low_part = (matrix - high_part.astype(jnp.float32)).astype(jnp.bfloat16)
    return (high_part, low_part)


def pack_block(coords, mode_shapes):
    wide = coords.astype(jnp.float32)
    high = jnp.floor(wide * (1.0 / 256.0))
    low = wide - 256.0 * high
    pad = jnp.zeros((10, wide.shape[1]), jnp.float32)
    extra = jnp.concatenate([high, low, pad], axis=0).astype(jnp.bfloat16)
    return jnp.concatenate([mode_shapes, extra], axis=0)


def unpack_points(packed, mode_count):
    high = packed[..., mode_count:mode_count + 3, :].astype(jnp.float32)
    low = packed[..., mode_count + 3:mode_count + 6, :].astype(jnp.float32)
    return high * 256.0 + low


CHUNK = 32
SIN_TERMS = [math.pi * (-1) ** k * math.pi ** (2 * k) / math.factorial(2 * k + 1) for k in range(6)]


def coherence_chunk(dx, dy, dz):
    squared = dx * dx + dy * dy + dz * dz
    safe = jnp.maximum(squared, 1e-30)
    root_inv = lax.rsqrt(safe)
    root_inv = root_inv * (1.5 - 0.5 * safe * root_inv * root_inv)
    x = squared * root_inv * wave_scale
    n = jnp.floor(x + 0.5)
    f = x - n
    h = n * 0.5
    sign = 1.0 - 4.0 * (h - jnp.floor(h))
    f2 = f * f
    q = SIN_TERMS[5]
    for term in SIN_TERMS[4::-1]:
        q = q * f2 + term
    scale = jnp.where(n == 0.0, 1.0 / math.pi, f * root_inv * (1.0 / (math.pi * wave_scale)))
    return sign * q * scale


def block_points(slot_ref, mode_count):
    tail = slot_ref[mode_count:mode_count + 16, :].astype(jnp.float32)
    return [tail[k:k + 1, :] * 256.0 + tail[k + 3:k + 4, :] for k in range(3)]


def accumulate_block(slot_ref, weight, rowpts_ref, out_ref, tile_ref, mode_count):
    bx, by, bz = block_points(slot_ref, mode_count)
    length = tile_ref.shape[0]

    def chunk(c, carry):
        r0 = pl.multiple_of(c * CHUNK, CHUNK)
        dx = rowpts_ref[0, pl.ds(r0, CHUNK), :] - bx
        dy = rowpts_ref[1, pl.ds(r0, CHUNK), :] - by
        dz = rowpts_ref[2, pl.ds(r0, CHUNK), :] - bz
        tile_ref[pl.ds(r0, CHUNK), :] = coherence_chunk(dx, dy, dz).astype(jnp.bfloat16)
        return carry

    lax.fori_loop(0, length // CHUNK, chunk, 0)
    shapes = slot_ref[0:mode_count, :]
    product = lax.dot_general(
        tile_ref[...], shapes, (((1,), (1,)), ((), ())), preferred_element_type=jnp.float32
    )
    out_ref[...] += weight * product


def shift_of(j, rows):
    odd = j % 2
    return odd * j + (1 - odd) * (rows - j)


def row_kernel(rows, cols, mode_count, packed_ref, out_ref, recv, colbuf, rowpts_ref, tile_ref, acc_ref,
               send_sems, recv_sems, col_send, col_recv):
    me = lax.axis_index("row")
    col = lax.axis_index("col")
    half = rows // 2
    nodes = packed_ref.shape[1]
    colbuf[...] = jnp.zeros_like(colbuf)
    barrier = pltpu.get_barrier_semaphore()
    for p in range(1, rows):
        pl.semaphore_signal(
            barrier, 1, device_id=(lax.rem(me + p, rows), col), device_id_type=pl.DeviceIdType.MESH
        )
    for p in range(1, cols):
        pl.semaphore_signal(
            barrier, 1, device_id=(me, lax.rem(col + p, cols)), device_id_type=pl.DeviceIdType.MESH
        )
    pl.semaphore_wait(barrier, rows - 1 + cols - 1)

    def col_copy(s, slot):
        return pltpu.make_async_remote_copy(
            src_ref=packed_ref,
            dst_ref=colbuf.at[slot],
            send_sem=col_send.at[s],
            recv_sem=col_recv.at[slot],
            device_id=(me, s),
            device_id_type=pl.DeviceIdType.MESH,
        )

    def transfer(k):
        target = lax.rem(me + rows - shift_of(k + 1, rows), rows)
        return pltpu.make_async_remote_copy(
            src_ref=packed_ref,
            dst_ref=recv.at[k],
            send_sem=send_sems.at[k],
            recv_sem=recv_sems.at[k],
            device_id=(target, col),
            device_id_type=pl.DeviceIdType.MESH,
        )

    for s in range(cols):
        @pl.when(s != col)
        def _():
            col_copy(s, col).start()
    for k in range(half):
        transfer(k).start()
    for s in range(cols):
        @pl.when(s != col)
        def _():
            col_copy(s, s).wait_recv()

    eye = (lax.broadcasted_iota(jnp.int32, (nodes, nodes), 0)
           == lax.broadcasted_iota(jnp.int32, (nodes, nodes), 1)).astype(jnp.bfloat16)
    own_tail = packed_ref[mode_count:mode_count + 16, :]
    for s in range(cols):
        tail = jnp.where(s == col, own_tail, colbuf[s, mode_count:mode_count + 16, :])
        moved = lax.dot_general(eye, tail, (((1,), (1,)), ((), ())), preferred_element_type=jnp.float32)
        for k in range(3):
            column = moved[:, k:k + 1] * 256.0 + moved[:, k + 3:k + 4]
            rowpts_ref[k, s * nodes:(s + 1) * nodes, :] = jnp.broadcast_to(column, (nodes, nodes))

    acc_ref[...] = jnp.zeros_like(acc_ref)
    accumulate_block(packed_ref, 0.5, rowpts_ref, acc_ref, tile_ref, mode_count)

    def step(k, carry):
        transfer(k).wait_recv()
        weight = jnp.where(k == half - 1, 0.5, 1.0).astype(jnp.float32)
        accumulate_block(recv.at[k], weight, rowpts_ref, acc_ref, tile_ref, mode_count)
        return carry

    lax.fori_loop(0, half, step, 0)

    own_shapes = packed_ref[0:mode_count, :]
    partial = jnp.zeros(out_ref.shape, jnp.float32)
    for s in range(cols):
        shapes = jnp.where(s == col, own_shapes, colbuf[s, 0:mode_count, :])
        part = acc_ref[s * nodes:(s + 1) * nodes, :]
        high = part.astype(jnp.bfloat16)
        low = (part - high.astype(jnp.float32)).astype(jnp.bfloat16)
        partial = partial + jnp.dot(shapes, high, preferred_element_type=jnp.float32)
        partial = partial + jnp.dot(shapes, low, preferred_element_type=jnp.float32)
    out_ref[...] = partial

    for k in range(half):
        transfer(k).wait_send()
    for s in range(cols):
        @pl.when(s != col)
        def _():
            col_copy(s, col).wait_send()


def row_exchange(packed, rows, cols, mode_count):
    nodes = packed.shape[1]
    length = cols * nodes
    half = rows // 2
    vmem = pltpu.MemorySpace.VMEM
    flops = 2 * (half + 1) * length * nodes * mode_count + 4 * length * mode_count * mode_count
    return pl.pallas_call(
        functools.partial(row_kernel, rows, cols, mode_count),
        out_shape=jax.ShapeDtypeStruct((mode_count, mode_count), jnp.float32),
        in_specs=[pl.BlockSpec(memory_space=vmem)],
        out_specs=pl.BlockSpec(memory_space=vmem),
        scratch_shapes=[
            pltpu.VMEM((half,) + packed.shape, packed.dtype),
            pltpu.VMEM((cols,) + packed.shape, packed.dtype),
            pltpu.VMEM((3, length, nodes), jnp.float32),
            pltpu.VMEM((length, nodes), jnp.bfloat16),
            pltpu.VMEM((length, mode_count), jnp.float32),
            pltpu.SemaphoreType.DMA((half,)),
            pltpu.SemaphoreType.DMA((half,)),
            pltpu.SemaphoreType.DMA((cols,)),
            pltpu.SemaphoreType.DMA((cols,)),
        ],
        compiler_params=pltpu.CompilerParams(
            collective_id=0, has_side_effects=True, vmem_limit_bytes=48 * 1024 * 1024
        ),
        cost_estimate=pl.CostEstimate(
            flops=flops, transcendentals=(half + 1) * length * nodes, bytes_accessed=4 * 1024 * 1024
        ),
    )(packed)

def gather_all(block, axis, count):
    spread = jnp.broadcast_to(block[None], (count,) + block.shape)
    return lax.all_to_all(spread, axis, 0, 0, tiled=True)


def ar_kernel(rows, cols, y_ref, out_ref, buf_a, buf_b, buf_c, red_a, red_b, sa, ra, sb, rb, sc, rc):
    me_r = lax.axis_index("row")
    me_c = lax.axis_index("col")
    buf_a[...] = jnp.zeros_like(buf_a)
    buf_b[...] = jnp.zeros_like(buf_b)
    buf_c[...] = jnp.zeros_like(buf_c)
    barrier = pltpu.get_barrier_semaphore()
    for p in range(1, cols):
        pl.semaphore_signal(
            barrier, 1, device_id=(me_r, lax.rem(me_c + p, cols)), device_id_type=pl.DeviceIdType.MESH
        )
    for p in range(1, rows):
        pl.semaphore_signal(
            barrier, 1, device_id=(lax.rem(me_r + p, rows), me_c), device_id_type=pl.DeviceIdType.MESH
        )
    pl.semaphore_wait(barrier, cols - 1 + rows - 1)

    def copy(src, buf, slot, send, recv, sem_index, peer):
        return pltpu.make_async_remote_copy(
            src_ref=src,
            dst_ref=buf.at[slot],
            send_sem=send.at[sem_index],
            recv_sem=recv.at[slot],
            device_id=peer,
            device_id_type=pl.DeviceIdType.MESH,
        )

    def exchange(src_of, buf, send, recv, count, me, peer_of):
        for s in range(count):
            @pl.when(s != me)
            def _():
                copy(src_of(s), buf, me, send, recv, s, peer_of(s)).start()
        for s in range(count):
            @pl.when(s != me)
            def _():
                copy(src_of(s), buf, s, send, recv, s, peer_of(s)).wait_recv()

    def finish(src_of, buf, send, recv, count, me, peer_of):
        for s in range(count):
            @pl.when(s != me)
            def _():
                copy(src_of(s), buf, me, send, recv, s, peer_of(s)).wait_send()

    col_peer = lambda s: (me_r, s)
    row_peer = lambda s: (s, me_c)
    exchange(lambda s: y_ref.at[s], buf_a, sa, ra, cols, me_c, col_peer)
    chunk = y_ref[me_c]
    for s in range(cols):
        chunk = chunk + buf_a[s]
    red_a[...] = chunk
    exchange(lambda s: red_a, buf_b, sb, rb, rows, me_r, row_peer)
    total = jnp.zeros_like(chunk)
    for s in range(rows):
        total = total + jnp.where(s == me_r, chunk, buf_b[s])
    red_b[...] = total
    exchange(lambda s: red_b, buf_c, sc, rc, cols, me_c, col_peer)
    for s in range(cols):
        out_ref[s] = jnp.where(s == me_c, total, buf_c[s])
    finish(lambda s: y_ref.at[s], buf_a, sa, ra, cols, me_c, col_peer)
    finish(lambda s: red_a, buf_b, sb, rb, rows, me_r, row_peer)
    finish(lambda s: red_b, buf_c, sc, rc, cols, me_c, col_peer)


def all_reduce(matrix, rows, cols):
    pieces = matrix.reshape(cols, -1, 128)
    shape = pieces.shape
    vmem = pltpu.MemorySpace.VMEM
    total = pl.pallas_call(
        functools.partial(ar_kernel, rows, cols),
        out_shape=jax.ShapeDtypeStruct(shape, jnp.float32),
        in_specs=[pl.BlockSpec(memory_space=vmem)],
        out_specs=pl.BlockSpec(memory_space=vmem),
        scratch_shapes=[
            pltpu.VMEM(shape, jnp.float32),
            pltpu.VMEM((rows,) + shape[1:], jnp.float32),
            pltpu.VMEM(shape, jnp.float32),
            pltpu.VMEM(shape[1:], jnp.float32),
            pltpu.VMEM(shape[1:], jnp.float32),
            pltpu.SemaphoreType.DMA((cols,)),
            pltpu.SemaphoreType.DMA((cols,)),
            pltpu.SemaphoreType.DMA((rows,)),
            pltpu.SemaphoreType.DMA((rows,)),
            pltpu.SemaphoreType.DMA((cols,)),
            pltpu.SemaphoreType.DMA((cols,)),
        ],
        compiler_params=pltpu.CompilerParams(collective_id=1, has_side_effects=True),
    )(pieces)
    return total.reshape(matrix.shape)


def local(coords, mode_shapes, output_shapes, response_gain):
    rows = lax.axis_size("row")
    cols = lax.axis_size("col")
    mode_count, block_nodes = mode_shapes.shape
    packed = pack_block(coords, mode_shapes)
    partial = row_exchange(packed, rows, cols, mode_count)
    total = all_reduce(partial, rows, cols)
    modal_csd = total + total.T
    real_part = response_gain[0]
    imag_part = response_gain[1]
    weighted = (
        real_part[:, None] * real_part[None, :] + imag_part[:, None] * imag_part[None, :]
    ) * modal_csd
    weighted_high, weighted_low = split_parts(weighted)
    mapped = jnp.dot(output_shapes, weighted_high, preferred_element_type=jnp.float32)
    mapped = mapped + jnp.dot(output_shapes, weighted_low, preferred_element_type=jnp.float32)
    response_power = jnp.sum(mapped * output_shapes.astype(jnp.float32), axis=1)
    return (response_power, modal_csd)


def solution(mesh):
    in_specs = (P(None, ("row", "col")), P(None, ("row", "col")), P(("row", "col"), None), P())
    out_specs = (P(("row", "col")), P())
    return jax.shard_map(local, mesh=mesh, in_specs=in_specs, out_specs=out_specs, check_vma=False)
```

```python
import functools
import math

import jax
import jax.numpy as jnp
from jax import lax
from jax.experimental import pallas as pl
from jax.experimental.pallas import tpu as pltpu
from jax.sharding import PartitionSpec as P

wave_scale = 0.35 / 64.0


def coherence(left_points, right_points):
    difference = left_points[:, :, None] - right_points[:, None, :]
    squared = jnp.sum(difference * difference, axis=0)
    return jnp.sinc(wave_scale * jnp.sqrt(squared)).astype(jnp.bfloat16)


def split_parts(matrix):
    high_part = matrix.astype(jnp.bfloat16)
    low_part = (matrix - high_part.astype(jnp.float32)).astype(jnp.bfloat16)
    return (high_part, low_part)


def pack_block(coords, mode_shapes):
    wide = coords.astype(jnp.float32)
    high = jnp.floor(wide * (1.0 / 256.0))
    low = wide - 256.0 * high
    pad = jnp.zeros((10, wide.shape[1]), jnp.float32)
    extra = jnp.concatenate([high, low, pad], axis=0).astype(jnp.bfloat16)
    return jnp.concatenate([mode_shapes, extra], axis=0)


def unpack_points(packed, mode_count):
    high = packed[..., mode_count:mode_count + 3, :].astype(jnp.float32)
    low = packed[..., mode_count + 3:mode_count + 6, :].astype(jnp.float32)
    return high * 256.0 + low


CHUNK = 32
SIN_TERMS = [math.pi * (-1) ** k * math.pi ** (2 * k) / math.factorial(2 * k + 1) for k in range(6)]


def coherence_chunk(dx, dy, dz):
    squared = dx * dx + dy * dy + dz * dz
    safe = jnp.maximum(squared, 1e-30)
    root_inv = lax.rsqrt(safe)
    x = safe * root_inv * wave_scale
    n = jnp.floor(x + 0.5)
    f = x - n
    h = n * 0.5
    sign = 1.0 - 4.0 * (h - jnp.floor(h))
    f2 = f * f
    q = SIN_TERMS[4]
    for term in SIN_TERMS[3::-1]:
        q = q * f2 + term
    scale = f * root_inv * (1.0 / (math.pi * wave_scale))
    return sign * q * scale


def block_points(slot_ref, mode_count):
    tail = slot_ref[mode_count:mode_count + 16, :].astype(jnp.float32)
    return [tail[k:k + 1, :] * 256.0 + tail[k + 3:k + 4, :] for k in range(3)]


def accumulate_block(slot_ref, weight, rowpts_ref, out_ref, tile_ref, mode_count):
    bx, by, bz = block_points(slot_ref, mode_count)
    length = tile_ref.shape[0]

    def chunk(c, carry):
        r0 = pl.multiple_of(c * CHUNK, CHUNK)
        dx = rowpts_ref[0, pl.ds(r0, CHUNK), :] - bx
        dy = rowpts_ref[1, pl.ds(r0, CHUNK), :] - by
        dz = rowpts_ref[2, pl.ds(r0, CHUNK), :] - bz
        tile_ref[pl.ds(r0, CHUNK), :] = coherence_chunk(dx, dy, dz).astype(jnp.bfloat16)
        return carry

    lax.fori_loop(0, length // CHUNK, chunk, 0)
    shapes = slot_ref[0:mode_count, :]
    product = lax.dot_general(
        tile_ref[...], shapes, (((1,), (1,)), ((), ())), preferred_element_type=jnp.float32
    )
    out_ref[...] += weight * product


def shift_of(j, rows):
    odd = j % 2
    return odd * j + (1 - odd) * (rows - j)


def row_kernel(rows, cols, mode_count, packed_ref, out_ref, recv, colbuf, rowpts_ref, tile_ref, acc_ref,
               send_sems, recv_sems, col_send, col_recv):
    me = lax.axis_index("row")
    col = lax.axis_index("col")
    half = rows // 2
    nodes = packed_ref.shape[1]
    colbuf[...] = jnp.zeros_like(colbuf)
    barrier = pltpu.get_barrier_semaphore()
    for p in range(1, rows):
        pl.semaphore_signal(
            barrier, 1, device_id=(lax.rem(me + p, rows), col), device_id_type=pl.DeviceIdType.MESH
        )
    for p in range(1, cols):
        pl.semaphore_signal(
            barrier, 1, device_id=(me, lax.rem(col + p, cols)), device_id_type=pl.DeviceIdType.MESH
        )
    pl.semaphore_wait(barrier, rows - 1 + cols - 1)

    def col_copy(s, slot):
        return pltpu.make_async_remote_copy(
            src_ref=packed_ref,
            dst_ref=colbuf.at[slot],
            send_sem=col_send.at[s],
            recv_sem=col_recv.at[slot],
            device_id=(me, s),
            device_id_type=pl.DeviceIdType.MESH,
        )

    def transfer(k):
        target = lax.rem(me + rows - shift_of(k + 1, rows), rows)
        return pltpu.make_async_remote_copy(
            src_ref=packed_ref,
            dst_ref=recv.at[k],
            send_sem=send_sems.at[k],
            recv_sem=recv_sems.at[k],
            device_id=(target, col),
            device_id_type=pl.DeviceIdType.MESH,
        )

    for s in range(cols):
        @pl.when(s != col)
        def _():
            col_copy(s, col).start()
    for k in range(half):
        transfer(k).start()
    for s in range(cols):
        @pl.when(s != col)
        def _():
            col_copy(s, s).wait_recv()

    eye = (lax.broadcasted_iota(jnp.int32, (nodes, nodes), 0)
           == lax.broadcasted_iota(jnp.int32, (nodes, nodes), 1)).astype(jnp.bfloat16)
    own_tail = packed_ref[mode_count:mode_count + 16, :]
    for s in range(cols):
        tail = jnp.where(s == col, own_tail, colbuf[s, mode_count:mode_count + 16, :])
        moved = lax.dot_general(eye, tail, (((1,), (1,)), ((), ())), preferred_element_type=jnp.float32)
        for k in range(3):
            column = moved[:, k:k + 1] * 256.0 + moved[:, k + 3:k + 4]
            rowpts_ref[k, s * nodes:(s + 1) * nodes, :] = jnp.broadcast_to(column, (nodes, nodes))

    acc_ref[...] = jnp.zeros_like(acc_ref)
    accumulate_block(packed_ref, 0.5, rowpts_ref, acc_ref, tile_ref, mode_count)

    def step(k, carry):
        transfer(k).wait_recv()
        weight = jnp.where(k == half - 1, 0.5, 1.0).astype(jnp.float32)
        accumulate_block(recv.at[k], weight, rowpts_ref, acc_ref, tile_ref, mode_count)
        return carry

    lax.fori_loop(0, half, step, 0)

    own_shapes = packed_ref[0:mode_count, :]
    partial = jnp.zeros(out_ref.shape, jnp.float32)
    for s in range(cols):
        shapes = jnp.where(s == col, own_shapes, colbuf[s, 0:mode_count, :])
        part = acc_ref[s * nodes:(s + 1) * nodes, :]
        high = part.astype(jnp.bfloat16)
        low = (part - high.astype(jnp.float32)).astype(jnp.bfloat16)
        partial = partial + jnp.dot(shapes, high, preferred_element_type=jnp.float32)
        partial = partial + jnp.dot(shapes, low, preferred_element_type=jnp.float32)
    out_ref[...] = partial

    for k in range(half):
        transfer(k).wait_send()
    for s in range(cols):
        @pl.when(s != col)
        def _():
            col_copy(s, col).wait_send()


def row_exchange(packed, rows, cols, mode_count):
    nodes = packed.shape[1]
    length = cols * nodes
    half = rows // 2
    vmem = pltpu.MemorySpace.VMEM
    flops = 2 * (half + 1) * length * nodes * mode_count + 4 * length * mode_count * mode_count
    return pl.pallas_call(
        functools.partial(row_kernel, rows, cols, mode_count),
        out_shape=jax.ShapeDtypeStruct((mode_count, mode_count), jnp.float32),
        in_specs=[pl.BlockSpec(memory_space=vmem)],
        out_specs=pl.BlockSpec(memory_space=vmem),
        scratch_shapes=[
            pltpu.VMEM((half,) + packed.shape, packed.dtype),
            pltpu.VMEM((cols,) + packed.shape, packed.dtype),
            pltpu.VMEM((3, length, nodes), jnp.float32),
            pltpu.VMEM((length, nodes), jnp.bfloat16),
            pltpu.VMEM((length, mode_count), jnp.float32),
            pltpu.SemaphoreType.DMA((half,)),
            pltpu.SemaphoreType.DMA((half,)),
            pltpu.SemaphoreType.DMA((cols,)),
            pltpu.SemaphoreType.DMA((cols,)),
        ],
        compiler_params=pltpu.CompilerParams(
            collective_id=0, has_side_effects=True, vmem_limit_bytes=48 * 1024 * 1024
        ),
        cost_estimate=pl.CostEstimate(
            flops=flops, transcendentals=(half + 1) * length * nodes, bytes_accessed=4 * 1024 * 1024
        ),
    )(packed)

def gather_all(block, axis, count):
    spread = jnp.broadcast_to(block[None], (count,) + block.shape)
    return lax.all_to_all(spread, axis, 0, 0, tiled=True)


def ar_kernel(rows, cols, y_ref, out_ref, buf_a, buf_b, buf_c, red_a, red_b, sa, ra, sb, rb, sc, rc):
    me_r = lax.axis_index("row")
    me_c = lax.axis_index("col")
    buf_a[...] = jnp.zeros_like(buf_a)
    buf_b[...] = jnp.zeros_like(buf_b)
    buf_c[...] = jnp.zeros_like(buf_c)
    barrier = pltpu.get_barrier_semaphore()
    for p in range(1, cols):
        pl.semaphore_signal(
            barrier, 1, device_id=(me_r, lax.rem(me_c + p, cols)), device_id_type=pl.DeviceIdType.MESH
        )
    for p in range(1, rows):
        pl.semaphore_signal(
            barrier, 1, device_id=(lax.rem(me_r + p, rows), me_c), device_id_type=pl.DeviceIdType.MESH
        )
    pl.semaphore_wait(barrier, cols - 1 + rows - 1)

    def copy(src, buf, slot, send, recv, sem_index, peer):
        return pltpu.make_async_remote_copy(
            src_ref=src,
            dst_ref=buf.at[slot],
            send_sem=send.at[sem_index],
            recv_sem=recv.at[slot],
            device_id=peer,
            device_id_type=pl.DeviceIdType.MESH,
        )

    def exchange(src_of, buf, send, recv, count, me, peer_of):
        for s in range(count):
            @pl.when(s != me)
            def _():
                copy(src_of(s), buf, me, send, recv, s, peer_of(s)).start()
        for s in range(count):
            @pl.when(s != me)
            def _():
                copy(src_of(s), buf, s, send, recv, s, peer_of(s)).wait_recv()

    def finish(src_of, buf, send, recv, count, me, peer_of):
        for s in range(count):
            @pl.when(s != me)
            def _():
                copy(src_of(s), buf, me, send, recv, s, peer_of(s)).wait_send()

    col_peer = lambda s: (me_r, s)
    row_peer = lambda s: (s, me_c)
    exchange(lambda s: y_ref.at[s], buf_a, sa, ra, cols, me_c, col_peer)
    chunk = y_ref[me_c]
    for s in range(cols):
        chunk = chunk + buf_a[s]
    red_a[...] = chunk
    exchange(lambda s: red_a, buf_b, sb, rb, rows, me_r, row_peer)
    total = jnp.zeros_like(chunk)
    for s in range(rows):
        total = total + jnp.where(s == me_r, chunk, buf_b[s])
    red_b[...] = total
    exchange(lambda s: red_b, buf_c, sc, rc, cols, me_c, col_peer)
    for s in range(cols):
        out_ref[s] = jnp.where(s == me_c, total, buf_c[s])
    finish(lambda s: y_ref.at[s], buf_a, sa, ra, cols, me_c, col_peer)
    finish(lambda s: red_a, buf_b, sb, rb, rows, me_r, row_peer)
    finish(lambda s: red_b, buf_c, sc, rc, cols, me_c, col_peer)


def all_reduce(matrix, rows, cols):
    pieces = matrix.reshape(cols, -1, 128)
    shape = pieces.shape
    vmem = pltpu.MemorySpace.VMEM
    total = pl.pallas_call(
        functools.partial(ar_kernel, rows, cols),
        out_shape=jax.ShapeDtypeStruct(shape, jnp.float32),
        in_specs=[pl.BlockSpec(memory_space=vmem)],
        out_specs=pl.BlockSpec(memory_space=vmem),
        scratch_shapes=[
            pltpu.VMEM(shape, jnp.float32),
            pltpu.VMEM((rows,) + shape[1:], jnp.float32),
            pltpu.VMEM(shape, jnp.float32),
            pltpu.VMEM(shape[1:], jnp.float32),
            pltpu.VMEM(shape[1:], jnp.float32),
            pltpu.SemaphoreType.DMA((cols,)),
            pltpu.SemaphoreType.DMA((cols,)),
            pltpu.SemaphoreType.DMA((rows,)),
            pltpu.SemaphoreType.DMA((rows,)),
            pltpu.SemaphoreType.DMA((cols,)),
            pltpu.SemaphoreType.DMA((cols,)),
        ],
        compiler_params=pltpu.CompilerParams(collective_id=1, has_side_effects=True),
    )(pieces)
    return total.reshape(matrix.shape)


def local(coords, mode_shapes, output_shapes, response_gain):
    rows = lax.axis_size("row")
    cols = lax.axis_size("col")
    mode_count, block_nodes = mode_shapes.shape
    packed = pack_block(coords, mode_shapes)
    partial = row_exchange(packed, rows, cols, mode_count)
    total = all_reduce(partial, rows, cols)
    modal_csd = total + total.T
    real_part = response_gain[0]
    imag_part = response_gain[1]
    weighted = (
        real_part[:, None] * real_part[None, :] + imag_part[:, None] * imag_part[None, :]
    ) * modal_csd
    weighted_high, weighted_low = split_parts(weighted)
    mapped = jnp.dot(output_shapes, weighted_high, preferred_element_type=jnp.float32)
    mapped = mapped + jnp.dot(output_shapes, weighted_low, preferred_element_type=jnp.float32)
    response_power = jnp.sum(mapped * output_shapes.astype(jnp.float32), axis=1)
    return (response_power, modal_csd)


def solution(mesh):
    in_specs = (P(None, ("row", "col")), P(None, ("row", "col")), P(("row", "col"), None), P())
    out_specs = (P(("row", "col")), P())
    return jax.shard_map(local, mesh=mesh, in_specs=in_specs, out_specs=out_specs, check_vma=False)
```

```python
import functools
import math

import jax
import jax.numpy as jnp
from jax import lax
from jax.experimental import pallas as pl
from jax.experimental.pallas import tpu as pltpu
from jax.sharding import PartitionSpec as P

wave_scale = 0.35 / 64.0


def coherence(left_points, right_points):
    difference = left_points[:, :, None] - right_points[:, None, :]
    squared = jnp.sum(difference * difference, axis=0)
    return jnp.sinc(wave_scale * jnp.sqrt(squared)).astype(jnp.bfloat16)


def split_parts(matrix):
    high_part = matrix.astype(jnp.bfloat16)
    low_part = (matrix - high_part.astype(jnp.float32)).astype(jnp.bfloat16)
    return (high_part, low_part)


def pack_block(coords, mode_shapes):
    wide = coords.astype(jnp.float32)
    high = jnp.floor(wide * (1.0 / 256.0))
    low = wide - 256.0 * high
    pad = jnp.zeros((10, wide.shape[1]), jnp.float32)
    extra = jnp.concatenate([high, low, pad], axis=0).astype(jnp.bfloat16)
    return jnp.concatenate([mode_shapes, extra], axis=0)


def unpack_points(packed, mode_count):
    high = packed[..., mode_count:mode_count + 3, :].astype(jnp.float32)
    low = packed[..., mode_count + 3:mode_count + 6, :].astype(jnp.float32)
    return high * 256.0 + low


CHUNK = 32
SIN_TERMS = [math.pi * (-1) ** k * math.pi ** (2 * k) / math.factorial(2 * k + 1) for k in range(6)]


def coherence_chunk(dx, dy, dz):
    squared = dx * dx + dy * dy + dz * dz
    safe = jnp.maximum(squared, 1e-30)
    root_inv = lax.rsqrt(safe)
    x = safe * root_inv * wave_scale
    n = jnp.floor(x + 0.5)
    f = x - n
    h = n * 0.5
    sign = 1.0 - 4.0 * (h - jnp.floor(h))
    f2 = f * f
    q = SIN_TERMS[4]
    for term in SIN_TERMS[3::-1]:
        q = q * f2 + term
    scale = f * root_inv * (1.0 / (math.pi * wave_scale))
    return sign * q * scale


def block_points(slot_ref, mode_count):
    tail = slot_ref[mode_count:mode_count + 16, :].astype(jnp.float32)
    return [tail[k:k + 1, :] * 256.0 + tail[k + 3:k + 4, :] for k in range(3)]


def accumulate_block(slot_ref, weight, rowpts_ref, out_ref, tile_ref, mode_count):
    bx, by, bz = block_points(slot_ref, mode_count)
    length = tile_ref.shape[0]

    def chunk(c, carry):
        r0 = pl.multiple_of(c * CHUNK, CHUNK)
        dx = rowpts_ref[0, pl.ds(r0, CHUNK), :] - bx
        dy = rowpts_ref[1, pl.ds(r0, CHUNK), :] - by
        dz = rowpts_ref[2, pl.ds(r0, CHUNK), :] - bz
        tile_ref[pl.ds(r0, CHUNK), :] = coherence_chunk(dx, dy, dz).astype(jnp.bfloat16)
        return carry

    lax.fori_loop(0, length // CHUNK, chunk, 0)
    shapes = slot_ref[0:mode_count, :]
    product = lax.dot_general(
        tile_ref[...], shapes, (((1,), (1,)), ((), ())), preferred_element_type=jnp.float32
    )
    out_ref[...] += weight * product


def shift_of(j, rows):
    odd = j % 2
    return odd * j + (1 - odd) * (rows - j)


def row_kernel(rows, cols, mode_count, packed_ref, out_ref, recv, colbuf, rowpts_ref, tile_ref, acc_ref,
               send_sems, recv_sems, col_send, col_recv):
    me = lax.axis_index("row")
    col = lax.axis_index("col")
    half = rows // 2
    nodes = packed_ref.shape[1]
    colbuf[...] = jnp.zeros_like(colbuf)
    barrier = pltpu.get_barrier_semaphore()
    for p in range(1, rows):
        pl.semaphore_signal(
            barrier, 1, device_id=(lax.rem(me + p, rows), col), device_id_type=pl.DeviceIdType.MESH
        )
    for p in range(1, cols):
        pl.semaphore_signal(
            barrier, 1, device_id=(me, lax.rem(col + p, cols)), device_id_type=pl.DeviceIdType.MESH
        )
    pl.semaphore_wait(barrier, rows - 1 + cols - 1)

    def col_copy(s, slot):
        return pltpu.make_async_remote_copy(
            src_ref=packed_ref,
            dst_ref=colbuf.at[slot],
            send_sem=col_send.at[s],
            recv_sem=col_recv.at[slot],
            device_id=(me, s),
            device_id_type=pl.DeviceIdType.MESH,
        )

    def transfer(k):
        target = lax.rem(me + rows - shift_of(k + 1, rows), rows)
        return pltpu.make_async_remote_copy(
            src_ref=packed_ref,
            dst_ref=recv.at[k],
            send_sem=send_sems.at[k],
            recv_sem=recv_sems.at[k],
            device_id=(target, col),
            device_id_type=pl.DeviceIdType.MESH,
        )

    for s in range(cols):
        @pl.when(s != col)
        def _():
            col_copy(s, col).start()
    for k in range(half):
        transfer(k).start()
    for s in range(cols):
        @pl.when(s != col)
        def _():
            col_copy(s, s).wait_recv()

    eye = (lax.broadcasted_iota(jnp.int32, (nodes, nodes), 0)
           == lax.broadcasted_iota(jnp.int32, (nodes, nodes), 1)).astype(jnp.bfloat16)
    own_tail = packed_ref[mode_count:mode_count + 16, :]
    for s in range(cols):
        tail = jnp.where(s == col, own_tail, colbuf[s, mode_count:mode_count + 16, :])
        moved = lax.dot_general(eye, tail, (((1,), (1,)), ((), ())), preferred_element_type=jnp.float32)
        for k in range(3):
            column = moved[:, k:k + 1] * 256.0 + moved[:, k + 3:k + 4]
            rowpts_ref[k, s * nodes:(s + 1) * nodes, :] = jnp.broadcast_to(column, (nodes, nodes))

    acc_ref[...] = jnp.zeros_like(acc_ref)
    accumulate_block(packed_ref, 0.5, rowpts_ref, acc_ref, tile_ref, mode_count)

    def step(k, carry):
        transfer(k).wait_recv()
        weight = jnp.where(k == half - 1, 0.5, 1.0).astype(jnp.float32)
        accumulate_block(recv.at[k], weight, rowpts_ref, acc_ref, tile_ref, mode_count)
        return carry

    lax.fori_loop(0, half, step, 0)

    own_shapes = packed_ref[0:mode_count, :]
    partial = jnp.zeros(out_ref.shape, jnp.float32)
    for s in range(cols):
        shapes = jnp.where(s == col, own_shapes, colbuf[s, 0:mode_count, :])
        part = acc_ref[s * nodes:(s + 1) * nodes, :]
        high = part.astype(jnp.bfloat16)
        low = (part - high.astype(jnp.float32)).astype(jnp.bfloat16)
        partial = partial + jnp.dot(shapes, high, preferred_element_type=jnp.float32)
        partial = partial + jnp.dot(shapes, low, preferred_element_type=jnp.float32)
    out_ref[...] = partial

    for k in range(half):
        transfer(k).wait_send()
    for s in range(cols):
        @pl.when(s != col)
        def _():
            col_copy(s, col).wait_send()


def row_exchange(packed, rows, cols, mode_count):
    nodes = packed.shape[1]
    length = cols * nodes
    half = rows // 2
    vmem = pltpu.MemorySpace.VMEM
    flops = 2 * (half + 1) * length * nodes * mode_count + 4 * length * mode_count * mode_count
    return pl.pallas_call(
        functools.partial(row_kernel, rows, cols, mode_count),
        out_shape=jax.ShapeDtypeStruct((mode_count, mode_count), jnp.float32),
        in_specs=[pl.BlockSpec(memory_space=vmem)],
        out_specs=pl.BlockSpec(memory_space=vmem),
        scratch_shapes=[
            pltpu.VMEM((half,) + packed.shape, packed.dtype),
            pltpu.VMEM((cols,) + packed.shape, packed.dtype),
            pltpu.VMEM((3, length, nodes), jnp.float32),
            pltpu.VMEM((length, nodes), jnp.bfloat16),
            pltpu.VMEM((length, mode_count), jnp.float32),
            pltpu.SemaphoreType.DMA((half,)),
            pltpu.SemaphoreType.DMA((half,)),
            pltpu.SemaphoreType.DMA((cols,)),
            pltpu.SemaphoreType.DMA((cols,)),
        ],
        compiler_params=pltpu.CompilerParams(
            collective_id=0, has_side_effects=True, vmem_limit_bytes=48 * 1024 * 1024
        ),
        cost_estimate=pl.CostEstimate(
            flops=flops, transcendentals=(half + 1) * length * nodes, bytes_accessed=4 * 1024 * 1024
        ),
    )(packed)

def gather_all(block, axis, count):
    spread = jnp.broadcast_to(block[None], (count,) + block.shape)
    return lax.all_to_all(spread, axis, 0, 0, tiled=True)


def ar_kernel(rows, cols, y_ref, out_ref, buf_a, buf_b, buf_g, buf_c, red_a, red_b, red_c,
              sa, ra, sb, rb, sg, rg, sc, rc):
    me_r = lax.axis_index("row")
    me_c = lax.axis_index("col")
    buf_a[...] = jnp.zeros_like(buf_a)
    buf_b[...] = jnp.zeros_like(buf_b)
    buf_g[...] = jnp.zeros_like(buf_g)
    buf_c[...] = jnp.zeros_like(buf_c)
    barrier = pltpu.get_barrier_semaphore()
    for p in range(1, cols):
        pl.semaphore_signal(
            barrier, 1, device_id=(me_r, lax.rem(me_c + p, cols)), device_id_type=pl.DeviceIdType.MESH
        )
    for p in range(1, rows):
        pl.semaphore_signal(
            barrier, 1, device_id=(lax.rem(me_r + p, rows), me_c), device_id_type=pl.DeviceIdType.MESH
        )
    pl.semaphore_wait(barrier, cols - 1 + rows - 1)

    def copy(src, dst, send, recv, sem_index, slot, peer):
        return pltpu.make_async_remote_copy(
            src_ref=src,
            dst_ref=dst,
            send_sem=send.at[sem_index],
            recv_sem=recv.at[slot],
            device_id=peer,
            device_id_type=pl.DeviceIdType.MESH,
        )

    def exchange(src_of, dst_of, send, recv, count, me, peer_of):
        for s in range(count):
            @pl.when(s != me)
            def _():
                copy(src_of(s), dst_of(me), send, recv, s, me, peer_of(s)).start()
        for s in range(count):
            @pl.when(s != me)
            def _():
                copy(src_of(s), dst_of(s), send, recv, s, s, peer_of(s)).wait_recv()

    def finish(src_of, dst_of, send, recv, count, me, peer_of):
        for s in range(count):
            @pl.when(s != me)
            def _():
                copy(src_of(s), dst_of(me), send, recv, s, me, peer_of(s)).wait_send()

    col_peer = lambda s: (me_r, s)
    row_peer = lambda s: (s, me_c)
    col_a = (lambda s: y_ref.at[s], lambda s: buf_a.at[s], sa, ra, cols, me_c, col_peer)
    exchange(*col_a)
    chunk = y_ref[me_c]
    for s in range(cols):
        chunk = chunk + buf_a[s]
    red_a[...] = chunk
    row_b = (lambda s: red_a.at[pl.ds(s, 1)], lambda s: buf_b.at[pl.ds(s, 1)], sb, rb, rows, me_r, row_peer)
    exchange(*row_b)
    piece = red_a[pl.ds(me_r, 1), :] + jnp.sum(buf_b[...], axis=0, keepdims=True)
    red_b[...] = piece
    row_g = (lambda s: red_b, lambda s: buf_g.at[pl.ds(s, 1)], sg, rg, rows, me_r, row_peer)
    exchange(*row_g)
    lines = lax.broadcasted_iota(jnp.int32, chunk.shape, 0)
    total = jnp.where(lines == me_r, jnp.broadcast_to(piece, chunk.shape), buf_g[...])
    red_c[...] = total
    col_c = (lambda s: red_c, lambda s: buf_c.at[s], sc, rc, cols, me_c, col_peer)
    exchange(*col_c)
    for s in range(cols):
        out_ref[s] = jnp.where(s == me_c, total, buf_c[s])
    finish(*col_a)
    finish(*row_b)
    finish(*row_g)
    finish(*col_c)


def all_reduce(matrix, rows, cols):
    pieces = matrix.reshape(cols, rows, -1)
    shape = pieces.shape
    vmem = pltpu.MemorySpace.VMEM
    total = pl.pallas_call(
        functools.partial(ar_kernel, rows, cols),
        out_shape=jax.ShapeDtypeStruct(shape, jnp.float32),
        in_specs=[pl.BlockSpec(memory_space=vmem)],
        out_specs=pl.BlockSpec(memory_space=vmem),
        scratch_shapes=[
            pltpu.VMEM(shape, jnp.float32),
            pltpu.VMEM(shape[1:], jnp.float32),
            pltpu.VMEM(shape[1:], jnp.float32),
            pltpu.VMEM(shape, jnp.float32),
            pltpu.VMEM(shape[1:], jnp.float32),
            pltpu.VMEM((1, shape[2]), jnp.float32),
            pltpu.VMEM(shape[1:], jnp.float32),
            pltpu.SemaphoreType.DMA((cols,)),
            pltpu.SemaphoreType.DMA((cols,)),
            pltpu.SemaphoreType.DMA((rows,)),
            pltpu.SemaphoreType.DMA((rows,)),
            pltpu.SemaphoreType.DMA((rows,)),
            pltpu.SemaphoreType.DMA((rows,)),
            pltpu.SemaphoreType.DMA((cols,)),
            pltpu.SemaphoreType.DMA((cols,)),
        ],
        compiler_params=pltpu.CompilerParams(collective_id=1, has_side_effects=True),
    )(pieces)
    return total.reshape(matrix.shape)

def local(coords, mode_shapes, output_shapes, response_gain):
    rows = lax.axis_size("row")
    cols = lax.axis_size("col")
    mode_count, block_nodes = mode_shapes.shape
    packed = pack_block(coords, mode_shapes)
    partial = row_exchange(packed, rows, cols, mode_count)
    total = all_reduce(partial, rows, cols)
    modal_csd = total + total.T
    real_part = response_gain[0]
    imag_part = response_gain[1]
    weighted = (
        real_part[:, None] * real_part[None, :] + imag_part[:, None] * imag_part[None, :]
    ) * modal_csd
    weighted_high, weighted_low = split_parts(weighted)
    mapped = jnp.dot(output_shapes, weighted_high, preferred_element_type=jnp.float32)
    mapped = mapped + jnp.dot(output_shapes, weighted_low, preferred_element_type=jnp.float32)
    response_power = jnp.sum(mapped * output_shapes.astype(jnp.float32), axis=1)
    return (response_power, modal_csd)


def solution(mesh):
    in_specs = (P(None, ("row", "col")), P(None, ("row", "col")), P(("row", "col"), None), P())
    out_specs = (P(("row", "col")), P())
    return jax.shard_map(local, mesh=mesh, in_specs=in_specs, out_specs=out_specs, check_vma=False)
```

```python
import functools
import math

import jax
import jax.numpy as jnp
from jax import lax
from jax.experimental import pallas as pl
from jax.experimental.pallas import tpu as pltpu
from jax.sharding import PartitionSpec as P

wave_scale = 0.35 / 64.0


def coherence(left_points, right_points):
    difference = left_points[:, :, None] - right_points[:, None, :]
    squared = jnp.sum(difference * difference, axis=0)
    return jnp.sinc(wave_scale * jnp.sqrt(squared)).astype(jnp.bfloat16)


def split_parts(matrix):
    high_part = matrix.astype(jnp.bfloat16)
    low_part = (matrix - high_part.astype(jnp.float32)).astype(jnp.bfloat16)
    return (high_part, low_part)


def pack_block(coords, mode_shapes):
    wide = coords.astype(jnp.float32)
    high = jnp.floor(wide * (1.0 / 256.0))
    low = wide - 256.0 * high
    pad = jnp.zeros((10, wide.shape[1]), jnp.float32)
    extra = jnp.concatenate([high, low, pad], axis=0).astype(jnp.bfloat16)
    return jnp.concatenate([mode_shapes, extra], axis=0)


def unpack_points(packed, mode_count):
    high = packed[..., mode_count:mode_count + 3, :].astype(jnp.float32)
    low = packed[..., mode_count + 3:mode_count + 6, :].astype(jnp.float32)
    return high * 256.0 + low


CHUNK = 32
SIN_TERMS = [math.pi * (-1) ** k * math.pi ** (2 * k) / math.factorial(2 * k + 1) for k in range(6)]


def coherence_chunk(dx, dy, dz):
    squared = dx * dx + dy * dy + dz * dz
    safe = jnp.maximum(squared, 1e-30)
    root_inv = lax.rsqrt(safe)
    x = safe * root_inv * wave_scale
    n = jnp.floor(x + 0.5)
    f = x - n
    h = n * 0.5
    sign = 1.0 - 4.0 * (h - jnp.floor(h))
    f2 = f * f
    q = SIN_TERMS[4]
    for term in SIN_TERMS[3::-1]:
        q = q * f2 + term
    scale = f * root_inv * (1.0 / (math.pi * wave_scale))
    return sign * q * scale


def block_points(slot_ref, mode_count):
    tail = slot_ref[mode_count:mode_count + 16, :].astype(jnp.float32)
    return [tail[k:k + 1, :] * 256.0 + tail[k + 3:k + 4, :] for k in range(3)]


def accumulate_block(slot_ref, weight, rowpts_ref, out_ref, tile_ref, mode_count):
    bx, by, bz = block_points(slot_ref, mode_count)
    length = tile_ref.shape[0]

    def chunk(c, carry):
        r0 = pl.multiple_of(c * CHUNK, CHUNK)
        dx = rowpts_ref[0, pl.ds(r0, CHUNK), :] - bx
        dy = rowpts_ref[1, pl.ds(r0, CHUNK), :] - by
        dz = rowpts_ref[2, pl.ds(r0, CHUNK), :] - bz
        tile_ref[pl.ds(r0, CHUNK), :] = coherence_chunk(dx, dy, dz).astype(jnp.bfloat16)
        return carry

    lax.fori_loop(0, length // CHUNK, chunk, 0, unroll=2)
    shapes = slot_ref[0:mode_count, :]
    product = lax.dot_general(
        tile_ref[...], shapes, (((1,), (1,)), ((), ())), preferred_element_type=jnp.float32
    )
    out_ref[...] += weight * product


def shift_of(j, rows):
    odd = j % 2
    return odd * j + (1 - odd) * (rows - j)


def row_kernel(rows, cols, mode_count, packed_ref, out_ref, recv, colbuf, rowpts_ref, tile_ref, acc_ref,
               send_sems, recv_sems, col_send, col_recv):
    me = lax.axis_index("row")
    col = lax.axis_index("col")
    half = rows // 2
    nodes = packed_ref.shape[1]
    colbuf[...] = jnp.zeros_like(colbuf)
    barrier = pltpu.get_barrier_semaphore()
    for p in range(1, rows):
        pl.semaphore_signal(
            barrier, 1, device_id=(lax.rem(me + p, rows), col), device_id_type=pl.DeviceIdType.MESH
        )
    for p in range(1, cols):
        pl.semaphore_signal(
            barrier, 1, device_id=(me, lax.rem(col + p, cols)), device_id_type=pl.DeviceIdType.MESH
        )
    pl.semaphore_wait(barrier, rows - 1 + cols - 1)

    def col_copy(s, slot):
        return pltpu.make_async_remote_copy(
            src_ref=packed_ref,
            dst_ref=colbuf.at[slot],
            send_sem=col_send.at[s],
            recv_sem=col_recv.at[slot],
            device_id=(me, s),
            device_id_type=pl.DeviceIdType.MESH,
        )

    def transfer(k):
        target = lax.rem(me + rows - shift_of(k + 1, rows), rows)
        return pltpu.make_async_remote_copy(
            src_ref=packed_ref,
            dst_ref=recv.at[k],
            send_sem=send_sems.at[k],
            recv_sem=recv_sems.at[k],
            device_id=(target, col),
            device_id_type=pl.DeviceIdType.MESH,
        )

    for s in range(cols):
        @pl.when(s != col)
        def _():
            col_copy(s, col).start()
    for k in range(half):
        transfer(k).start()
    for s in range(cols):
        @pl.when(s != col)
        def _():
            col_copy(s, s).wait_recv()

    eye = (lax.broadcasted_iota(jnp.int32, (nodes, nodes), 0)
           == lax.broadcasted_iota(jnp.int32, (nodes, nodes), 1)).astype(jnp.bfloat16)
    own_tail = packed_ref[mode_count:mode_count + 16, :]
    for s in range(cols):
        tail = jnp.where(s == col, own_tail, colbuf[s, mode_count:mode_count + 16, :])
        moved = lax.dot_general(eye, tail, (((1,), (1,)), ((), ())), preferred_element_type=jnp.float32)
        for k in range(3):
            column = moved[:, k:k + 1] * 256.0 + moved[:, k + 3:k + 4]
            rowpts_ref[k, s * nodes:(s + 1) * nodes, :] = jnp.broadcast_to(column, (nodes, nodes))

    acc_ref[...] = jnp.zeros_like(acc_ref)
    accumulate_block(packed_ref, 0.5, rowpts_ref, acc_ref, tile_ref, mode_count)

    def step(k, carry):
        transfer(k).wait_recv()
        weight = jnp.where(k == half - 1, 0.5, 1.0).astype(jnp.float32)
        accumulate_block(recv.at[k], weight, rowpts_ref, acc_ref, tile_ref, mode_count)
        return carry

    lax.fori_loop(0, half, step, 0)

    own_shapes = packed_ref[0:mode_count, :]
    partial = jnp.zeros(out_ref.shape, jnp.float32)
    for s in range(cols):
        shapes = jnp.where(s == col, own_shapes, colbuf[s, 0:mode_count, :])
        part = acc_ref[s * nodes:(s + 1) * nodes, :]
        high = part.astype(jnp.bfloat16)
        low = (part - high.astype(jnp.float32)).astype(jnp.bfloat16)
        partial = partial + jnp.dot(shapes, high, preferred_element_type=jnp.float32)
        partial = partial + jnp.dot(shapes, low, preferred_element_type=jnp.float32)
    out_ref[...] = partial

    for k in range(half):
        transfer(k).wait_send()
    for s in range(cols):
        @pl.when(s != col)
        def _():
            col_copy(s, col).wait_send()


def row_exchange(packed, rows, cols, mode_count):
    nodes = packed.shape[1]
    length = cols * nodes
    half = rows // 2
    vmem = pltpu.MemorySpace.VMEM
    flops = 2 * (half + 1) * length * nodes * mode_count + 4 * length * mode_count * mode_count
    return pl.pallas_call(
        functools.partial(row_kernel, rows, cols, mode_count),
        out_shape=jax.ShapeDtypeStruct((mode_count, mode_count), jnp.float32),
        in_specs=[pl.BlockSpec(memory_space=vmem)],
        out_specs=pl.BlockSpec(memory_space=vmem),
        scratch_shapes=[
            pltpu.VMEM((half,) + packed.shape, packed.dtype),
            pltpu.VMEM((cols,) + packed.shape, packed.dtype),
            pltpu.VMEM((3, length, nodes), jnp.float32),
            pltpu.VMEM((length, nodes), jnp.bfloat16),
            pltpu.VMEM((length, mode_count), jnp.float32),
            pltpu.SemaphoreType.DMA((half,)),
            pltpu.SemaphoreType.DMA((half,)),
            pltpu.SemaphoreType.DMA((cols,)),
            pltpu.SemaphoreType.DMA((cols,)),
        ],
        compiler_params=pltpu.CompilerParams(
            collective_id=0, has_side_effects=True, vmem_limit_bytes=48 * 1024 * 1024
        ),
        cost_estimate=pl.CostEstimate(
            flops=flops, transcendentals=(half + 1) * length * nodes, bytes_accessed=4 * 1024 * 1024
        ),
    )(packed)

def gather_all(block, axis, count):
    spread = jnp.broadcast_to(block[None], (count,) + block.shape)
    return lax.all_to_all(spread, axis, 0, 0, tiled=True)


def ar_kernel(rows, cols, y_ref, out_ref, buf_a, buf_b, buf_g, buf_c, red_a, red_b, red_c,
              sa, ra, sb, rb, sg, rg, sc, rc):
    me_r = lax.axis_index("row")
    me_c = lax.axis_index("col")
    buf_a[...] = jnp.zeros_like(buf_a)
    buf_b[...] = jnp.zeros_like(buf_b)
    buf_g[...] = jnp.zeros_like(buf_g)
    buf_c[...] = jnp.zeros_like(buf_c)
    barrier = pltpu.get_barrier_semaphore()
    for p in range(1, cols):
        pl.semaphore_signal(
            barrier, 1, device_id=(me_r, lax.rem(me_c + p, cols)), device_id_type=pl.DeviceIdType.MESH
        )
    for p in range(1, rows):
        pl.semaphore_signal(
            barrier, 1, device_id=(lax.rem(me_r + p, rows), me_c), device_id_type=pl.DeviceIdType.MESH
        )
    pl.semaphore_wait(barrier, cols - 1 + rows - 1)

    def copy(src, dst, send, recv, sem_index, slot, peer):
        return pltpu.make_async_remote_copy(
            src_ref=src,
            dst_ref=dst,
            send_sem=send.at[sem_index],
            recv_sem=recv.at[slot],
            device_id=peer,
            device_id_type=pl.DeviceIdType.MESH,
        )

    def exchange(src_of, dst_of, send, recv, count, me, peer_of):
        for s in range(count):
            @pl.when(s != me)
            def _():
                copy(src_of(s), dst_of(me), send, recv, s, me, peer_of(s)).start()
        for s in range(count):
            @pl.when(s != me)
            def _():
                copy(src_of(s), dst_of(s), send, recv, s, s, peer_of(s)).wait_recv()

    def finish(src_of, dst_of, send, recv, count, me, peer_of):
        for s in range(count):
            @pl.when(s != me)
            def _():
                copy(src_of(s), dst_of(me), send, recv, s, me, peer_of(s)).wait_send()

    col_peer = lambda s: (me_r, s)
    row_peer = lambda s: (s, me_c)
    col_a = (lambda s: y_ref.at[s], lambda s: buf_a.at[s], sa, ra, cols, me_c, col_peer)
    exchange(*col_a)
    chunk = y_ref[me_c]
    for s in range(cols):
        chunk = chunk + buf_a[s]
    red_a[...] = chunk
    row_b = (lambda s: red_a.at[pl.ds(s, 1)], lambda s: buf_b.at[pl.ds(s, 1)], sb, rb, rows, me_r, row_peer)
    exchange(*row_b)
    piece = red_a[pl.ds(me_r, 1), :] + jnp.sum(buf_b[...], axis=0, keepdims=True)
    red_b[...] = piece
    row_g = (lambda s: red_b, lambda s: buf_g.at[pl.ds(s, 1)], sg, rg, rows, me_r, row_peer)
    exchange(*row_g)
    lines = lax.broadcasted_iota(jnp.int32, chunk.shape, 0)
    total = jnp.where(lines == me_r, jnp.broadcast_to(piece, chunk.shape), buf_g[...])
    red_c[...] = total
    col_c = (lambda s: red_c, lambda s: buf_c.at[s], sc, rc, cols, me_c, col_peer)
    exchange(*col_c)
    for s in range(cols):
        out_ref[s] = jnp.where(s == me_c, total, buf_c[s])
    finish(*col_a)
    finish(*row_b)
    finish(*row_g)
    finish(*col_c)


def all_reduce(matrix, rows, cols):
    pieces = matrix.reshape(cols, rows, -1)
    shape = pieces.shape
    vmem = pltpu.MemorySpace.VMEM
    total = pl.pallas_call(
        functools.partial(ar_kernel, rows, cols),
        out_shape=jax.ShapeDtypeStruct(shape, jnp.float32),
        in_specs=[pl.BlockSpec(memory_space=vmem)],
        out_specs=pl.BlockSpec(memory_space=vmem),
        scratch_shapes=[
            pltpu.VMEM(shape, jnp.float32),
            pltpu.VMEM(shape[1:], jnp.float32),
            pltpu.VMEM(shape[1:], jnp.float32),
            pltpu.VMEM(shape, jnp.float32),
            pltpu.VMEM(shape[1:], jnp.float32),
            pltpu.VMEM((1, shape[2]), jnp.float32),
            pltpu.VMEM(shape[1:], jnp.float32),
            pltpu.SemaphoreType.DMA((cols,)),
            pltpu.SemaphoreType.DMA((cols,)),
            pltpu.SemaphoreType.DMA((rows,)),
            pltpu.SemaphoreType.DMA((rows,)),
            pltpu.SemaphoreType.DMA((rows,)),
            pltpu.SemaphoreType.DMA((rows,)),
            pltpu.SemaphoreType.DMA((cols,)),
            pltpu.SemaphoreType.DMA((cols,)),
        ],
        compiler_params=pltpu.CompilerParams(collective_id=1, has_side_effects=True),
    )(pieces)
    return total.reshape(matrix.shape)

def local(coords, mode_shapes, output_shapes, response_gain):
    rows = lax.axis_size("row")
    cols = lax.axis_size("col")
    mode_count, block_nodes = mode_shapes.shape
    packed = pack_block(coords, mode_shapes)
    partial = row_exchange(packed, rows, cols, mode_count)
    total = all_reduce(partial, rows, cols)
    modal_csd = total + total.T
    real_part = response_gain[0]
    imag_part = response_gain[1]
    weighted = (
        real_part[:, None] * real_part[None, :] + imag_part[:, None] * imag_part[None, :]
    ) * modal_csd
    weighted_high, weighted_low = split_parts(weighted)
    mapped = jnp.dot(output_shapes, weighted_high, preferred_element_type=jnp.float32)
    mapped = mapped + jnp.dot(output_shapes, weighted_low, preferred_element_type=jnp.float32)
    response_power = jnp.sum(mapped * output_shapes.astype(jnp.float32), axis=1)
    return (response_power, modal_csd)


def solution(mesh):
    in_specs = (P(None, ("row", "col")), P(None, ("row", "col")), P(("row", "col"), None), P())
    out_specs = (P(("row", "col")), P())
    return jax.shard_map(local, mesh=mesh, in_specs=in_specs, out_specs=out_specs, check_vma=False)
```

```python
import functools
import math

import jax
import jax.numpy as jnp
from jax import lax
from jax.experimental import pallas as pl
from jax.experimental.pallas import tpu as pltpu
from jax.sharding import PartitionSpec as P

wave_scale = 0.35 / 64.0


def coherence(left_points, right_points):
    difference = left_points[:, :, None] - right_points[:, None, :]
    squared = jnp.sum(difference * difference, axis=0)
    return jnp.sinc(wave_scale * jnp.sqrt(squared)).astype(jnp.bfloat16)


def split_parts(matrix):
    high_part = matrix.astype(jnp.bfloat16)
    low_part = (matrix - high_part.astype(jnp.float32)).astype(jnp.bfloat16)
    return (high_part, low_part)


def pack_block(coords, mode_shapes):
    wide = coords.astype(jnp.float32)
    high = jnp.floor(wide * (1.0 / 256.0))
    low = wide - 256.0 * high
    pad = jnp.zeros((10, wide.shape[1]), jnp.float32)
    extra = jnp.concatenate([high, low, pad], axis=0).astype(jnp.bfloat16)
    return jnp.concatenate([mode_shapes, extra], axis=0)


def unpack_points(packed, mode_count):
    high = packed[..., mode_count:mode_count + 3, :].astype(jnp.float32)
    low = packed[..., mode_count + 3:mode_count + 6, :].astype(jnp.float32)
    return high * 256.0 + low


CHUNK = 32
SIN_TERMS = [math.pi * (-1) ** k * math.pi ** (2 * k) / math.factorial(2 * k + 1) for k in range(6)]


def coherence_chunk(dx, dy, dz):
    squared = dx * dx + dy * dy + dz * dz
    safe = jnp.maximum(squared, 1e-30)
    root_inv = lax.rsqrt(safe)
    x = safe * root_inv * wave_scale
    n = jnp.floor(x + 0.5)
    f = x - n
    h = n * 0.5
    sign = 1.0 - 4.0 * (h - jnp.floor(h))
    f2 = f * f
    q = SIN_TERMS[4]
    for term in SIN_TERMS[3::-1]:
        q = q * f2 + term
    scale = f * root_inv * (1.0 / (math.pi * wave_scale))
    return sign * q * scale


def block_points(slot_ref, mode_count):
    tail = slot_ref[mode_count:mode_count + 16, :].astype(jnp.float32)
    return [tail[k:k + 1, :] * 256.0 + tail[k + 3:k + 4, :] for k in range(3)]


def accumulate_block(slot_ref, weight, rowpts_ref, out_ref, tile_ref, mode_count):
    bx, by, bz = block_points(slot_ref, mode_count)
    length = tile_ref.shape[0]

    def chunk(c, carry):
        r0 = pl.multiple_of(c * CHUNK, CHUNK)
        dx = rowpts_ref[0, pl.ds(r0, CHUNK), :] - bx
        dy = rowpts_ref[1, pl.ds(r0, CHUNK), :] - by
        dz = rowpts_ref[2, pl.ds(r0, CHUNK), :] - bz
        tile_ref[pl.ds(r0, CHUNK), :] = coherence_chunk(dx, dy, dz).astype(jnp.bfloat16)
        return carry

    lax.fori_loop(0, length // CHUNK, chunk, 0, unroll=4)
    shapes = slot_ref[0:mode_count, :]
    product = lax.dot_general(
        tile_ref[...], shapes, (((1,), (1,)), ((), ())), preferred_element_type=jnp.float32
    )
    out_ref[...] += weight * product


def shift_of(j, rows):
    odd = j % 2
    return odd * j + (1 - odd) * (rows - j)


def row_kernel(rows, cols, mode_count, packed_ref, out_ref, recv, colbuf, rowpts_ref, tile_ref, acc_ref,
               send_sems, recv_sems, col_send, col_recv):
    me = lax.axis_index("row")
    col = lax.axis_index("col")
    half = rows // 2
    nodes = packed_ref.shape[1]
    colbuf[...] = jnp.zeros_like(colbuf)
    barrier = pltpu.get_barrier_semaphore()
    for p in range(1, rows):
        pl.semaphore_signal(
            barrier, 1, device_id=(lax.rem(me + p, rows), col), device_id_type=pl.DeviceIdType.MESH
        )
    for p in range(1, cols):
        pl.semaphore_signal(
            barrier, 1, device_id=(me, lax.rem(col + p, cols)), device_id_type=pl.DeviceIdType.MESH
        )
    pl.semaphore_wait(barrier, rows - 1 + cols - 1)

    def col_copy(s, slot):
        return pltpu.make_async_remote_copy(
            src_ref=packed_ref,
            dst_ref=colbuf.at[slot],
            send_sem=col_send.at[s],
            recv_sem=col_recv.at[slot],
            device_id=(me, s),
            device_id_type=pl.DeviceIdType.MESH,
        )

    def transfer(k):
        target = lax.rem(me + rows - shift_of(k + 1, rows), rows)
        return pltpu.make_async_remote_copy(
            src_ref=packed_ref,
            dst_ref=recv.at[k],
            send_sem=send_sems.at[k],
            recv_sem=recv_sems.at[k],
            device_id=(target, col),
            device_id_type=pl.DeviceIdType.MESH,
        )

    for s in range(cols):
        @pl.when(s != col)
        def _():
            col_copy(s, col).start()
    for k in range(half):
        transfer(k).start()
    for s in range(cols):
        @pl.when(s != col)
        def _():
            col_copy(s, s).wait_recv()

    eye = (lax.broadcasted_iota(jnp.int32, (nodes, nodes), 0)
           == lax.broadcasted_iota(jnp.int32, (nodes, nodes), 1)).astype(jnp.bfloat16)
    own_tail = packed_ref[mode_count:mode_count + 16, :]
    for s in range(cols):
        tail = jnp.where(s == col, own_tail, colbuf[s, mode_count:mode_count + 16, :])
        moved = lax.dot_general(eye, tail, (((1,), (1,)), ((), ())), preferred_element_type=jnp.float32)
        for k in range(3):
            column = moved[:, k:k + 1] * 256.0 + moved[:, k + 3:k + 4]
            rowpts_ref[k, s * nodes:(s + 1) * nodes, :] = jnp.broadcast_to(column, (nodes, nodes))

    acc_ref[...] = jnp.zeros_like(acc_ref)
    accumulate_block(packed_ref, 0.5, rowpts_ref, acc_ref, tile_ref, mode_count)

    def step(k, carry):
        transfer(k).wait_recv()
        weight = jnp.where(k == half - 1, 0.5, 1.0).astype(jnp.float32)
        accumulate_block(recv.at[k], weight, rowpts_ref, acc_ref, tile_ref, mode_count)
        return carry

    lax.fori_loop(0, half, step, 0)

    own_shapes = packed_ref[0:mode_count, :]
    partial = jnp.zeros(out_ref.shape, jnp.float32)
    for s in range(cols):
        shapes = jnp.where(s == col, own_shapes, colbuf[s, 0:mode_count, :])
        part = acc_ref[s * nodes:(s + 1) * nodes, :]
        high = part.astype(jnp.bfloat16)
        low = (part - high.astype(jnp.float32)).astype(jnp.bfloat16)
        partial = partial + jnp.dot(shapes, high, preferred_element_type=jnp.float32)
        partial = partial + jnp.dot(shapes, low, preferred_element_type=jnp.float32)
    out_ref[...] = partial

    for k in range(half):
        transfer(k).wait_send()
    for s in range(cols):
        @pl.when(s != col)
        def _():
            col_copy(s, col).wait_send()


def row_exchange(packed, rows, cols, mode_count):
    nodes = packed.shape[1]
    length = cols * nodes
    half = rows // 2
    vmem = pltpu.MemorySpace.VMEM
    flops = 2 * (half + 1) * length * nodes * mode_count + 4 * length * mode_count * mode_count
    return pl.pallas_call(
        functools.partial(row_kernel, rows, cols, mode_count),
        out_shape=jax.ShapeDtypeStruct((mode_count, mode_count), jnp.float32),
        in_specs=[pl.BlockSpec(memory_space=vmem)],
        out_specs=pl.BlockSpec(memory_space=vmem),
        scratch_shapes=[
            pltpu.VMEM((half,) + packed.shape, packed.dtype),
            pltpu.VMEM((cols,) + packed.shape, packed.dtype),
            pltpu.VMEM((3, length, nodes), jnp.float32),
            pltpu.VMEM((length, nodes), jnp.bfloat16),
            pltpu.VMEM((length, mode_count), jnp.float32),
            pltpu.SemaphoreType.DMA((half,)),
            pltpu.SemaphoreType.DMA((half,)),
            pltpu.SemaphoreType.DMA((cols,)),
            pltpu.SemaphoreType.DMA((cols,)),
        ],
        compiler_params=pltpu.CompilerParams(
            collective_id=0, has_side_effects=True, vmem_limit_bytes=48 * 1024 * 1024
        ),
        cost_estimate=pl.CostEstimate(
            flops=flops, transcendentals=(half + 1) * length * nodes, bytes_accessed=4 * 1024 * 1024
        ),
    )(packed)

def gather_all(block, axis, count):
    spread = jnp.broadcast_to(block[None], (count,) + block.shape)
    return lax.all_to_all(spread, axis, 0, 0, tiled=True)


def ar_kernel(rows, cols, y_ref, out_ref, buf_a, buf_b, buf_g, buf_c, red_a, red_b, red_c,
              sa, ra, sb, rb, sg, rg, sc, rc):
    me_r = lax.axis_index("row")
    me_c = lax.axis_index("col")
    buf_a[...] = jnp.zeros_like(buf_a)
    buf_b[...] = jnp.zeros_like(buf_b)
    buf_g[...] = jnp.zeros_like(buf_g)
    buf_c[...] = jnp.zeros_like(buf_c)
    barrier = pltpu.get_barrier_semaphore()
    for p in range(1, cols):
        pl.semaphore_signal(
            barrier, 1, device_id=(me_r, lax.rem(me_c + p, cols)), device_id_type=pl.DeviceIdType.MESH
        )
    for p in range(1, rows):
        pl.semaphore_signal(
            barrier, 1, device_id=(lax.rem(me_r + p, rows), me_c), device_id_type=pl.DeviceIdType.MESH
        )
    pl.semaphore_wait(barrier, cols - 1 + rows - 1)

    def copy(src, dst, send, recv, sem_index, slot, peer):
        return pltpu.make_async_remote_copy(
            src_ref=src,
            dst_ref=dst,
            send_sem=send.at[sem_index],
            recv_sem=recv.at[slot],
            device_id=peer,
            device_id_type=pl.DeviceIdType.MESH,
        )

    def exchange(src_of, dst_of, send, recv, count, me, peer_of):
        for s in range(count):
            @pl.when(s != me)
            def _():
                copy(src_of(s), dst_of(me), send, recv, s, me, peer_of(s)).start()
        for s in range(count):
            @pl.when(s != me)
            def _():
                copy(src_of(s), dst_of(s), send, recv, s, s, peer_of(s)).wait_recv()

    def finish(src_of, dst_of, send, recv, count, me, peer_of):
        for s in range(count):
            @pl.when(s != me)
            def _():
                copy(src_of(s), dst_of(me), send, recv, s, me, peer_of(s)).wait_send()

    col_peer = lambda s: (me_r, s)
    row_peer = lambda s: (s, me_c)
    col_a = (lambda s: y_ref.at[s], lambda s: buf_a.at[s], sa, ra, cols, me_c, col_peer)
    exchange(*col_a)
    chunk = y_ref[me_c]
    for s in range(cols):
        chunk = chunk + buf_a[s]
    red_a[...] = chunk
    row_b = (lambda s: red_a.at[pl.ds(s, 1)], lambda s: buf_b.at[pl.ds(s, 1)], sb, rb, rows, me_r, row_peer)
    exchange(*row_b)
    piece = red_a[pl.ds(me_r, 1), :] + jnp.sum(buf_b[...], axis=0, keepdims=True)
    red_b[...] = piece
    row_g = (lambda s: red_b, lambda s: buf_g.at[pl.ds(s, 1)], sg, rg, rows, me_r, row_peer)
    exchange(*row_g)
    lines = lax.broadcasted_iota(jnp.int32, chunk.shape, 0)
    total = jnp.where(lines == me_r, jnp.broadcast_to(piece, chunk.shape), buf_g[...])
    red_c[...] = total
    col_c = (lambda s: red_c, lambda s: buf_c.at[s], sc, rc, cols, me_c, col_peer)
    exchange(*col_c)
    for s in range(cols):
        out_ref[s] = jnp.where(s == me_c, total, buf_c[s])
    finish(*col_a)
    finish(*row_b)
    finish(*row_g)
    finish(*col_c)


def all_reduce(matrix, rows, cols):
    pieces = matrix.reshape(cols, rows, -1)
    shape = pieces.shape
    vmem = pltpu.MemorySpace.VMEM
    total = pl.pallas_call(
        functools.partial(ar_kernel, rows, cols),
        out_shape=jax.ShapeDtypeStruct(shape, jnp.float32),
        in_specs=[pl.BlockSpec(memory_space=vmem)],
        out_specs=pl.BlockSpec(memory_space=vmem),
        scratch_shapes=[
            pltpu.VMEM(shape, jnp.float32),
            pltpu.VMEM(shape[1:], jnp.float32),
            pltpu.VMEM(shape[1:], jnp.float32),
            pltpu.VMEM(shape, jnp.float32),
            pltpu.VMEM(shape[1:], jnp.float32),
            pltpu.VMEM((1, shape[2]), jnp.float32),
            pltpu.VMEM(shape[1:], jnp.float32),
            pltpu.SemaphoreType.DMA((cols,)),
            pltpu.SemaphoreType.DMA((cols,)),
            pltpu.SemaphoreType.DMA((rows,)),
            pltpu.SemaphoreType.DMA((rows,)),
            pltpu.SemaphoreType.DMA((rows,)),
            pltpu.SemaphoreType.DMA((rows,)),
            pltpu.SemaphoreType.DMA((cols,)),
            pltpu.SemaphoreType.DMA((cols,)),
        ],
        compiler_params=pltpu.CompilerParams(collective_id=1, has_side_effects=True),
    )(pieces)
    return total.reshape(matrix.shape)

def local(coords, mode_shapes, output_shapes, response_gain):
    rows = lax.axis_size("row")
    cols = lax.axis_size("col")
    mode_count, block_nodes = mode_shapes.shape
    packed = pack_block(coords, mode_shapes)
    partial = row_exchange(packed, rows, cols, mode_count)
    total = all_reduce(partial, rows, cols)
    modal_csd = total + total.T
    real_part = response_gain[0]
    imag_part = response_gain[1]
    weighted = (
        real_part[:, None] * real_part[None, :] + imag_part[:, None] * imag_part[None, :]
    ) * modal_csd
    weighted_high, weighted_low = split_parts(weighted)
    mapped = jnp.dot(output_shapes, weighted_high, preferred_element_type=jnp.float32)
    mapped = mapped + jnp.dot(output_shapes, weighted_low, preferred_element_type=jnp.float32)
    response_power = jnp.sum(mapped * output_shapes.astype(jnp.float32), axis=1)
    return (response_power, modal_csd)


def solution(mesh):
    in_specs = (P(None, ("row", "col")), P(None, ("row", "col")), P(("row", "col"), None), P())
    out_specs = (P(("row", "col")), P())
    return jax.shard_map(local, mesh=mesh, in_specs=in_specs, out_specs=out_specs, check_vma=False)
```

```python
import functools
import math

import jax
import jax.numpy as jnp
from jax import lax
from jax.experimental import pallas as pl
from jax.experimental.pallas import tpu as pltpu
from jax.sharding import PartitionSpec as P

wave_scale = 0.35 / 64.0


def coherence(left_points, right_points):
    difference = left_points[:, :, None] - right_points[:, None, :]
    squared = jnp.sum(difference * difference, axis=0)
    return jnp.sinc(wave_scale * jnp.sqrt(squared)).astype(jnp.bfloat16)


def split_parts(matrix):
    high_part = matrix.astype(jnp.bfloat16)
    low_part = (matrix - high_part.astype(jnp.float32)).astype(jnp.bfloat16)
    return (high_part, low_part)


def pack_block(coords, mode_shapes):
    wide = coords.astype(jnp.float32)
    high = jnp.floor(wide * (1.0 / 256.0))
    low = wide - 256.0 * high
    pad = jnp.zeros((10, wide.shape[1]), jnp.float32)
    extra = jnp.concatenate([high, low, pad], axis=0).astype(jnp.bfloat16)
    return jnp.concatenate([mode_shapes, extra], axis=0)


def unpack_points(packed, mode_count):
    high = packed[..., mode_count:mode_count + 3, :].astype(jnp.float32)
    low = packed[..., mode_count + 3:mode_count + 6, :].astype(jnp.float32)
    return high * 256.0 + low


CHUNK = 32
SIN_TERMS = [math.pi * (-1) ** k * math.pi ** (2 * k) / math.factorial(2 * k + 1) for k in range(6)]


def coherence_chunk(dx, dy, dz):
    squared = dx * dx + dy * dy + dz * dz
    safe = jnp.maximum(squared, 1e-30)
    root_inv = lax.rsqrt(safe)
    x = safe * root_inv * wave_scale
    n = jnp.floor(x + 0.5)
    f = x - n
    h = n * 0.5
    sign = 1.0 - 4.0 * (h - jnp.floor(h))
    f2 = f * f
    q = SIN_TERMS[4]
    for term in SIN_TERMS[3::-1]:
        q = q * f2 + term
    scale = f * root_inv * (1.0 / (math.pi * wave_scale))
    return sign * q * scale


def block_points(slot_ref, mode_count):
    tail = slot_ref[mode_count:mode_count + 16, :].astype(jnp.float32)
    return [tail[k:k + 1, :] * 256.0 + tail[k + 3:k + 4, :] for k in range(3)]


def accumulate_block(slot_ref, weight, rowpts_ref, out_ref, tile_ref, mode_count):
    bx, by, bz = block_points(slot_ref, mode_count)
    length = tile_ref.shape[0]

    def chunk(c, carry):
        r0 = pl.multiple_of(c * CHUNK, CHUNK)
        dx = rowpts_ref[0, pl.ds(r0, CHUNK), :] - bx
        dy = rowpts_ref[1, pl.ds(r0, CHUNK), :] - by
        dz = rowpts_ref[2, pl.ds(r0, CHUNK), :] - bz
        tile_ref[pl.ds(r0, CHUNK), :] = coherence_chunk(dx, dy, dz).astype(jnp.bfloat16)
        return carry

    lax.fori_loop(0, length // CHUNK, chunk, 0, unroll=8)
    shapes = slot_ref[0:mode_count, :]
    product = lax.dot_general(
        tile_ref[...], shapes, (((1,), (1,)), ((), ())), preferred_element_type=jnp.float32
    )
    out_ref[...] += weight * product


def shift_of(j, rows):
    odd = j % 2
    return odd * j + (1 - odd) * (rows - j)


def row_kernel(rows, cols, mode_count, packed_ref, out_ref, recv, colbuf, rowpts_ref, tile_ref, acc_ref,
               send_sems, recv_sems, col_send, col_recv):
    me = lax.axis_index("row")
    col = lax.axis_index("col")
    half = rows // 2
    nodes = packed_ref.shape[1]
    colbuf[...] = jnp.zeros_like(colbuf)
    barrier = pltpu.get_barrier_semaphore()
    for p in range(1, rows):
        pl.semaphore_signal(
            barrier, 1, device_id=(lax.rem(me + p, rows), col), device_id_type=pl.DeviceIdType.MESH
        )
    for p in range(1, cols):
        pl.semaphore_signal(
            barrier, 1, device_id=(me, lax.rem(col + p, cols)), device_id_type=pl.DeviceIdType.MESH
        )
    pl.semaphore_wait(barrier, rows - 1 + cols - 1)

    def col_copy(s, slot):
        return pltpu.make_async_remote_copy(
            src_ref=packed_ref,
            dst_ref=colbuf.at[slot],
            send_sem=col_send.at[s],
            recv_sem=col_recv.at[slot],
            device_id=(me, s),
            device_id_type=pl.DeviceIdType.MESH,
        )

    def transfer(k):
        target = lax.rem(me + rows - shift_of(k + 1, rows), rows)
        return pltpu.make_async_remote_copy(
            src_ref=packed_ref,
            dst_ref=recv.at[k],
            send_sem=send_sems.at[k],
            recv_sem=recv_sems.at[k],
            device_id=(target, col),
            device_id_type=pl.DeviceIdType.MESH,
        )

    for s in range(cols):
        @pl.when(s != col)
        def _():
            col_copy(s, col).start()
    for k in range(half):
        transfer(k).start()
    for s in range(cols):
        @pl.when(s != col)
        def _():
            col_copy(s, s).wait_recv()

    eye = (lax.broadcasted_iota(jnp.int32, (nodes, nodes), 0)
           == lax.broadcasted_iota(jnp.int32, (nodes, nodes), 1)).astype(jnp.bfloat16)
    own_tail = packed_ref[mode_count:mode_count + 16, :]
    for s in range(cols):
        tail = jnp.where(s == col, own_tail, colbuf[s, mode_count:mode_count + 16, :])
        moved = lax.dot_general(eye, tail, (((1,), (1,)), ((), ())), preferred_element_type=jnp.float32)
        for k in range(3):
            column = moved[:, k:k + 1] * 256.0 + moved[:, k + 3:k + 4]
            rowpts_ref[k, s * nodes:(s + 1) * nodes, :] = jnp.broadcast_to(column, (nodes, nodes))

    acc_ref[...] = jnp.zeros_like(acc_ref)
    accumulate_block(packed_ref, 0.5, rowpts_ref, acc_ref, tile_ref, mode_count)

    def step(k, carry):
        transfer(k).wait_recv()
        weight = jnp.where(k == half - 1, 0.5, 1.0).astype(jnp.float32)
        accumulate_block(recv.at[k], weight, rowpts_ref, acc_ref, tile_ref, mode_count)
        return carry

    lax.fori_loop(0, half, step, 0)

    own_shapes = packed_ref[0:mode_count, :]
    partial = jnp.zeros(out_ref.shape, jnp.float32)
    for s in range(cols):
        shapes = jnp.where(s == col, own_shapes, colbuf[s, 0:mode_count, :])
        part = acc_ref[s * nodes:(s + 1) * nodes, :]
        high = part.astype(jnp.bfloat16)
        low = (part - high.astype(jnp.float32)).astype(jnp.bfloat16)
        partial = partial + jnp.dot(shapes, high, preferred_element_type=jnp.float32)
        partial = partial + jnp.dot(shapes, low, preferred_element_type=jnp.float32)
    out_ref[...] = partial

    for k in range(half):
        transfer(k).wait_send()
    for s in range(cols):
        @pl.when(s != col)
        def _():
            col_copy(s, col).wait_send()


def row_exchange(packed, rows, cols, mode_count):
    nodes = packed.shape[1]
    length = cols * nodes
    half = rows // 2
    vmem = pltpu.MemorySpace.VMEM
    flops = 2 * (half + 1) * length * nodes * mode_count + 4 * length * mode_count * mode_count
    return pl.pallas_call(
        functools.partial(row_kernel, rows, cols, mode_count),
        out_shape=jax.ShapeDtypeStruct((mode_count, mode_count), jnp.float32),
        in_specs=[pl.BlockSpec(memory_space=vmem)],
        out_specs=pl.BlockSpec(memory_space=vmem),
        scratch_shapes=[
            pltpu.VMEM((half,) + packed.shape, packed.dtype),
            pltpu.VMEM((cols,) + packed.shape, packed.dtype),
            pltpu.VMEM((3, length, nodes), jnp.float32),
            pltpu.VMEM((length, nodes), jnp.bfloat16),
            pltpu.VMEM((length, mode_count), jnp.float32),
            pltpu.SemaphoreType.DMA((half,)),
            pltpu.SemaphoreType.DMA((half,)),
            pltpu.SemaphoreType.DMA((cols,)),
            pltpu.SemaphoreType.DMA((cols,)),
        ],
        compiler_params=pltpu.CompilerParams(
            collective_id=0, has_side_effects=True, vmem_limit_bytes=48 * 1024 * 1024
        ),
        cost_estimate=pl.CostEstimate(
            flops=flops, transcendentals=(half + 1) * length * nodes, bytes_accessed=4 * 1024 * 1024
        ),
    )(packed)

def gather_all(block, axis, count):
    spread = jnp.broadcast_to(block[None], (count,) + block.shape)
    return lax.all_to_all(spread, axis, 0, 0, tiled=True)


def ar_kernel(rows, cols, y_ref, out_ref, buf_a, buf_b, buf_g, buf_c, red_a, red_b, red_c,
              sa, ra, sb, rb, sg, rg, sc, rc):
    me_r = lax.axis_index("row")
    me_c = lax.axis_index("col")
    buf_a[...] = jnp.zeros_like(buf_a)
    buf_b[...] = jnp.zeros_like(buf_b)
    buf_g[...] = jnp.zeros_like(buf_g)
    buf_c[...] = jnp.zeros_like(buf_c)
    barrier = pltpu.get_barrier_semaphore()
    for p in range(1, cols):
        pl.semaphore_signal(
            barrier, 1, device_id=(me_r, lax.rem(me_c + p, cols)), device_id_type=pl.DeviceIdType.MESH
        )
    for p in range(1, rows):
        pl.semaphore_signal(
            barrier, 1, device_id=(lax.rem(me_r + p, rows), me_c), device_id_type=pl.DeviceIdType.MESH
        )
    pl.semaphore_wait(barrier, cols - 1 + rows - 1)

    def copy(src, dst, send, recv, sem_index, slot, peer):
        return pltpu.make_async_remote_copy(
            src_ref=src,
            dst_ref=dst,
            send_sem=send.at[sem_index],
            recv_sem=recv.at[slot],
            device_id=peer,
            device_id_type=pl.DeviceIdType.MESH,
        )

    def exchange(src_of, dst_of, send, recv, count, me, peer_of):
        for s in range(count):
            @pl.when(s != me)
            def _():
                copy(src_of(s), dst_of(me), send, recv, s, me, peer_of(s)).start()
        for s in range(count):
            @pl.when(s != me)
            def _():
                copy(src_of(s), dst_of(s), send, recv, s, s, peer_of(s)).wait_recv()

    def finish(src_of, dst_of, send, recv, count, me, peer_of):
        for s in range(count):
            @pl.when(s != me)
            def _():
                copy(src_of(s), dst_of(me), send, recv, s, me, peer_of(s)).wait_send()

    col_peer = lambda s: (me_r, s)
    row_peer = lambda s: (s, me_c)
    col_a = (lambda s: y_ref.at[s], lambda s: buf_a.at[s], sa, ra, cols, me_c, col_peer)
    exchange(*col_a)
    chunk = y_ref[me_c]
    for s in range(cols):
        chunk = chunk + buf_a[s]
    red_a[...] = chunk
    row_b = (lambda s: red_a.at[pl.ds(s, 1)], lambda s: buf_b.at[pl.ds(s, 1)], sb, rb, rows, me_r, row_peer)
    exchange(*row_b)
    piece = red_a[pl.ds(me_r, 1), :] + jnp.sum(buf_b[...], axis=0, keepdims=True)
    red_b[...] = piece
    row_g = (lambda s: red_b, lambda s: buf_g.at[pl.ds(s, 1)], sg, rg, rows, me_r, row_peer)
    exchange(*row_g)
    lines = lax.broadcasted_iota(jnp.int32, chunk.shape, 0)
    total = jnp.where(lines == me_r, jnp.broadcast_to(piece, chunk.shape), buf_g[...])
    red_c[...] = total
    col_c = (lambda s: red_c, lambda s: buf_c.at[s], sc, rc, cols, me_c, col_peer)
    exchange(*col_c)
    for s in range(cols):
        out_ref[s] = jnp.where(s == me_c, total, buf_c[s])
    finish(*col_a)
    finish(*row_b)
    finish(*row_g)
    finish(*col_c)


def all_reduce(matrix, rows, cols):
    pieces = matrix.reshape(cols, rows, -1)
    shape = pieces.shape
    vmem = pltpu.MemorySpace.VMEM
    total = pl.pallas_call(
        functools.partial(ar_kernel, rows, cols),
        out_shape=jax.ShapeDtypeStruct(shape, jnp.float32),
        in_specs=[pl.BlockSpec(memory_space=vmem)],
        out_specs=pl.BlockSpec(memory_space=vmem),
        scratch_shapes=[
            pltpu.VMEM(shape, jnp.float32),
            pltpu.VMEM(shape[1:], jnp.float32),
            pltpu.VMEM(shape[1:], jnp.float32),
            pltpu.VMEM(shape, jnp.float32),
            pltpu.VMEM(shape[1:], jnp.float32),
            pltpu.VMEM((1, shape[2]), jnp.float32),
            pltpu.VMEM(shape[1:], jnp.float32),
            pltpu.SemaphoreType.DMA((cols,)),
            pltpu.SemaphoreType.DMA((cols,)),
            pltpu.SemaphoreType.DMA((rows,)),
            pltpu.SemaphoreType.DMA((rows,)),
            pltpu.SemaphoreType.DMA((rows,)),
            pltpu.SemaphoreType.DMA((rows,)),
            pltpu.SemaphoreType.DMA((cols,)),
            pltpu.SemaphoreType.DMA((cols,)),
        ],
        compiler_params=pltpu.CompilerParams(collective_id=1, has_side_effects=True),
    )(pieces)
    return total.reshape(matrix.shape)

def local(coords, mode_shapes, output_shapes, response_gain):
    rows = lax.axis_size("row")
    cols = lax.axis_size("col")
    mode_count, block_nodes = mode_shapes.shape
    packed = pack_block(coords, mode_shapes)
    partial = row_exchange(packed, rows, cols, mode_count)
    total = all_reduce(partial, rows, cols)
    modal_csd = total + total.T
    real_part = response_gain[0]
    imag_part = response_gain[1]
    weighted = (
        real_part[:, None] * real_part[None, :] + imag_part[:, None] * imag_part[None, :]
    ) * modal_csd
    weighted_high, weighted_low = split_parts(weighted)
    mapped = jnp.dot(output_shapes, weighted_high, preferred_element_type=jnp.float32)
    mapped = mapped + jnp.dot(output_shapes, weighted_low, preferred_element_type=jnp.float32)
    response_power = jnp.sum(mapped * output_shapes.astype(jnp.float32), axis=1)
    return (response_power, modal_csd)


def solution(mesh):
    in_specs = (P(None, ("row", "col")), P(None, ("row", "col")), P(("row", "col"), None), P())
    out_specs = (P(("row", "col")), P())
    return jax.shard_map(local, mesh=mesh, in_specs=in_specs, out_specs=out_specs, check_vma=False)
```

```python
import functools
import math

import jax
import jax.numpy as jnp
from jax import lax
from jax.experimental import pallas as pl
from jax.experimental.pallas import tpu as pltpu
from jax.sharding import PartitionSpec as P

wave_scale = 0.35 / 64.0


def coherence(left_points, right_points):
    difference = left_points[:, :, None] - right_points[:, None, :]
    squared = jnp.sum(difference * difference, axis=0)
    return jnp.sinc(wave_scale * jnp.sqrt(squared)).astype(jnp.bfloat16)


def split_parts(matrix):
    high_part = matrix.astype(jnp.bfloat16)
    low_part = (matrix - high_part.astype(jnp.float32)).astype(jnp.bfloat16)
    return (high_part, low_part)


def pack_block(coords, mode_shapes):
    wide = coords.astype(jnp.float32)
    high = jnp.floor(wide * (1.0 / 256.0))
    low = wide - 256.0 * high
    pad = jnp.zeros((10, wide.shape[1]), jnp.float32)
    extra = jnp.concatenate([high, low, pad], axis=0).astype(jnp.bfloat16)
    return jnp.concatenate([mode_shapes, extra], axis=0)


def unpack_points(packed, mode_count):
    high = packed[..., mode_count:mode_count + 3, :].astype(jnp.float32)
    low = packed[..., mode_count + 3:mode_count + 6, :].astype(jnp.float32)
    return high * 256.0 + low


CHUNK = 32
SIN_TERMS = [(-1) ** k * math.pi ** (2 * k) / math.factorial(2 * k + 1) / wave_scale for k in range(6)]


def coherence_chunk(dx, dy, dz):
    squared = dx * dx + dy * dy + dz * dz
    safe = jnp.maximum(squared, 1e-30)
    root_inv = lax.rsqrt(safe)
    x = safe * root_inv * wave_scale
    n = jnp.floor(x + 0.5)
    f = x - n
    h = n * 0.5
    sign = 1.0 - 4.0 * (h - jnp.floor(h))
    f2 = f * f
    q = SIN_TERMS[4]
    for term in SIN_TERMS[3::-1]:
        q = q * f2 + term
    return (sign * f) * (q * root_inv)


def block_points(slot_ref, mode_count):
    tail = slot_ref[mode_count:mode_count + 16, :].astype(jnp.float32)
    return [tail[k:k + 1, :] * 256.0 + tail[k + 3:k + 4, :] for k in range(3)]


def accumulate_block(slot_ref, weight, rowpts_ref, out_ref, tile_ref, mode_count):
    bx, by, bz = block_points(slot_ref, mode_count)
    length = tile_ref.shape[0]

    def chunk(c, carry):
        r0 = pl.multiple_of(c * CHUNK, CHUNK)
        dx = rowpts_ref[0, pl.ds(r0, CHUNK), :] - bx
        dy = rowpts_ref[1, pl.ds(r0, CHUNK), :] - by
        dz = rowpts_ref[2, pl.ds(r0, CHUNK), :] - bz
        tile_ref[pl.ds(r0, CHUNK), :] = coherence_chunk(dx, dy, dz).astype(jnp.bfloat16)
        return carry

    lax.fori_loop(0, length // CHUNK, chunk, 0, unroll=8)
    shapes = slot_ref[0:mode_count, :] * weight.astype(jnp.bfloat16)
    product = lax.dot_general(
        tile_ref[...], shapes, (((1,), (1,)), ((), ())), preferred_element_type=jnp.float32
    )
    out_ref[...] += product


def shift_of(j, rows):
    odd = j % 2
    return odd * j + (1 - odd) * (rows - j)


def row_kernel(rows, cols, mode_count, packed_ref, out_ref, recv, colbuf, rowpts_ref, tile_ref, acc_ref,
               send_sems, recv_sems, col_send, col_recv):
    me = lax.axis_index("row")
    col = lax.axis_index("col")
    half = rows // 2
    nodes = packed_ref.shape[1]
    colbuf[...] = jnp.zeros_like(colbuf)
    barrier = pltpu.get_barrier_semaphore()
    for p in range(1, rows):
        pl.semaphore_signal(
            barrier, 1, device_id=(lax.rem(me + p, rows), col), device_id_type=pl.DeviceIdType.MESH
        )
    for p in range(1, cols):
        pl.semaphore_signal(
            barrier, 1, device_id=(me, lax.rem(col + p, cols)), device_id_type=pl.DeviceIdType.MESH
        )
    pl.semaphore_wait(barrier, rows - 1 + cols - 1)

    def col_copy(s, slot):
        return pltpu.make_async_remote_copy(
            src_ref=packed_ref,
            dst_ref=colbuf.at[slot],
            send_sem=col_send.at[s],
            recv_sem=col_recv.at[slot],
            device_id=(me, s),
            device_id_type=pl.DeviceIdType.MESH,
        )

    def transfer(k):
        target = lax.rem(me + rows - shift_of(k + 1, rows), rows)
        return pltpu.make_async_remote_copy(
            src_ref=packed_ref,
            dst_ref=recv.at[k],
            send_sem=send_sems.at[k],
            recv_sem=recv_sems.at[k],
            device_id=(target, col),
            device_id_type=pl.DeviceIdType.MESH,
        )

    for s in range(cols):
        @pl.when(s != col)
        def _():
            col_copy(s, col).start()
    for k in range(half):
        transfer(k).start()
    for s in range(cols):
        @pl.when(s != col)
        def _():
            col_copy(s, s).wait_recv()

    eye = (lax.broadcasted_iota(jnp.int32, (nodes, nodes), 0)
           == lax.broadcasted_iota(jnp.int32, (nodes, nodes), 1)).astype(jnp.bfloat16)
    own_tail = packed_ref[mode_count:mode_count + 16, :]
    for s in range(cols):
        tail = jnp.where(s == col, own_tail, colbuf[s, mode_count:mode_count + 16, :])
        moved = lax.dot_general(eye, tail, (((1,), (1,)), ((), ())), preferred_element_type=jnp.float32)
        for k in range(3):
            column = moved[:, k:k + 1] * 256.0 + moved[:, k + 3:k + 4]
            rowpts_ref[k, s * nodes:(s + 1) * nodes, :] = jnp.broadcast_to(column, (nodes, nodes))

    acc_ref[...] = jnp.zeros_like(acc_ref)
    accumulate_block(packed_ref, jnp.float32(0.5), rowpts_ref, acc_ref, tile_ref, mode_count)

    def step(k, carry):
        transfer(k).wait_recv()
        weight = jnp.where(k == half - 1, 0.5, 1.0).astype(jnp.float32)
        accumulate_block(recv.at[k], weight, rowpts_ref, acc_ref, tile_ref, mode_count)
        return carry

    lax.fori_loop(0, half, step, 0)

    own_shapes = packed_ref[0:mode_count, :]
    partial = jnp.zeros(out_ref.shape, jnp.float32)
    for s in range(cols):
        shapes = jnp.where(s == col, own_shapes, colbuf[s, 0:mode_count, :])
        part = acc_ref[s * nodes:(s + 1) * nodes, :]
        high = part.astype(jnp.bfloat16)
        low = (part - high.astype(jnp.float32)).astype(jnp.bfloat16)
        partial = partial + jnp.dot(shapes, high, preferred_element_type=jnp.float32)
        partial = partial + jnp.dot(shapes, low, preferred_element_type=jnp.float32)
    out_ref[...] = partial

    for k in range(half):
        transfer(k).wait_send()
    for s in range(cols):
        @pl.when(s != col)
        def _():
            col_copy(s, col).wait_send()


def row_exchange(packed, rows, cols, mode_count):
    nodes = packed.shape[1]
    length = cols * nodes
    half = rows // 2
    vmem = pltpu.MemorySpace.VMEM
    flops = 2 * (half + 1) * length * nodes * mode_count + 4 * length * mode_count * mode_count
    return pl.pallas_call(
        functools.partial(row_kernel, rows, cols, mode_count),
        out_shape=jax.ShapeDtypeStruct((mode_count, mode_count), jnp.float32),
        in_specs=[pl.BlockSpec(memory_space=vmem)],
        out_specs=pl.BlockSpec(memory_space=vmem),
        scratch_shapes=[
            pltpu.VMEM((half,) + packed.shape, packed.dtype),
            pltpu.VMEM((cols,) + packed.shape, packed.dtype),
            pltpu.VMEM((3, length, nodes), jnp.float32),
            pltpu.VMEM((length, nodes), jnp.bfloat16),
            pltpu.VMEM((length, mode_count), jnp.float32),
            pltpu.SemaphoreType.DMA((half,)),
            pltpu.SemaphoreType.DMA((half,)),
            pltpu.SemaphoreType.DMA((cols,)),
            pltpu.SemaphoreType.DMA((cols,)),
        ],
        compiler_params=pltpu.CompilerParams(
            collective_id=0, has_side_effects=True, vmem_limit_bytes=48 * 1024 * 1024
        ),
        cost_estimate=pl.CostEstimate(
            flops=flops, transcendentals=(half + 1) * length * nodes, bytes_accessed=4 * 1024 * 1024
        ),
    )(packed)

def gather_all(block, axis, count):
    spread = jnp.broadcast_to(block[None], (count,) + block.shape)
    return lax.all_to_all(spread, axis, 0, 0, tiled=True)


def ar_kernel(rows, cols, y_ref, out_ref, buf_a, buf_b, buf_g, buf_c, red_a, red_b, red_c,
              sa, ra, sb, rb, sg, rg, sc, rc):
    me_r = lax.axis_index("row")
    me_c = lax.axis_index("col")
    buf_a[...] = jnp.zeros_like(buf_a)
    buf_b[...] = jnp.zeros_like(buf_b)
    buf_g[...] = jnp.zeros_like(buf_g)
    buf_c[...] = jnp.zeros_like(buf_c)
    barrier = pltpu.get_barrier_semaphore()
    for p in range(1, cols):
        pl.semaphore_signal(
            barrier, 1, device_id=(me_r, lax.rem(me_c + p, cols)), device_id_type=pl.DeviceIdType.MESH
        )
    for p in range(1, rows):
        pl.semaphore_signal(
            barrier, 1, device_id=(lax.rem(me_r + p, rows), me_c), device_id_type=pl.DeviceIdType.MESH
        )
    pl.semaphore_wait(barrier, cols - 1 + rows - 1)

    def copy(src, dst, send, recv, sem_index, slot, peer):
        return pltpu.make_async_remote_copy(
            src_ref=src,
            dst_ref=dst,
            send_sem=send.at[sem_index],
            recv_sem=recv.at[slot],
            device_id=peer,
            device_id_type=pl.DeviceIdType.MESH,
        )

    def exchange(src_of, dst_of, send, recv, count, me, peer_of):
        for s in range(count):
            @pl.when(s != me)
            def _():
                copy(src_of(s), dst_of(me), send, recv, s, me, peer_of(s)).start()
        for s in range(count):
            @pl.when(s != me)
            def _():
                copy(src_of(s), dst_of(s), send, recv, s, s, peer_of(s)).wait_recv()

    def finish(src_of, dst_of, send, recv, count, me, peer_of):
        for s in range(count):
            @pl.when(s != me)
            def _():
                copy(src_of(s), dst_of(me), send, recv, s, me, peer_of(s)).wait_send()

    col_peer = lambda s: (me_r, s)
    row_peer = lambda s: (s, me_c)
    col_a = (lambda s: y_ref.at[s], lambda s: buf_a.at[s], sa, ra, cols, me_c, col_peer)
    exchange(*col_a)
    chunk = y_ref[me_c]
    for s in range(cols):
        chunk = chunk + buf_a[s]
    red_a[...] = chunk
    row_b = (lambda s: red_a.at[pl.ds(s, 1)], lambda s: buf_b.at[pl.ds(s, 1)], sb, rb, rows, me_r, row_peer)
    exchange(*row_b)
    piece = red_a[pl.ds(me_r, 1), :] + jnp.sum(buf_b[...], axis=0, keepdims=True)
    red_b[...] = piece
    row_g = (lambda s: red_b, lambda s: buf_g.at[pl.ds(s, 1)], sg, rg, rows, me_r, row_peer)
    exchange(*row_g)
    lines = lax.broadcasted_iota(jnp.int32, chunk.shape, 0)
    total = jnp.where(lines == me_r, jnp.broadcast_to(piece, chunk.shape), buf_g[...])
    red_c[...] = total
    col_c = (lambda s: red_c, lambda s: buf_c.at[s], sc, rc, cols, me_c, col_peer)
    exchange(*col_c)
    for s in range(cols):
        out_ref[s] = jnp.where(s == me_c, total, buf_c[s])
    finish(*col_a)
    finish(*row_b)
    finish(*row_g)
    finish(*col_c)


def all_reduce(matrix, rows, cols):
    pieces = matrix.reshape(cols, rows, -1)
    shape = pieces.shape
    vmem = pltpu.MemorySpace.VMEM
    total = pl.pallas_call(
        functools.partial(ar_kernel, rows, cols),
        out_shape=jax.ShapeDtypeStruct(shape, jnp.float32),
        in_specs=[pl.BlockSpec(memory_space=vmem)],
        out_specs=pl.BlockSpec(memory_space=vmem),
        scratch_shapes=[
            pltpu.VMEM(shape, jnp.float32),
            pltpu.VMEM(shape[1:], jnp.float32),
            pltpu.VMEM(shape[1:], jnp.float32),
            pltpu.VMEM(shape, jnp.float32),
            pltpu.VMEM(shape[1:], jnp.float32),
            pltpu.VMEM((1, shape[2]), jnp.float32),
            pltpu.VMEM(shape[1:], jnp.float32),
            pltpu.SemaphoreType.DMA((cols,)),
            pltpu.SemaphoreType.DMA((cols,)),
            pltpu.SemaphoreType.DMA((rows,)),
            pltpu.SemaphoreType.DMA((rows,)),
            pltpu.SemaphoreType.DMA((rows,)),
            pltpu.SemaphoreType.DMA((rows,)),
            pltpu.SemaphoreType.DMA((cols,)),
            pltpu.SemaphoreType.DMA((cols,)),
        ],
        compiler_params=pltpu.CompilerParams(collective_id=1, has_side_effects=True),
    )(pieces)
    return total.reshape(matrix.shape)

def local(coords, mode_shapes, output_shapes, response_gain):
    rows = lax.axis_size("row")
    cols = lax.axis_size("col")
    mode_count, block_nodes = mode_shapes.shape
    packed = pack_block(coords, mode_shapes)
    partial = row_exchange(packed, rows, cols, mode_count)
    total = all_reduce(partial, rows, cols)
    modal_csd = total + total.T
    real_part = response_gain[0]
    imag_part = response_gain[1]
    weighted = (
        real_part[:, None] * real_part[None, :] + imag_part[:, None] * imag_part[None, :]
    ) * modal_csd
    weighted_high, weighted_low = split_parts(weighted)
    mapped = jnp.dot(output_shapes, weighted_high, preferred_element_type=jnp.float32)
    mapped = mapped + jnp.dot(output_shapes, weighted_low, preferred_element_type=jnp.float32)
    response_power = jnp.sum(mapped * output_shapes.astype(jnp.float32), axis=1)
    return (response_power, modal_csd)


def solution(mesh):
    in_specs = (P(None, ("row", "col")), P(None, ("row", "col")), P(("row", "col"), None), P())
    out_specs = (P(("row", "col")), P())
    return jax.shard_map(local, mesh=mesh, in_specs=in_specs, out_specs=out_specs, check_vma=False)
```

```python
import functools
import math

import jax
import jax.numpy as jnp
from jax import lax
from jax.experimental import pallas as pl
from jax.experimental.pallas import tpu as pltpu
from jax.sharding import PartitionSpec as P

wave_scale = 0.35 / 64.0


def coherence(left_points, right_points):
    difference = left_points[:, :, None] - right_points[:, None, :]
    squared = jnp.sum(difference * difference, axis=0)
    return jnp.sinc(wave_scale * jnp.sqrt(squared)).astype(jnp.bfloat16)


def split_parts(matrix):
    high_part = matrix.astype(jnp.bfloat16)
    low_part = (matrix - high_part.astype(jnp.float32)).astype(jnp.bfloat16)
    return (high_part, low_part)


def pack_block(coords, mode_shapes):
    wide = coords.astype(jnp.float32)
    high = jnp.floor(wide * (1.0 / 256.0))
    low = wide - 256.0 * high
    pad = jnp.zeros((10, wide.shape[1]), jnp.float32)
    extra = jnp.concatenate([high, low, pad], axis=0).astype(jnp.bfloat16)
    return jnp.concatenate([mode_shapes, extra], axis=0)


def unpack_points(packed, mode_count):
    high = packed[..., mode_count:mode_count + 3, :].astype(jnp.float32)
    low = packed[..., mode_count + 3:mode_count + 6, :].astype(jnp.float32)
    return high * 256.0 + low


CHUNK = 32
SIN_TERMS = [(-1) ** k * math.pi ** (2 * k) / math.factorial(2 * k + 1) / wave_scale for k in range(6)]


def coherence_chunk(dx, dy, dz):
    squared = dx * dx + dy * dy + dz * dz
    safe = jnp.maximum(squared, 1e-30)
    root_inv = lax.rsqrt(safe)
    x = safe * root_inv * wave_scale
    n = jnp.floor(x + 0.5)
    f = x - n
    h = n * 0.5
    sign = 1.0 - 4.0 * (h - jnp.floor(h))
    f2 = f * f
    q = SIN_TERMS[4]
    for term in SIN_TERMS[3::-1]:
        q = q * f2 + term
    return (sign * f) * (q * root_inv)


def block_points(slot_ref, mode_count):
    tail = slot_ref[mode_count:mode_count + 16, :].astype(jnp.float32)
    return [tail[k:k + 1, :] * 256.0 + tail[k + 3:k + 4, :] for k in range(3)]


def accumulate_block(slot_ref, weight, rowpts_ref, out_ref, tile_ref, mode_count):
    bx, by, bz = block_points(slot_ref, mode_count)
    length = tile_ref.shape[0]

    def chunk(c, carry):
        r0 = pl.multiple_of(c * CHUNK, CHUNK)
        dx = rowpts_ref[0, pl.ds(r0, CHUNK), :] - bx
        dy = rowpts_ref[1, pl.ds(r0, CHUNK), :] - by
        dz = rowpts_ref[2, pl.ds(r0, CHUNK), :] - bz
        tile_ref[pl.ds(r0, CHUNK), :] = coherence_chunk(dx, dy, dz).astype(jnp.bfloat16)
        return carry

    lax.fori_loop(0, length // CHUNK, chunk, 0, unroll=8)
    shapes = slot_ref[0:mode_count, :] * weight.astype(jnp.bfloat16)
    product = lax.dot_general(
        tile_ref[...], shapes, (((1,), (1,)), ((), ())), preferred_element_type=jnp.float32
    )
    out_ref[...] += product


def shift_of(j, rows):
    odd = j % 2
    return odd * j + (1 - odd) * (rows - j)


def row_kernel(rows, cols, mode_count, packed_ref, out_ref, recv, colbuf, rowpts_ref, tile_ref, acc_ref,
               send_sems, recv_sems, col_send, col_recv):
    me = lax.axis_index("row")
    col = lax.axis_index("col")
    half = rows // 2
    nodes = packed_ref.shape[1]
    colbuf[...] = jnp.zeros_like(colbuf)
    barrier = pltpu.get_barrier_semaphore()
    for p in range(1, rows):
        pl.semaphore_signal(
            barrier, 1, device_id=(lax.rem(me + p, rows), col), device_id_type=pl.DeviceIdType.MESH
        )
    for p in range(1, cols):
        pl.semaphore_signal(
            barrier, 1, device_id=(me, lax.rem(col + p, cols)), device_id_type=pl.DeviceIdType.MESH
        )
    pl.semaphore_wait(barrier, rows - 1 + cols - 1)

    def col_copy(s, slot):
        return pltpu.make_async_remote_copy(
            src_ref=packed_ref,
            dst_ref=colbuf.at[slot],
            send_sem=col_send.at[s],
            recv_sem=col_recv.at[slot],
            device_id=(me, s),
            device_id_type=pl.DeviceIdType.MESH,
        )

    def transfer(k):
        target = lax.rem(me + rows - shift_of(k + 1, rows), rows)
        return pltpu.make_async_remote_copy(
            src_ref=packed_ref,
            dst_ref=recv.at[k],
            send_sem=send_sems.at[k],
            recv_sem=recv_sems.at[k],
            device_id=(target, col),
            device_id_type=pl.DeviceIdType.MESH,
        )

    for k in range(half):
        transfer(k).start()
    for s in range(cols):
        @pl.when(s != col)
        def _():
            col_copy(s, col).start()
    for s in range(cols):
        @pl.when(s != col)
        def _():
            col_copy(s, s).wait_recv()

    eye = (lax.broadcasted_iota(jnp.int32, (nodes, nodes), 0)
           == lax.broadcasted_iota(jnp.int32, (nodes, nodes), 1)).astype(jnp.bfloat16)
    own_tail = packed_ref[mode_count:mode_count + 16, :]
    for s in range(cols):
        tail = jnp.where(s == col, own_tail, colbuf[s, mode_count:mode_count + 16, :])
        moved = lax.dot_general(eye, tail, (((1,), (1,)), ((), ())), preferred_element_type=jnp.float32)
        for k in range(3):
            column = moved[:, k:k + 1] * 256.0 + moved[:, k + 3:k + 4]
            rowpts_ref[k, s * nodes:(s + 1) * nodes, :] = jnp.broadcast_to(column, (nodes, nodes))

    acc_ref[...] = jnp.zeros_like(acc_ref)
    accumulate_block(packed_ref, jnp.float32(0.5), rowpts_ref, acc_ref, tile_ref, mode_count)

    def step(k, carry):
        transfer(k).wait_recv()
        weight = jnp.where(k == half - 1, 0.5, 1.0).astype(jnp.float32)
        accumulate_block(recv.at[k], weight, rowpts_ref, acc_ref, tile_ref, mode_count)
        return carry

    lax.fori_loop(0, half, step, 0)

    own_shapes = packed_ref[0:mode_count, :]
    partial = jnp.zeros(out_ref.shape, jnp.float32)
    for s in range(cols):
        shapes = jnp.where(s == col, own_shapes, colbuf[s, 0:mode_count, :])
        part = acc_ref[s * nodes:(s + 1) * nodes, :]
        high = part.astype(jnp.bfloat16)
        low = (part - high.astype(jnp.float32)).astype(jnp.bfloat16)
        partial = partial + jnp.dot(shapes, high, preferred_element_type=jnp.float32)
        partial = partial + jnp.dot(shapes, low, preferred_element_type=jnp.float32)
    out_ref[...] = partial

    for k in range(half):
        transfer(k).wait_send()
    for s in range(cols):
        @pl.when(s != col)
        def _():
            col_copy(s, col).wait_send()


def row_exchange(packed, rows, cols, mode_count):
    nodes = packed.shape[1]
    length = cols * nodes
    half = rows // 2
    vmem = pltpu.MemorySpace.VMEM
    flops = 2 * (half + 1) * length * nodes * mode_count + 4 * length * mode_count * mode_count
    return pl.pallas_call(
        functools.partial(row_kernel, rows, cols, mode_count),
        out_shape=jax.ShapeDtypeStruct((mode_count, mode_count), jnp.float32),
        in_specs=[pl.BlockSpec(memory_space=vmem)],
        out_specs=pl.BlockSpec(memory_space=vmem),
        scratch_shapes=[
            pltpu.VMEM((half,) + packed.shape, packed.dtype),
            pltpu.VMEM((cols,) + packed.shape, packed.dtype),
            pltpu.VMEM((3, length, nodes), jnp.float32),
            pltpu.VMEM((length, nodes), jnp.bfloat16),
            pltpu.VMEM((length, mode_count), jnp.float32),
            pltpu.SemaphoreType.DMA((half,)),
            pltpu.SemaphoreType.DMA((half,)),
            pltpu.SemaphoreType.DMA((cols,)),
            pltpu.SemaphoreType.DMA((cols,)),
        ],
        compiler_params=pltpu.CompilerParams(
            collective_id=0, has_side_effects=True, vmem_limit_bytes=48 * 1024 * 1024
        ),
        cost_estimate=pl.CostEstimate(
            flops=flops, transcendentals=(half + 1) * length * nodes, bytes_accessed=4 * 1024 * 1024
        ),
    )(packed)

def gather_all(block, axis, count):
    spread = jnp.broadcast_to(block[None], (count,) + block.shape)
    return lax.all_to_all(spread, axis, 0, 0, tiled=True)


def ar_kernel(rows, cols, y_ref, out_ref, buf_a, buf_b, buf_g, buf_c, red_a, red_b, red_c,
              sa, ra, sb, rb, sg, rg, sc, rc):
    me_r = lax.axis_index("row")
    me_c = lax.axis_index("col")
    buf_a[...] = jnp.zeros_like(buf_a)
    buf_b[...] = jnp.zeros_like(buf_b)
    buf_g[...] = jnp.zeros_like(buf_g)
    buf_c[...] = jnp.zeros_like(buf_c)
    barrier = pltpu.get_barrier_semaphore()
    for p in range(1, cols):
        pl.semaphore_signal(
            barrier, 1, device_id=(me_r, lax.rem(me_c + p, cols)), device_id_type=pl.DeviceIdType.MESH
        )
    for p in range(1, rows):
        pl.semaphore_signal(
            barrier, 1, device_id=(lax.rem(me_r + p, rows), me_c), device_id_type=pl.DeviceIdType.MESH
        )
    pl.semaphore_wait(barrier, cols - 1 + rows - 1)

    def copy(src, dst, send, recv, sem_index, slot, peer):
        return pltpu.make_async_remote_copy(
            src_ref=src,
            dst_ref=dst,
            send_sem=send.at[sem_index],
            recv_sem=recv.at[slot],
            device_id=peer,
            device_id_type=pl.DeviceIdType.MESH,
        )

    def exchange(src_of, dst_of, send, recv, count, me, peer_of):
        for s in range(count):
            @pl.when(s != me)
            def _():
                copy(src_of(s), dst_of(me), send, recv, s, me, peer_of(s)).start()
        for s in range(count):
            @pl.when(s != me)
            def _():
                copy(src_of(s), dst_of(s), send, recv, s, s, peer_of(s)).wait_recv()

    def finish(src_of, dst_of, send, recv, count, me, peer_of):
        for s in range(count):
            @pl.when(s != me)
            def _():
                copy(src_of(s), dst_of(me), send, recv, s, me, peer_of(s)).wait_send()

    col_peer = lambda s: (me_r, s)
    row_peer = lambda s: (s, me_c)
    col_a = (lambda s: y_ref.at[s], lambda s: buf_a.at[s], sa, ra, cols, me_c, col_peer)
    exchange(*col_a)
    chunk = y_ref[me_c]
    for s in range(cols):
        chunk = chunk + buf_a[s]
    red_a[...] = chunk
    row_b = (lambda s: red_a.at[pl.ds(s, 1)], lambda s: buf_b.at[pl.ds(s, 1)], sb, rb, rows, me_r, row_peer)
    exchange(*row_b)
    piece = red_a[pl.ds(me_r, 1), :] + jnp.sum(buf_b[...], axis=0, keepdims=True)
    red_b[...] = piece
    row_g = (lambda s: red_b, lambda s: buf_g.at[pl.ds(s, 1)], sg, rg, rows, me_r, row_peer)
    exchange(*row_g)
    lines = lax.broadcasted_iota(jnp.int32, chunk.shape, 0)
    total = jnp.where(lines == me_r, jnp.broadcast_to(piece, chunk.shape), buf_g[...])
    red_c[...] = total
    col_c = (lambda s: red_c, lambda s: buf_c.at[s], sc, rc, cols, me_c, col_peer)
    exchange(*col_c)
    for s in range(cols):
        out_ref[s] = jnp.where(s == me_c, total, buf_c[s])
    finish(*col_a)
    finish(*row_b)
    finish(*row_g)
    finish(*col_c)


def all_reduce(matrix, rows, cols):
    pieces = matrix.reshape(cols, rows, -1)
    shape = pieces.shape
    vmem = pltpu.MemorySpace.VMEM
    total = pl.pallas_call(
        functools.partial(ar_kernel, rows, cols),
        out_shape=jax.ShapeDtypeStruct(shape, jnp.float32),
        in_specs=[pl.BlockSpec(memory_space=vmem)],
        out_specs=pl.BlockSpec(memory_space=vmem),
        scratch_shapes=[
            pltpu.VMEM(shape, jnp.float32),
            pltpu.VMEM(shape[1:], jnp.float32),
            pltpu.VMEM(shape[1:], jnp.float32),
            pltpu.VMEM(shape, jnp.float32),
            pltpu.VMEM(shape[1:], jnp.float32),
            pltpu.VMEM((1, shape[2]), jnp.float32),
            pltpu.VMEM(shape[1:], jnp.float32),
            pltpu.SemaphoreType.DMA((cols,)),
            pltpu.SemaphoreType.DMA((cols,)),
            pltpu.SemaphoreType.DMA((rows,)),
            pltpu.SemaphoreType.DMA((rows,)),
            pltpu.SemaphoreType.DMA((rows,)),
            pltpu.SemaphoreType.DMA((rows,)),
            pltpu.SemaphoreType.DMA((cols,)),
            pltpu.SemaphoreType.DMA((cols,)),
        ],
        compiler_params=pltpu.CompilerParams(collective_id=1, has_side_effects=True),
    )(pieces)
    return total.reshape(matrix.shape)

def local(coords, mode_shapes, output_shapes, response_gain):
    rows = lax.axis_size("row")
    cols = lax.axis_size("col")
    mode_count, block_nodes = mode_shapes.shape
    packed = pack_block(coords, mode_shapes)
    partial = row_exchange(packed, rows, cols, mode_count)
    total = all_reduce(partial, rows, cols)
    modal_csd = total + total.T
    real_part = response_gain[0]
    imag_part = response_gain[1]
    weighted = (
        real_part[:, None] * real_part[None, :] + imag_part[:, None] * imag_part[None, :]
    ) * modal_csd
    weighted_high, weighted_low = split_parts(weighted)
    mapped = jnp.dot(output_shapes, weighted_high, preferred_element_type=jnp.float32)
    mapped = mapped + jnp.dot(output_shapes, weighted_low, preferred_element_type=jnp.float32)
    response_power = jnp.sum(mapped * output_shapes.astype(jnp.float32), axis=1)
    return (response_power, modal_csd)


def solution(mesh):
    in_specs = (P(None, ("row", "col")), P(None, ("row", "col")), P(("row", "col"), None), P())
    out_specs = (P(("row", "col")), P())
    return jax.shard_map(local, mesh=mesh, in_specs=in_specs, out_specs=out_specs, check_vma=False)
```

```python
import functools
import math

import jax
import jax.numpy as jnp
from jax import lax
from jax.experimental import pallas as pl
from jax.experimental.pallas import tpu as pltpu
from jax.sharding import PartitionSpec as P

wave_scale = 0.35 / 64.0


def coherence(left_points, right_points):
    difference = left_points[:, :, None] - right_points[:, None, :]
    squared = jnp.sum(difference * difference, axis=0)
    return jnp.sinc(wave_scale * jnp.sqrt(squared)).astype(jnp.bfloat16)


def split_parts(matrix):
    high_part = matrix.astype(jnp.bfloat16)
    low_part = (matrix - high_part.astype(jnp.float32)).astype(jnp.bfloat16)
    return (high_part, low_part)


def pack_block(coords, mode_shapes):
    wide = coords.astype(jnp.float32)
    high = jnp.floor(wide * (1.0 / 256.0))
    low = wide - 256.0 * high
    pad = jnp.zeros((10, wide.shape[1]), jnp.float32)
    extra = jnp.concatenate([high, low, pad], axis=0).astype(jnp.bfloat16)
    return jnp.concatenate([mode_shapes, extra], axis=0)


def unpack_points(packed, mode_count):
    high = packed[..., mode_count:mode_count + 3, :].astype(jnp.float32)
    low = packed[..., mode_count + 3:mode_count + 6, :].astype(jnp.float32)
    return high * 256.0 + low


CHUNK = 32
SIN_TERMS = [(-1) ** k * math.pi ** (2 * k) / math.factorial(2 * k + 1) / wave_scale for k in range(6)]


def coherence_chunk(dx, dy, dz):
    squared = dx * dx + dy * dy + dz * dz
    safe = jnp.maximum(squared, 1e-30)
    root_inv = lax.rsqrt(safe)
    x = safe * root_inv * wave_scale
    n = jnp.floor(x + 0.5)
    f = x - n
    h = n * 0.5
    sign = 1.0 - 4.0 * (h - jnp.floor(h))
    f2 = f * f
    q = SIN_TERMS[4]
    for term in SIN_TERMS[3::-1]:
        q = q * f2 + term
    return (sign * f) * (q * root_inv)


def block_points(slot_ref, mode_count):
    tail = slot_ref[mode_count:mode_count + 16, :].astype(jnp.float32)
    return [tail[k:k + 1, :] * 256.0 + tail[k + 3:k + 4, :] for k in range(3)]


def accumulate_block(slot_ref, weight, rowpts_ref, out_ref, tile_ref, mode_count):
    bx, by, bz = block_points(slot_ref, mode_count)
    length = tile_ref.shape[0]

    def chunk(c, carry):
        r0 = pl.multiple_of(c * CHUNK, CHUNK)
        dx = rowpts_ref[0, pl.ds(r0, CHUNK), :] - bx
        dy = rowpts_ref[1, pl.ds(r0, CHUNK), :] - by
        dz = rowpts_ref[2, pl.ds(r0, CHUNK), :] - bz
        tile_ref[pl.ds(r0, CHUNK), :] = coherence_chunk(dx, dy, dz).astype(jnp.bfloat16)
        return carry

    lax.fori_loop(0, length // CHUNK, chunk, 0, unroll=8)
    shapes = slot_ref[0:mode_count, :] * weight.astype(jnp.bfloat16)
    product = lax.dot_general(
        tile_ref[...], shapes, (((1,), (1,)), ((), ())), preferred_element_type=jnp.float32
    )
    out_ref[...] += product


def shift_of(j, rows):
    odd = j % 2
    return odd * j + (1 - odd) * (rows - j)


def row_kernel(rows, cols, mode_count, packed_ref, out_ref, recv, colbuf, rowpts_ref, tile_ref, acc_ref,
               send_sems, recv_sems, col_send, col_recv):
    me = lax.axis_index("row")
    col = lax.axis_index("col")
    half = rows // 2
    nodes = packed_ref.shape[1]
    colbuf[...] = jnp.zeros_like(colbuf)
    barrier = pltpu.get_barrier_semaphore()
    for p in range(1, rows):
        pl.semaphore_signal(
            barrier, 1, device_id=(lax.rem(me + p, rows), col), device_id_type=pl.DeviceIdType.MESH
        )
    for p in range(1, cols):
        pl.semaphore_signal(
            barrier, 1, device_id=(me, lax.rem(col + p, cols)), device_id_type=pl.DeviceIdType.MESH
        )
    pl.semaphore_wait(barrier, rows - 1 + cols - 1)

    def col_copy(s, slot):
        return pltpu.make_async_remote_copy(
            src_ref=packed_ref,
            dst_ref=colbuf.at[slot],
            send_sem=col_send.at[s],
            recv_sem=col_recv.at[slot],
            device_id=(me, s),
            device_id_type=pl.DeviceIdType.MESH,
        )

    def transfer(k):
        target = lax.rem(me + rows - shift_of(k + 1, rows), rows)
        return pltpu.make_async_remote_copy(
            src_ref=packed_ref,
            dst_ref=recv.at[k],
            send_sem=send_sems.at[k],
            recv_sem=recv_sems.at[k],
            device_id=(target, col),
            device_id_type=pl.DeviceIdType.MESH,
        )

    for k in range(half):
        transfer(k).start()
    for p in range(1, cols):
        col_copy(lax.rem(col + p, cols), col).start()
    for s in range(cols):
        @pl.when(s != col)
        def _():
            col_copy(s, s).wait_recv()

    eye = (lax.broadcasted_iota(jnp.int32, (nodes, nodes), 0)
           == lax.broadcasted_iota(jnp.int32, (nodes, nodes), 1)).astype(jnp.bfloat16)
    own_tail = packed_ref[mode_count:mode_count + 16, :]
    for s in range(cols):
        tail = jnp.where(s == col, own_tail, colbuf[s, mode_count:mode_count + 16, :])
        moved = lax.dot_general(eye, tail, (((1,), (1,)), ((), ())), preferred_element_type=jnp.float32)
        for k in range(3):
            column = moved[:, k:k + 1] * 256.0 + moved[:, k + 3:k + 4]
            rowpts_ref[k, s * nodes:(s + 1) * nodes, :] = jnp.broadcast_to(column, (nodes, nodes))

    acc_ref[...] = jnp.zeros_like(acc_ref)
    accumulate_block(packed_ref, jnp.float32(0.5), rowpts_ref, acc_ref, tile_ref, mode_count)

    def step(k, carry):
        transfer(k).wait_recv()
        weight = jnp.where(k == half - 1, 0.5, 1.0).astype(jnp.float32)
        accumulate_block(recv.at[k], weight, rowpts_ref, acc_ref, tile_ref, mode_count)
        return carry

    lax.fori_loop(0, half, step, 0)

    own_shapes = packed_ref[0:mode_count, :]
    partial = jnp.zeros(out_ref.shape, jnp.float32)
    for s in range(cols):
        shapes = jnp.where(s == col, own_shapes, colbuf[s, 0:mode_count, :])
        part = acc_ref[s * nodes:(s + 1) * nodes, :]
        high = part.astype(jnp.bfloat16)
        low = (part - high.astype(jnp.float32)).astype(jnp.bfloat16)
        partial = partial + jnp.dot(shapes, high, preferred_element_type=jnp.float32)
        partial = partial + jnp.dot(shapes, low, preferred_element_type=jnp.float32)
    out_ref[...] = partial

    for k in range(half):
        transfer(k).wait_send()
    for s in range(cols):
        @pl.when(s != col)
        def _():
            col_copy(s, col).wait_send()


def row_exchange(packed, rows, cols, mode_count):
    nodes = packed.shape[1]
    length = cols * nodes
    half = rows // 2
    vmem = pltpu.MemorySpace.VMEM
    flops = 2 * (half + 1) * length * nodes * mode_count + 4 * length * mode_count * mode_count
    return pl.pallas_call(
        functools.partial(row_kernel, rows, cols, mode_count),
        out_shape=jax.ShapeDtypeStruct((mode_count, mode_count), jnp.float32),
        in_specs=[pl.BlockSpec(memory_space=vmem)],
        out_specs=pl.BlockSpec(memory_space=vmem),
        scratch_shapes=[
            pltpu.VMEM((half,) + packed.shape, packed.dtype),
            pltpu.VMEM((cols,) + packed.shape, packed.dtype),
            pltpu.VMEM((3, length, nodes), jnp.float32),
            pltpu.VMEM((length, nodes), jnp.bfloat16),
            pltpu.VMEM((length, mode_count), jnp.float32),
            pltpu.SemaphoreType.DMA((half,)),
            pltpu.SemaphoreType.DMA((half,)),
            pltpu.SemaphoreType.DMA((cols,)),
            pltpu.SemaphoreType.DMA((cols,)),
        ],
        compiler_params=pltpu.CompilerParams(
            collective_id=0, has_side_effects=True, vmem_limit_bytes=48 * 1024 * 1024
        ),
        cost_estimate=pl.CostEstimate(
            flops=flops, transcendentals=(half + 1) * length * nodes, bytes_accessed=4 * 1024 * 1024
        ),
    )(packed)

def gather_all(block, axis, count):
    spread = jnp.broadcast_to(block[None], (count,) + block.shape)
    return lax.all_to_all(spread, axis, 0, 0, tiled=True)


def ar_kernel(rows, cols, y_ref, out_ref, buf_a, buf_b, buf_g, buf_c, red_a, red_b, red_c,
              sa, ra, sb, rb, sg, rg, sc, rc):
    me_r = lax.axis_index("row")
    me_c = lax.axis_index("col")
    buf_a[...] = jnp.zeros_like(buf_a)
    buf_b[...] = jnp.zeros_like(buf_b)
    buf_g[...] = jnp.zeros_like(buf_g)
    buf_c[...] = jnp.zeros_like(buf_c)
    barrier = pltpu.get_barrier_semaphore()
    for p in range(1, cols):
        pl.semaphore_signal(
            barrier, 1, device_id=(me_r, lax.rem(me_c + p, cols)), device_id_type=pl.DeviceIdType.MESH
        )
    for p in range(1, rows):
        pl.semaphore_signal(
            barrier, 1, device_id=(lax.rem(me_r + p, rows), me_c), device_id_type=pl.DeviceIdType.MESH
        )
    pl.semaphore_wait(barrier, cols - 1 + rows - 1)

    def copy(src, dst, send, recv, sem_index, slot, peer):
        return pltpu.make_async_remote_copy(
            src_ref=src,
            dst_ref=dst,
            send_sem=send.at[sem_index],
            recv_sem=recv.at[slot],
            device_id=peer,
            device_id_type=pl.DeviceIdType.MESH,
        )

    def exchange(src_of, dst_of, send, recv, count, me, peer_of):
        for p in range(1, count):
            s = lax.rem(me + p, count)
            copy(src_of(s), dst_of(me), send, recv, s, me, peer_of(s)).start()
        for s in range(count):
            @pl.when(s != me)
            def _():
                copy(src_of(s), dst_of(s), send, recv, s, s, peer_of(s)).wait_recv()

    def finish(src_of, dst_of, send, recv, count, me, peer_of):
        for s in range(count):
            @pl.when(s != me)
            def _():
                copy(src_of(s), dst_of(me), send, recv, s, me, peer_of(s)).wait_send()

    col_peer = lambda s: (me_r, s)
    row_peer = lambda s: (s, me_c)
    col_a = (lambda s: y_ref.at[s], lambda s: buf_a.at[s], sa, ra, cols, me_c, col_peer)
    exchange(*col_a)
    chunk = y_ref[me_c]
    for s in range(cols):
        chunk = chunk + buf_a[s]
    red_a[...] = chunk
    row_b = (lambda s: red_a.at[pl.ds(s, 1)], lambda s: buf_b.at[pl.ds(s, 1)], sb, rb, rows, me_r, row_peer)
    exchange(*row_b)
    piece = red_a[pl.ds(me_r, 1), :] + jnp.sum(buf_b[...], axis=0, keepdims=True)
    red_b[...] = piece
    row_g = (lambda s: red_b, lambda s: buf_g.at[pl.ds(s, 1)], sg, rg, rows, me_r, row_peer)
    exchange(*row_g)
    lines = lax.broadcasted_iota(jnp.int32, chunk.shape, 0)
    total = jnp.where(lines == me_r, jnp.broadcast_to(piece, chunk.shape), buf_g[...])
    red_c[...] = total
    col_c = (lambda s: red_c, lambda s: buf_c.at[s], sc, rc, cols, me_c, col_peer)
    exchange(*col_c)
    for s in range(cols):
        out_ref[s] = jnp.where(s == me_c, total, buf_c[s])
    finish(*col_a)
    finish(*row_b)
    finish(*row_g)
    finish(*col_c)


def all_reduce(matrix, rows, cols):
    pieces = matrix.reshape(cols, rows, -1)
    shape = pieces.shape
    vmem = pltpu.MemorySpace.VMEM
    total = pl.pallas_call(
        functools.partial(ar_kernel, rows, cols),
        out_shape=jax.ShapeDtypeStruct(shape, jnp.float32),
        in_specs=[pl.BlockSpec(memory_space=vmem)],
        out_specs=pl.BlockSpec(memory_space=vmem),
        scratch_shapes=[
            pltpu.VMEM(shape, jnp.float32),
            pltpu.VMEM(shape[1:], jnp.float32),
            pltpu.VMEM(shape[1:], jnp.float32),
            pltpu.VMEM(shape, jnp.float32),
            pltpu.VMEM(shape[1:], jnp.float32),
            pltpu.VMEM((1, shape[2]), jnp.float32),
            pltpu.VMEM(shape[1:], jnp.float32),
            pltpu.SemaphoreType.DMA((cols,)),
            pltpu.SemaphoreType.DMA((cols,)),
            pltpu.SemaphoreType.DMA((rows,)),
            pltpu.SemaphoreType.DMA((rows,)),
            pltpu.SemaphoreType.DMA((rows,)),
            pltpu.SemaphoreType.DMA((rows,)),
            pltpu.SemaphoreType.DMA((cols,)),
            pltpu.SemaphoreType.DMA((cols,)),
        ],
        compiler_params=pltpu.CompilerParams(collective_id=1, has_side_effects=True),
    )(pieces)
    return total.reshape(matrix.shape)

def local(coords, mode_shapes, output_shapes, response_gain):
    rows = lax.axis_size("row")
    cols = lax.axis_size("col")
    mode_count, block_nodes = mode_shapes.shape
    packed = pack_block(coords, mode_shapes)
    partial = row_exchange(packed, rows, cols, mode_count)
    total = all_reduce(partial, rows, cols)
    modal_csd = total + total.T
    real_part = response_gain[0]
    imag_part = response_gain[1]
    weighted = (
        real_part[:, None] * real_part[None, :] + imag_part[:, None] * imag_part[None, :]
    ) * modal_csd
    weighted_high, weighted_low = split_parts(weighted)
    mapped = jnp.dot(output_shapes, weighted_high, preferred_element_type=jnp.float32)
    mapped = mapped + jnp.dot(output_shapes, weighted_low, preferred_element_type=jnp.float32)
    response_power = jnp.sum(mapped * output_shapes.astype(jnp.float32), axis=1)
    return (response_power, modal_csd)


def solution(mesh):
    in_specs = (P(None, ("row", "col")), P(None, ("row", "col")), P(("row", "col"), None), P())
    out_specs = (P(("row", "col")), P())
    return jax.shard_map(local, mesh=mesh, in_specs=in_specs, out_specs=out_specs, check_vma=False)
```

```python
import functools
import math

import jax
import jax.numpy as jnp
from jax import lax
from jax.experimental import pallas as pl
from jax.experimental.pallas import tpu as pltpu
from jax.sharding import PartitionSpec as P

wave_scale = 0.35 / 64.0


def coherence(left_points, right_points):
    difference = left_points[:, :, None] - right_points[:, None, :]
    squared = jnp.sum(difference * difference, axis=0)
    return jnp.sinc(wave_scale * jnp.sqrt(squared)).astype(jnp.bfloat16)


def split_parts(matrix):
    high_part = matrix.astype(jnp.bfloat16)
    low_part = (matrix - high_part.astype(jnp.float32)).astype(jnp.bfloat16)
    return (high_part, low_part)


def pack_block(coords, mode_shapes):
    wide = coords.astype(jnp.float32)
    high = jnp.floor(wide * (1.0 / 256.0))
    low = wide - 256.0 * high
    pad = jnp.zeros((10, wide.shape[1]), jnp.float32)
    extra = jnp.concatenate([high, low, pad], axis=0).astype(jnp.bfloat16)
    return jnp.concatenate([mode_shapes, extra], axis=0)


def unpack_points(packed, mode_count):
    high = packed[..., mode_count:mode_count + 3, :].astype(jnp.float32)
    low = packed[..., mode_count + 3:mode_count + 6, :].astype(jnp.float32)
    return high * 256.0 + low


CHUNK = 32
SIN_TERMS = [(-1) ** k * math.pi ** (2 * k) / math.factorial(2 * k + 1) / wave_scale for k in range(6)]


def coherence_chunk(dx, dy, dz):
    squared = dx * dx + dy * dy + dz * dz
    safe = jnp.maximum(squared, 1e-30)
    root_inv = lax.rsqrt(safe)
    x = safe * root_inv * wave_scale
    n = jnp.floor(x + 0.5)
    f = x - n
    h = n * 0.5
    sign = 1.0 - 4.0 * (h - jnp.floor(h))
    f2 = f * f
    q = SIN_TERMS[4]
    for term in SIN_TERMS[3::-1]:
        q = q * f2 + term
    return (sign * f) * (q * root_inv)


def block_points(slot_ref, mode_count):
    tail = slot_ref[mode_count:mode_count + 16, :].astype(jnp.float32)
    return [tail[k:k + 1, :] * 256.0 + tail[k + 3:k + 4, :] for k in range(3)]


def accumulate_block(slot_ref, weight, rowpts_ref, out_ref, tile_ref, mode_count):
    bx, by, bz = block_points(slot_ref, mode_count)
    length = tile_ref.shape[0]

    def chunk(c, carry):
        r0 = pl.multiple_of(c * CHUNK, CHUNK)
        dx = rowpts_ref[0, pl.ds(r0, CHUNK), :] - bx
        dy = rowpts_ref[1, pl.ds(r0, CHUNK), :] - by
        dz = rowpts_ref[2, pl.ds(r0, CHUNK), :] - bz
        tile_ref[pl.ds(r0, CHUNK), :] = coherence_chunk(dx, dy, dz).astype(jnp.bfloat16)
        return carry

    lax.fori_loop(0, length // CHUNK, chunk, 0, unroll=8)
    shapes = slot_ref[0:mode_count, :] * weight.astype(jnp.bfloat16)
    product = lax.dot_general(
        tile_ref[...], shapes, (((1,), (1,)), ((), ())), preferred_element_type=jnp.float32
    )
    out_ref[...] += product


def shift_of(j, rows):
    odd = j % 2
    return odd * j + (1 - odd) * (rows - j)


def row_kernel(rows, cols, mode_count, packed_ref, out_ref, recv, colbuf, rowpts_ref, tile_ref, acc_ref,
               send_sems, recv_sems, col_send, col_recv):
    me = lax.axis_index("row")
    col = lax.axis_index("col")
    half = rows // 2
    nodes = packed_ref.shape[1]
    colbuf[...] = jnp.zeros_like(colbuf)
    barrier = pltpu.get_barrier_semaphore()
    for p in range(1, rows):
        pl.semaphore_signal(
            barrier, 1, device_id=(lax.rem(me + p, rows), col), device_id_type=pl.DeviceIdType.MESH
        )
    for p in range(1, cols):
        pl.semaphore_signal(
            barrier, 1, device_id=(me, lax.rem(col + p, cols)), device_id_type=pl.DeviceIdType.MESH
        )
    pl.semaphore_wait(barrier, rows - 1 + cols - 1)

    def col_copy(s, slot):
        return pltpu.make_async_remote_copy(
            src_ref=packed_ref,
            dst_ref=colbuf.at[slot],
            send_sem=col_send.at[s],
            recv_sem=col_recv.at[slot],
            device_id=(me, s),
            device_id_type=pl.DeviceIdType.MESH,
        )

    def transfer(k):
        target = lax.rem(me + rows - shift_of(k + 1, rows), rows)
        return pltpu.make_async_remote_copy(
            src_ref=packed_ref,
            dst_ref=recv.at[k],
            send_sem=send_sems.at[k],
            recv_sem=recv_sems.at[k],
            device_id=(target, col),
            device_id_type=pl.DeviceIdType.MESH,
        )

    for k in range(half):
        transfer(k).start()
    for p in range(1, cols):
        col_copy(lax.rem(col + p, cols), col).start()
    eye = (lax.broadcasted_iota(jnp.int32, (nodes, nodes), 0)
           == lax.broadcasted_iota(jnp.int32, (nodes, nodes), 1)).astype(jnp.bfloat16)

    def place_points(slot, tail):
        moved = lax.dot_general(eye, tail, (((1,), (1,)), ((), ())), preferred_element_type=jnp.float32)
        start = pl.multiple_of(slot * nodes, nodes)
        for k in range(3):
            column = moved[:, k:k + 1] * 256.0 + moved[:, k + 3:k + 4]
            rowpts_ref[k, pl.ds(start, nodes), :] = jnp.broadcast_to(column, (nodes, nodes))

    place_points(col, packed_ref[mode_count:mode_count + 16, :])
    for p in range(1, cols):
        s = lax.rem(col + cols - p, cols)
        col_copy(s, s).wait_recv()
        place_points(s, colbuf[s, mode_count:mode_count + 16, :])

    acc_ref[...] = jnp.zeros_like(acc_ref)
    accumulate_block(packed_ref, jnp.float32(0.5), rowpts_ref, acc_ref, tile_ref, mode_count)

    def step(k, carry):
        transfer(k).wait_recv()
        weight = jnp.where(k == half - 1, 0.5, 1.0).astype(jnp.float32)
        accumulate_block(recv.at[k], weight, rowpts_ref, acc_ref, tile_ref, mode_count)
        return carry

    lax.fori_loop(0, half, step, 0)

    own_shapes = packed_ref[0:mode_count, :]
    partial = jnp.zeros(out_ref.shape, jnp.float32)
    for s in range(cols):
        shapes = jnp.where(s == col, own_shapes, colbuf[s, 0:mode_count, :])
        part = acc_ref[s * nodes:(s + 1) * nodes, :]
        high = part.astype(jnp.bfloat16)
        low = (part - high.astype(jnp.float32)).astype(jnp.bfloat16)
        partial = partial + jnp.dot(shapes, high, preferred_element_type=jnp.float32)
        partial = partial + jnp.dot(shapes, low, preferred_element_type=jnp.float32)
    out_ref[...] = partial

    for k in range(half):
        transfer(k).wait_send()
    for s in range(cols):
        @pl.when(s != col)
        def _():
            col_copy(s, col).wait_send()


def row_exchange(packed, rows, cols, mode_count):
    nodes = packed.shape[1]
    length = cols * nodes
    half = rows // 2
    vmem = pltpu.MemorySpace.VMEM
    flops = 2 * (half + 1) * length * nodes * mode_count + 4 * length * mode_count * mode_count
    return pl.pallas_call(
        functools.partial(row_kernel, rows, cols, mode_count),
        out_shape=jax.ShapeDtypeStruct((mode_count, mode_count), jnp.float32),
        in_specs=[pl.BlockSpec(memory_space=vmem)],
        out_specs=pl.BlockSpec(memory_space=vmem),
        scratch_shapes=[
            pltpu.VMEM((half,) + packed.shape, packed.dtype),
            pltpu.VMEM((cols,) + packed.shape, packed.dtype),
            pltpu.VMEM((3, length, nodes), jnp.float32),
            pltpu.VMEM((length, nodes), jnp.bfloat16),
            pltpu.VMEM((length, mode_count), jnp.float32),
            pltpu.SemaphoreType.DMA((half,)),
            pltpu.SemaphoreType.DMA((half,)),
            pltpu.SemaphoreType.DMA((cols,)),
            pltpu.SemaphoreType.DMA((cols,)),
        ],
        compiler_params=pltpu.CompilerParams(
            collective_id=0, has_side_effects=True, vmem_limit_bytes=48 * 1024 * 1024
        ),
        cost_estimate=pl.CostEstimate(
            flops=flops, transcendentals=(half + 1) * length * nodes, bytes_accessed=4 * 1024 * 1024
        ),
    )(packed)

def gather_all(block, axis, count):
    spread = jnp.broadcast_to(block[None], (count,) + block.shape)
    return lax.all_to_all(spread, axis, 0, 0, tiled=True)


def ar_kernel(rows, cols, y_ref, out_ref, buf_a, buf_b, buf_g, buf_c, red_a, red_b, red_c,
              sa, ra, sb, rb, sg, rg, sc, rc):
    me_r = lax.axis_index("row")
    me_c = lax.axis_index("col")
    buf_a[...] = jnp.zeros_like(buf_a)
    buf_b[...] = jnp.zeros_like(buf_b)
    buf_g[...] = jnp.zeros_like(buf_g)
    buf_c[...] = jnp.zeros_like(buf_c)
    barrier = pltpu.get_barrier_semaphore()
    for p in range(1, cols):
        pl.semaphore_signal(
            barrier, 1, device_id=(me_r, lax.rem(me_c + p, cols)), device_id_type=pl.DeviceIdType.MESH
        )
    for p in range(1, rows):
        pl.semaphore_signal(
            barrier, 1, device_id=(lax.rem(me_r + p, rows), me_c), device_id_type=pl.DeviceIdType.MESH
        )
    pl.semaphore_wait(barrier, cols - 1 + rows - 1)

    def copy(src, dst, send, recv, sem_index, slot, peer):
        return pltpu.make_async_remote_copy(
            src_ref=src,
            dst_ref=dst,
            send_sem=send.at[sem_index],
            recv_sem=recv.at[slot],
            device_id=peer,
            device_id_type=pl.DeviceIdType.MESH,
        )

    def exchange(src_of, dst_of, send, recv, count, me, peer_of):
        for p in range(1, count):
            s = lax.rem(me + p, count)
            copy(src_of(s), dst_of(me), send, recv, s, me, peer_of(s)).start()
        for s in range(count):
            @pl.when(s != me)
            def _():
                copy(src_of(s), dst_of(s), send, recv, s, s, peer_of(s)).wait_recv()

    def finish(src_of, dst_of, send, recv, count, me, peer_of):
        for s in range(count):
            @pl.when(s != me)
            def _():
                copy(src_of(s), dst_of(me), send, recv, s, me, peer_of(s)).wait_send()

    col_peer = lambda s: (me_r, s)
    row_peer = lambda s: (s, me_c)
    col_a = (lambda s: y_ref.at[s], lambda s: buf_a.at[s], sa, ra, cols, me_c, col_peer)
    exchange(*col_a)
    chunk = y_ref[me_c]
    for s in range(cols):
        chunk = chunk + buf_a[s]
    red_a[...] = chunk
    row_b = (lambda s: red_a.at[pl.ds(s, 1)], lambda s: buf_b.at[pl.ds(s, 1)], sb, rb, rows, me_r, row_peer)
    exchange(*row_b)
    piece = red_a[pl.ds(me_r, 1), :] + jnp.sum(buf_b[...], axis=0, keepdims=True)
    red_b[...] = piece
    row_g = (lambda s: red_b, lambda s: buf_g.at[pl.ds(s, 1)], sg, rg, rows, me_r, row_peer)
    exchange(*row_g)
    lines = lax.broadcasted_iota(jnp.int32, chunk.shape, 0)
    total = jnp.where(lines == me_r, jnp.broadcast_to(piece, chunk.shape), buf_g[...])
    red_c[...] = total
    col_c = (lambda s: red_c, lambda s: buf_c.at[s], sc, rc, cols, me_c, col_peer)
    exchange(*col_c)
    for s in range(cols):
        out_ref[s] = jnp.where(s == me_c, total, buf_c[s])
    finish(*col_a)
    finish(*row_b)
    finish(*row_g)
    finish(*col_c)


def all_reduce(matrix, rows, cols):
    pieces = matrix.reshape(cols, rows, -1)
    shape = pieces.shape
    vmem = pltpu.MemorySpace.VMEM
    total = pl.pallas_call(
        functools.partial(ar_kernel, rows, cols),
        out_shape=jax.ShapeDtypeStruct(shape, jnp.float32),
        in_specs=[pl.BlockSpec(memory_space=vmem)],
        out_specs=pl.BlockSpec(memory_space=vmem),
        scratch_shapes=[
            pltpu.VMEM(shape, jnp.float32),
            pltpu.VMEM(shape[1:], jnp.float32),
            pltpu.VMEM(shape[1:], jnp.float32),
            pltpu.VMEM(shape, jnp.float32),
            pltpu.VMEM(shape[1:], jnp.float32),
            pltpu.VMEM((1, shape[2]), jnp.float32),
            pltpu.VMEM(shape[1:], jnp.float32),
            pltpu.SemaphoreType.DMA((cols,)),
            pltpu.SemaphoreType.DMA((cols,)),
            pltpu.SemaphoreType.DMA((rows,)),
            pltpu.SemaphoreType.DMA((rows,)),
            pltpu.SemaphoreType.DMA((rows,)),
            pltpu.SemaphoreType.DMA((rows,)),
            pltpu.SemaphoreType.DMA((cols,)),
            pltpu.SemaphoreType.DMA((cols,)),
        ],
        compiler_params=pltpu.CompilerParams(collective_id=1, has_side_effects=True),
    )(pieces)
    return total.reshape(matrix.shape)

def local(coords, mode_shapes, output_shapes, response_gain):
    rows = lax.axis_size("row")
    cols = lax.axis_size("col")
    mode_count, block_nodes = mode_shapes.shape
    packed = pack_block(coords, mode_shapes)
    partial = row_exchange(packed, rows, cols, mode_count)
    total = all_reduce(partial, rows, cols)
    modal_csd = total + total.T
    real_part = response_gain[0]
    imag_part = response_gain[1]
    weighted = (
        real_part[:, None] * real_part[None, :] + imag_part[:, None] * imag_part[None, :]
    ) * modal_csd
    weighted_high, weighted_low = split_parts(weighted)
    mapped = jnp.dot(output_shapes, weighted_high, preferred_element_type=jnp.float32)
    mapped = mapped + jnp.dot(output_shapes, weighted_low, preferred_element_type=jnp.float32)
    response_power = jnp.sum(mapped * output_shapes.astype(jnp.float32), axis=1)
    return (response_power, modal_csd)


def solution(mesh):
    in_specs = (P(None, ("row", "col")), P(None, ("row", "col")), P(("row", "col"), None), P())
    out_specs = (P(("row", "col")), P())
    return jax.shard_map(local, mesh=mesh, in_specs=in_specs, out_specs=out_specs, check_vma=False)
```

```python
import functools
import math

import jax
import jax.numpy as jnp
from jax import lax
from jax.experimental import pallas as pl
from jax.experimental.pallas import tpu as pltpu
from jax.sharding import PartitionSpec as P

wave_scale = 0.35 / 64.0


def coherence(left_points, right_points):
    difference = left_points[:, :, None] - right_points[:, None, :]
    squared = jnp.sum(difference * difference, axis=0)
    return jnp.sinc(wave_scale * jnp.sqrt(squared)).astype(jnp.bfloat16)


def split_parts(matrix):
    high_part = matrix.astype(jnp.bfloat16)
    low_part = (matrix - high_part.astype(jnp.float32)).astype(jnp.bfloat16)
    return (high_part, low_part)


def pack_block(coords, mode_shapes):
    wide = coords.astype(jnp.float32)
    high = jnp.floor(wide * (1.0 / 256.0))
    low = wide - 256.0 * high
    pad = jnp.zeros((10, wide.shape[1]), jnp.float32)
    extra = jnp.concatenate([high, low, pad], axis=0).astype(jnp.bfloat16)
    return jnp.concatenate([mode_shapes, extra], axis=0)


def unpack_points(packed, mode_count):
    high = packed[..., mode_count:mode_count + 3, :].astype(jnp.float32)
    low = packed[..., mode_count + 3:mode_count + 6, :].astype(jnp.float32)
    return high * 256.0 + low


CHUNK = 32
SIN_TERMS = [(-1) ** k * math.pi ** (2 * k) / math.factorial(2 * k + 1) / wave_scale for k in range(6)]


def coherence_chunk(dx, dy, dz):
    squared = dx * dx + dy * dy + dz * dz
    safe = jnp.maximum(squared, 1e-30)
    root_inv = lax.rsqrt(safe)
    x = safe * root_inv * wave_scale
    n = jnp.floor(x + 0.5)
    f = x - n
    h = n * 0.5
    sign = 1.0 - 4.0 * (h - jnp.floor(h))
    f2 = f * f
    q = SIN_TERMS[4]
    for term in SIN_TERMS[3::-1]:
        q = q * f2 + term
    return (sign * f) * (q * root_inv)


def block_points(slot_ref, mode_count):
    tail = slot_ref[mode_count:mode_count + 16, :].astype(jnp.float32)
    return [tail[k:k + 1, :] * 256.0 + tail[k + 3:k + 4, :] for k in range(3)]


def accumulate_block(slot_ref, weight, rowpts_ref, out_ref, tile_ref, mode_count):
    bx, by, bz = block_points(slot_ref, mode_count)
    length = tile_ref.shape[0]

    def chunk(c, carry):
        r0 = pl.multiple_of(c * CHUNK, CHUNK)
        dx = rowpts_ref[0, pl.ds(r0, CHUNK), :] - bx
        dy = rowpts_ref[1, pl.ds(r0, CHUNK), :] - by
        dz = rowpts_ref[2, pl.ds(r0, CHUNK), :] - bz
        tile_ref[pl.ds(r0, CHUNK), :] = coherence_chunk(dx, dy, dz).astype(jnp.bfloat16)
        return carry

    lax.fori_loop(0, length // CHUNK, chunk, 0, unroll=8)
    shapes = slot_ref[0:mode_count, :] * weight.astype(jnp.bfloat16)
    product = lax.dot_general(
        tile_ref[...], shapes, (((1,), (1,)), ((), ())), preferred_element_type=jnp.float32
    )
    out_ref[...] += product


def shift_of(j, rows):
    odd = j % 2
    return odd * j + (1 - odd) * (rows - j)


def row_kernel(rows, cols, mode_count, coords_ref, shapes_ref, out_ref, packed_ref, recv, colbuf, rowpts_ref,
               tile_ref, acc_ref, send_sems, recv_sems, col_send, col_recv):
    me = lax.axis_index("row")
    col = lax.axis_index("col")
    half = rows // 2
    nodes = packed_ref.shape[1]
    wide = coords_ref[...].astype(jnp.float32)
    high = jnp.floor(wide * (1.0 / 256.0))
    low = wide - 256.0 * high
    packed_ref[0:mode_count, :] = shapes_ref[...]
    packed_ref[mode_count:mode_count + 3, :] = high.astype(jnp.bfloat16)
    packed_ref[mode_count + 3:mode_count + 6, :] = low.astype(jnp.bfloat16)
    packed_ref[mode_count + 6:mode_count + 16, :] = jnp.zeros((10, nodes), jnp.bfloat16)
    colbuf[...] = jnp.zeros_like(colbuf)
    barrier = pltpu.get_barrier_semaphore()
    for p in range(1, rows):
        pl.semaphore_signal(
            barrier, 1, device_id=(lax.rem(me + p, rows), col), device_id_type=pl.DeviceIdType.MESH
        )
    for p in range(1, cols):
        pl.semaphore_signal(
            barrier, 1, device_id=(me, lax.rem(col + p, cols)), device_id_type=pl.DeviceIdType.MESH
        )
    pl.semaphore_wait(barrier, rows - 1 + cols - 1)

    def col_copy(s, slot):
        return pltpu.make_async_remote_copy(
            src_ref=packed_ref,
            dst_ref=colbuf.at[slot],
            send_sem=col_send.at[s],
            recv_sem=col_recv.at[slot],
            device_id=(me, s),
            device_id_type=pl.DeviceIdType.MESH,
        )

    def transfer(k):
        target = lax.rem(me + rows - shift_of(k + 1, rows), rows)
        return pltpu.make_async_remote_copy(
            src_ref=packed_ref,
            dst_ref=recv.at[k],
            send_sem=send_sems.at[k],
            recv_sem=recv_sems.at[k],
            device_id=(target, col),
            device_id_type=pl.DeviceIdType.MESH,
        )

    for k in range(half):
        transfer(k).start()
    for p in range(1, cols):
        col_copy(lax.rem(col + p, cols), col).start()
    for s in range(cols):
        @pl.when(s != col)
        def _():
            col_copy(s, s).wait_recv()

    eye = (lax.broadcasted_iota(jnp.int32, (nodes, nodes), 0)
           == lax.broadcasted_iota(jnp.int32, (nodes, nodes), 1)).astype(jnp.bfloat16)
    own_tail = packed_ref[mode_count:mode_count + 16, :]
    for s in range(cols):
        tail = jnp.where(s == col, own_tail, colbuf[s, mode_count:mode_count + 16, :])
        moved = lax.dot_general(eye, tail, (((1,), (1,)), ((), ())), preferred_element_type=jnp.float32)
        for k in range(3):
            column = moved[:, k:k + 1] * 256.0 + moved[:, k + 3:k + 4]
            rowpts_ref[k, s * nodes:(s + 1) * nodes, :] = jnp.broadcast_to(column, (nodes, nodes))

    acc_ref[...] = jnp.zeros_like(acc_ref)
    accumulate_block(packed_ref, jnp.float32(0.5), rowpts_ref, acc_ref, tile_ref, mode_count)

    def step(k, carry):
        transfer(k).wait_recv()
        weight = jnp.where(k == half - 1, 0.5, 1.0).astype(jnp.float32)
        accumulate_block(recv.at[k], weight, rowpts_ref, acc_ref, tile_ref, mode_count)
        return carry

    lax.fori_loop(0, half, step, 0)

    own_shapes = packed_ref[0:mode_count, :]
    partial = jnp.zeros(out_ref.shape, jnp.float32)
    for s in range(cols):
        shapes = jnp.where(s == col, own_shapes, colbuf[s, 0:mode_count, :])
        part = acc_ref[s * nodes:(s + 1) * nodes, :]
        high = part.astype(jnp.bfloat16)
        low = (part - high.astype(jnp.float32)).astype(jnp.bfloat16)
        partial = partial + jnp.dot(shapes, high, preferred_element_type=jnp.float32)
        partial = partial + jnp.dot(shapes, low, preferred_element_type=jnp.float32)
    out_ref[...] = partial

    for k in range(half):
        transfer(k).wait_send()
    for s in range(cols):
        @pl.when(s != col)
        def _():
            col_copy(s, col).wait_send()


def row_exchange(coords, mode_shapes, rows, cols, mode_count):
    nodes = mode_shapes.shape[1]
    packed = jax.ShapeDtypeStruct((mode_count + 16, nodes), mode_shapes.dtype)
    length = cols * nodes
    half = rows // 2
    vmem = pltpu.MemorySpace.VMEM
    flops = 2 * (half + 1) * length * nodes * mode_count + 4 * length * mode_count * mode_count
    return pl.pallas_call(
        functools.partial(row_kernel, rows, cols, mode_count),
        out_shape=jax.ShapeDtypeStruct((mode_count, mode_count), jnp.float32),
        in_specs=[pl.BlockSpec(memory_space=vmem)] * 2,
        out_specs=pl.BlockSpec(memory_space=vmem),
        scratch_shapes=[
            pltpu.VMEM(packed.shape, packed.dtype),
            pltpu.VMEM((half,) + packed.shape, packed.dtype),
            pltpu.VMEM((cols,) + packed.shape, packed.dtype),
            pltpu.VMEM((3, length, nodes), jnp.float32),
            pltpu.VMEM((length, nodes), jnp.bfloat16),
            pltpu.VMEM((length, mode_count), jnp.float32),
            pltpu.SemaphoreType.DMA((half,)),
            pltpu.SemaphoreType.DMA((half,)),
            pltpu.SemaphoreType.DMA((cols,)),
            pltpu.SemaphoreType.DMA((cols,)),
        ],
        compiler_params=pltpu.CompilerParams(
            collective_id=0, has_side_effects=True, vmem_limit_bytes=48 * 1024 * 1024
        ),
        cost_estimate=pl.CostEstimate(
            flops=flops, transcendentals=(half + 1) * length * nodes, bytes_accessed=4 * 1024 * 1024
        ),
    )(coords, mode_shapes)

def gather_all(block, axis, count):
    spread = jnp.broadcast_to(block[None], (count,) + block.shape)
    return lax.all_to_all(spread, axis, 0, 0, tiled=True)


def ar_kernel(rows, cols, y_ref, out_ref, buf_a, buf_b, buf_g, buf_c, red_a, red_b, red_c,
              sa, ra, sb, rb, sg, rg, sc, rc):
    me_r = lax.axis_index("row")
    me_c = lax.axis_index("col")
    buf_a[...] = jnp.zeros_like(buf_a)
    buf_b[...] = jnp.zeros_like(buf_b)
    buf_g[...] = jnp.zeros_like(buf_g)
    buf_c[...] = jnp.zeros_like(buf_c)
    barrier = pltpu.get_barrier_semaphore()
    for p in range(1, cols):
        pl.semaphore_signal(
            barrier, 1, device_id=(me_r, lax.rem(me_c + p, cols)), device_id_type=pl.DeviceIdType.MESH
        )
    for p in range(1, rows):
        pl.semaphore_signal(
            barrier, 1, device_id=(lax.rem(me_r + p, rows), me_c), device_id_type=pl.DeviceIdType.MESH
        )
    pl.semaphore_wait(barrier, cols - 1 + rows - 1)

    def copy(src, dst, send, recv, sem_index, slot, peer):
        return pltpu.make_async_remote_copy(
            src_ref=src,
            dst_ref=dst,
            send_sem=send.at[sem_index],
            recv_sem=recv.at[slot],
            device_id=peer,
            device_id_type=pl.DeviceIdType.MESH,
        )

    def exchange(src_of, dst_of, send, recv, count, me, peer_of):
        for p in range(1, count):
            s = lax.rem(me + p, count)
            copy(src_of(s), dst_of(me), send, recv, s, me, peer_of(s)).start()
        for s in range(count):
            @pl.when(s != me)
            def _():
                copy(src_of(s), dst_of(s), send, recv, s, s, peer_of(s)).wait_recv()

    def finish(src_of, dst_of, send, recv, count, me, peer_of):
        for s in range(count):
            @pl.when(s != me)
            def _():
                copy(src_of(s), dst_of(me), send, recv, s, me, peer_of(s)).wait_send()

    col_peer = lambda s: (me_r, s)
    row_peer = lambda s: (s, me_c)
    col_a = (lambda s: y_ref.at[s], lambda s: buf_a.at[s], sa, ra, cols, me_c, col_peer)
    exchange(*col_a)
    chunk = y_ref[me_c]
    for s in range(cols):
        chunk = chunk + buf_a[s]
    red_a[...] = chunk
    row_b = (lambda s: red_a.at[pl.ds(s, 1)], lambda s: buf_b.at[pl.ds(s, 1)], sb, rb, rows, me_r, row_peer)
    exchange(*row_b)
    piece = red_a[pl.ds(me_r, 1), :] + jnp.sum(buf_b[...], axis=0, keepdims=True)
    red_b[...] = piece
    row_g = (lambda s: red_b, lambda s: buf_g.at[pl.ds(s, 1)], sg, rg, rows, me_r, row_peer)
    exchange(*row_g)
    lines = lax.broadcasted_iota(jnp.int32, chunk.shape, 0)
    total = jnp.where(lines == me_r, jnp.broadcast_to(piece, chunk.shape), buf_g[...])
    red_c[...] = total
    col_c = (lambda s: red_c, lambda s: buf_c.at[s], sc, rc, cols, me_c, col_peer)
    exchange(*col_c)
    for s in range(cols):
        out_ref[s] = jnp.where(s == me_c, total, buf_c[s])
    finish(*col_a)
    finish(*row_b)
    finish(*row_g)
    finish(*col_c)


def all_reduce(matrix, rows, cols):
    pieces = matrix.reshape(cols, rows, -1)
    shape = pieces.shape
    vmem = pltpu.MemorySpace.VMEM
    total = pl.pallas_call(
        functools.partial(ar_kernel, rows, cols),
        out_shape=jax.ShapeDtypeStruct(shape, jnp.float32),
        in_specs=[pl.BlockSpec(memory_space=vmem)],
        out_specs=pl.BlockSpec(memory_space=vmem),
        scratch_shapes=[
            pltpu.VMEM(shape, jnp.float32),
            pltpu.VMEM(shape[1:], jnp.float32),
            pltpu.VMEM(shape[1:], jnp.float32),
            pltpu.VMEM(shape, jnp.float32),
            pltpu.VMEM(shape[1:], jnp.float32),
            pltpu.VMEM((1, shape[2]), jnp.float32),
            pltpu.VMEM(shape[1:], jnp.float32),
            pltpu.SemaphoreType.DMA((cols,)),
            pltpu.SemaphoreType.DMA((cols,)),
            pltpu.SemaphoreType.DMA((rows,)),
            pltpu.SemaphoreType.DMA((rows,)),
            pltpu.SemaphoreType.DMA((rows,)),
            pltpu.SemaphoreType.DMA((rows,)),
            pltpu.SemaphoreType.DMA((cols,)),
            pltpu.SemaphoreType.DMA((cols,)),
        ],
        compiler_params=pltpu.CompilerParams(collective_id=1, has_side_effects=True),
    )(pieces)
    return total.reshape(matrix.shape)

def local(coords, mode_shapes, output_shapes, response_gain):
    rows = lax.axis_size("row")
    cols = lax.axis_size("col")
    mode_count, block_nodes = mode_shapes.shape
    partial = row_exchange(coords, mode_shapes, rows, cols, mode_count)
    total = all_reduce(partial, rows, cols)
    modal_csd = total + total.T
    real_part = response_gain[0]
    imag_part = response_gain[1]
    weighted = (
        real_part[:, None] * real_part[None, :] + imag_part[:, None] * imag_part[None, :]
    ) * modal_csd
    weighted_high, weighted_low = split_parts(weighted)
    mapped = jnp.dot(output_shapes, weighted_high, preferred_element_type=jnp.float32)
    mapped = mapped + jnp.dot(output_shapes, weighted_low, preferred_element_type=jnp.float32)
    response_power = jnp.sum(mapped * output_shapes.astype(jnp.float32), axis=1)
    return (response_power, modal_csd)


def solution(mesh):
    in_specs = (P(None, ("row", "col")), P(None, ("row", "col")), P(("row", "col"), None), P())
    out_specs = (P(("row", "col")), P())
    return jax.shard_map(local, mesh=mesh, in_specs=in_specs, out_specs=out_specs, check_vma=False)
```

```python
import functools
import math

import jax
import jax.numpy as jnp
from jax import lax
from jax.experimental import pallas as pl
from jax.experimental.pallas import tpu as pltpu
from jax.sharding import PartitionSpec as P

wave_scale = 0.35 / 64.0


def coherence(left_points, right_points):
    difference = left_points[:, :, None] - right_points[:, None, :]
    squared = jnp.sum(difference * difference, axis=0)
    return jnp.sinc(wave_scale * jnp.sqrt(squared)).astype(jnp.bfloat16)


def split_parts(matrix):
    high_part = matrix.astype(jnp.bfloat16)
    low_part = (matrix - high_part.astype(jnp.float32)).astype(jnp.bfloat16)
    return (high_part, low_part)


def pack_block(coords, mode_shapes):
    wide = coords.astype(jnp.float32)
    high = jnp.floor(wide * (1.0 / 256.0))
    low = wide - 256.0 * high
    pad = jnp.zeros((10, wide.shape[1]), jnp.float32)
    extra = jnp.concatenate([high, low, pad], axis=0).astype(jnp.bfloat16)
    return jnp.concatenate([mode_shapes, extra], axis=0)


def unpack_points(packed, mode_count):
    high = packed[..., mode_count:mode_count + 3, :].astype(jnp.float32)
    low = packed[..., mode_count + 3:mode_count + 6, :].astype(jnp.float32)
    return high * 256.0 + low


CHUNK = 32
SIN_TERMS = [(-1) ** k * math.pi ** (2 * k) / math.factorial(2 * k + 1) / wave_scale for k in range(6)]


def coherence_chunk(dx, dy, dz):
    squared = dx * dx + dy * dy + dz * dz
    safe = jnp.maximum(squared, 1e-30)
    root_inv = lax.rsqrt(safe)
    x = safe * root_inv * wave_scale
    n = jnp.floor(x + 0.5)
    f = x - n
    h = n * 0.5
    sign = 1.0 - 4.0 * (h - jnp.floor(h))
    f2 = f * f
    q = SIN_TERMS[4]
    for term in SIN_TERMS[3::-1]:
        q = q * f2 + term
    return (sign * f) * (q * root_inv)


def block_points(slot_ref, mode_count):
    tail = slot_ref[mode_count:mode_count + 16, :].astype(jnp.float32)
    return [tail[k:k + 1, :] * 256.0 + tail[k + 3:k + 4, :] for k in range(3)]


def accumulate_block(slot_ref, weight, rowpts_ref, out_ref, tile_ref, mode_count):
    bx, by, bz = block_points(slot_ref, mode_count)
    length = tile_ref.shape[0]

    def chunk(c, carry):
        r0 = pl.multiple_of(c * CHUNK, CHUNK)
        dx = rowpts_ref[0, pl.ds(r0, CHUNK), :] - bx
        dy = rowpts_ref[1, pl.ds(r0, CHUNK), :] - by
        dz = rowpts_ref[2, pl.ds(r0, CHUNK), :] - bz
        tile_ref[pl.ds(r0, CHUNK), :] = coherence_chunk(dx, dy, dz).astype(jnp.bfloat16)
        return carry

    lax.fori_loop(0, length // CHUNK, chunk, 0, unroll=8)
    shapes = slot_ref[0:mode_count, :] * weight.astype(jnp.bfloat16)
    product = lax.dot_general(
        tile_ref[...], shapes, (((1,), (1,)), ((), ())), preferred_element_type=jnp.float32
    )
    out_ref[...] += product


def shift_of(j, rows):
    odd = j % 2
    return odd * j + (1 - odd) * (rows - j)


def row_kernel(rows, cols, mode_count, packed_ref, out_ref, recv, colbuf, rowpts_ref, tile_ref, acc_ref,
               send_sems, recv_sems, col_send, col_recv):
    me = lax.axis_index("row")
    col = lax.axis_index("col")
    half = rows // 2
    nodes = packed_ref.shape[1]
    colbuf[...] = jnp.zeros_like(colbuf)
    barrier = pltpu.get_barrier_semaphore()
    for p in range(1, rows):
        pl.semaphore_signal(
            barrier, 1, device_id=(lax.rem(me + p, rows), col), device_id_type=pl.DeviceIdType.MESH
        )
    for p in range(1, cols):
        pl.semaphore_signal(
            barrier, 1, device_id=(me, lax.rem(col + p, cols)), device_id_type=pl.DeviceIdType.MESH
        )
    pl.semaphore_wait(barrier, rows - 1 + cols - 1)

    def col_copy(s, slot):
        return pltpu.make_async_remote_copy(
            src_ref=packed_ref,
            dst_ref=colbuf.at[slot],
            send_sem=col_send.at[s],
            recv_sem=col_recv.at[slot],
            device_id=(me, s),
            device_id_type=pl.DeviceIdType.MESH,
        )

    def transfer(k):
        target = lax.rem(me + rows - shift_of(k + 1, rows), rows)
        return pltpu.make_async_remote_copy(
            src_ref=packed_ref,
            dst_ref=recv.at[k],
            send_sem=send_sems.at[k],
            recv_sem=recv_sems.at[k],
            device_id=(target, col),
            device_id_type=pl.DeviceIdType.MESH,
        )

    for k in range(half):
        transfer(k).start()
    for p in range(1, cols):
        col_copy(lax.rem(col + p, cols), col).start()
    for s in range(cols):
        @pl.when(s != col)
        def _():
            col_copy(s, s).wait_recv()

    eye = (lax.broadcasted_iota(jnp.int32, (nodes, nodes), 0)
           == lax.broadcasted_iota(jnp.int32, (nodes, nodes), 1)).astype(jnp.bfloat16)
    own_tail = packed_ref[mode_count:mode_count + 16, :]
    for s in range(cols):
        tail = jnp.where(s == col, own_tail, colbuf[s, mode_count:mode_count + 16, :])
        moved = lax.dot_general(eye, tail, (((1,), (1,)), ((), ())), preferred_element_type=jnp.float32)
        for k in range(3):
            column = moved[:, k:k + 1] * 256.0 + moved[:, k + 3:k + 4]
            rowpts_ref[k, s * nodes:(s + 1) * nodes, :] = jnp.broadcast_to(column, (nodes, nodes))

    acc_ref[...] = jnp.zeros_like(acc_ref)
    accumulate_block(packed_ref, jnp.float32(0.5), rowpts_ref, acc_ref, tile_ref, mode_count)

    def step(k, carry):
        transfer(k).wait_recv()
        weight = jnp.where(k == half - 1, 0.5, 1.0).astype(jnp.float32)
        accumulate_block(recv.at[k], weight, rowpts_ref, acc_ref, tile_ref, mode_count)
        return carry

    lax.fori_loop(0, half, step, 0)

    own_shapes = packed_ref[0:mode_count, :]
    partial = jnp.zeros(out_ref.shape, jnp.float32)
    for s in range(cols):
        shapes = jnp.where(s == col, own_shapes, colbuf[s, 0:mode_count, :])
        part = acc_ref[s * nodes:(s + 1) * nodes, :]
        high = part.astype(jnp.bfloat16)
        low = (part - high.astype(jnp.float32)).astype(jnp.bfloat16)
        partial = partial + jnp.dot(shapes, high, preferred_element_type=jnp.float32)
        partial = partial + jnp.dot(shapes, low, preferred_element_type=jnp.float32)
    out_ref[...] = partial

    for k in range(half):
        transfer(k).wait_send()
    for s in range(cols):
        @pl.when(s != col)
        def _():
            col_copy(s, col).wait_send()


def row_exchange(packed, rows, cols, mode_count):
    nodes = packed.shape[1]
    length = cols * nodes
    half = rows // 2
    vmem = pltpu.MemorySpace.VMEM
    flops = 2 * (half + 1) * length * nodes * mode_count + 4 * length * mode_count * mode_count
    return pl.pallas_call(
        functools.partial(row_kernel, rows, cols, mode_count),
        out_shape=jax.ShapeDtypeStruct((mode_count, mode_count), jnp.float32),
        in_specs=[pl.BlockSpec(memory_space=vmem)],
        out_specs=pl.BlockSpec(memory_space=vmem),
        scratch_shapes=[
            pltpu.VMEM((half,) + packed.shape, packed.dtype),
            pltpu.VMEM((cols,) + packed.shape, packed.dtype),
            pltpu.VMEM((3, length, nodes), jnp.float32),
            pltpu.VMEM((length, nodes), jnp.bfloat16),
            pltpu.VMEM((length, mode_count), jnp.float32),
            pltpu.SemaphoreType.DMA((half,)),
            pltpu.SemaphoreType.DMA((half,)),
            pltpu.SemaphoreType.DMA((cols,)),
            pltpu.SemaphoreType.DMA((cols,)),
        ],
        compiler_params=pltpu.CompilerParams(
            collective_id=0, has_side_effects=True, vmem_limit_bytes=48 * 1024 * 1024
        ),
        cost_estimate=pl.CostEstimate(
            flops=flops, transcendentals=(half + 1) * length * nodes, bytes_accessed=4 * 1024 * 1024
        ),
    )(packed)

def gather_all(block, axis, count):
    spread = jnp.broadcast_to(block[None], (count,) + block.shape)
    return lax.all_to_all(spread, axis, 0, 0, tiled=True)


def ar_kernel(rows, cols, y_ref, out_ref, buf_a, buf_b, buf_g, buf_c, red_a, red_b, red_c,
              sa, ra, sb, rb, sg, rg, sc, rc):
    me_r = lax.axis_index("row")
    me_c = lax.axis_index("col")
    buf_a[...] = jnp.zeros_like(buf_a)
    buf_b[...] = jnp.zeros_like(buf_b)
    buf_g[...] = jnp.zeros_like(buf_g)
    buf_c[...] = jnp.zeros_like(buf_c)
    barrier = pltpu.get_barrier_semaphore()
    for p in range(1, cols):
        pl.semaphore_signal(
            barrier, 1, device_id=(me_r, lax.rem(me_c + p, cols)), device_id_type=pl.DeviceIdType.MESH
        )
    for p in range(1, rows):
        pl.semaphore_signal(
            barrier, 1, device_id=(lax.rem(me_r + p, rows), me_c), device_id_type=pl.DeviceIdType.MESH
        )
    pl.semaphore_wait(barrier, cols - 1 + rows - 1)

    def copy(src, dst, send, recv, sem_index, slot, peer):
        return pltpu.make_async_remote_copy(
            src_ref=src,
            dst_ref=dst,
            send_sem=send.at[sem_index],
            recv_sem=recv.at[slot],
            device_id=peer,
            device_id_type=pl.DeviceIdType.MESH,
        )

    def exchange(src_of, dst_of, send, recv, count, me, peer_of):
        for p in range(1, count):
            s = lax.rem(me + p, count)
            copy(src_of(s), dst_of(me), send, recv, s, me, peer_of(s)).start()
        for s in range(count):
            @pl.when(s != me)
            def _():
                copy(src_of(s), dst_of(s), send, recv, s, s, peer_of(s)).wait_recv()

    def finish(src_of, dst_of, send, recv, count, me, peer_of):
        for s in range(count):
            @pl.when(s != me)
            def _():
                copy(src_of(s), dst_of(me), send, recv, s, me, peer_of(s)).wait_send()

    col_peer = lambda s: (me_r, s)
    row_peer = lambda s: (s, me_c)
    col_a = (lambda s: y_ref.at[s], lambda s: buf_a.at[s], sa, ra, cols, me_c, col_peer)
    exchange(*col_a)
    chunk = y_ref[me_c]
    for s in range(cols):
        chunk = chunk + buf_a[s]
    red_a[...] = chunk
    row_b = (lambda s: red_a.at[pl.ds(s, 1)], lambda s: buf_b.at[pl.ds(s, 1)], sb, rb, rows, me_r, row_peer)
    exchange(*row_b)
    piece = red_a[pl.ds(me_r, 1), :] + jnp.sum(buf_b[...], axis=0, keepdims=True)
    red_b[...] = piece
    row_g = (lambda s: red_b, lambda s: buf_g.at[pl.ds(s, 1)], sg, rg, rows, me_r, row_peer)
    exchange(*row_g)
    lines = lax.broadcasted_iota(jnp.int32, chunk.shape, 0)
    total = jnp.where(lines == me_r, jnp.broadcast_to(piece, chunk.shape), buf_g[...])
    red_c[...] = total
    col_c = (lambda s: red_c, lambda s: buf_c.at[s], sc, rc, cols, me_c, col_peer)
    exchange(*col_c)
    for s in range(cols):
        out_ref[s] = jnp.where(s == me_c, total, buf_c[s])
    finish(*col_a)
    finish(*row_b)
    finish(*row_g)
    finish(*col_c)


def all_reduce(matrix, rows, cols):
    pieces = matrix.reshape(cols, rows, -1)
    shape = pieces.shape
    vmem = pltpu.MemorySpace.VMEM
    total = pl.pallas_call(
        functools.partial(ar_kernel, rows, cols),
        out_shape=jax.ShapeDtypeStruct(shape, jnp.float32),
        in_specs=[pl.BlockSpec(memory_space=vmem)],
        out_specs=pl.BlockSpec(memory_space=vmem),
        scratch_shapes=[
            pltpu.VMEM(shape, jnp.float32),
            pltpu.VMEM(shape[1:], jnp.float32),
            pltpu.VMEM(shape[1:], jnp.float32),
            pltpu.VMEM(shape, jnp.float32),
            pltpu.VMEM(shape[1:], jnp.float32),
            pltpu.VMEM((1, shape[2]), jnp.float32),
            pltpu.VMEM(shape[1:], jnp.float32),
            pltpu.SemaphoreType.DMA((cols,)),
            pltpu.SemaphoreType.DMA((cols,)),
            pltpu.SemaphoreType.DMA((rows,)),
            pltpu.SemaphoreType.DMA((rows,)),
            pltpu.SemaphoreType.DMA((rows,)),
            pltpu.SemaphoreType.DMA((rows,)),
            pltpu.SemaphoreType.DMA((cols,)),
            pltpu.SemaphoreType.DMA((cols,)),
        ],
        compiler_params=pltpu.CompilerParams(collective_id=1, has_side_effects=True),
    )(pieces)
    return total.reshape(matrix.shape)

def local(coords, mode_shapes, output_shapes, response_gain):
    rows = lax.axis_size("row")
    cols = lax.axis_size("col")
    mode_count, block_nodes = mode_shapes.shape
    packed = pack_block(coords, mode_shapes)
    partial = row_exchange(packed, rows, cols, mode_count)
    total = all_reduce(partial, rows, cols)
    modal_csd = total + total.T
    real_part = response_gain[0]
    imag_part = response_gain[1]
    weighted = (
        real_part[:, None] * real_part[None, :] + imag_part[:, None] * imag_part[None, :]
    ) * modal_csd
    weighted_high, weighted_low = split_parts(weighted)
    both = jnp.dot(output_shapes, jnp.concatenate([weighted_high, weighted_low], axis=1),
                   preferred_element_type=jnp.float32)
    mapped = both[:, :mode_count] + both[:, mode_count:]
    response_power = jnp.sum(mapped * output_shapes.astype(jnp.float32), axis=1)
    return (response_power, modal_csd)


def solution(mesh):
    in_specs = (P(None, ("row", "col")), P(None, ("row", "col")), P(("row", "col"), None), P())
    out_specs = (P(("row", "col")), P())
    return jax.shard_map(local, mesh=mesh, in_specs=in_specs, out_specs=out_specs, check_vma=False)
```

```python
import functools
import math

import jax
import jax.numpy as jnp
from jax import lax
from jax.experimental import pallas as pl
from jax.experimental.pallas import tpu as pltpu
from jax.sharding import PartitionSpec as P

wave_scale = 0.35 / 64.0


def coherence(left_points, right_points):
    difference = left_points[:, :, None] - right_points[:, None, :]
    squared = jnp.sum(difference * difference, axis=0)
    return jnp.sinc(wave_scale * jnp.sqrt(squared)).astype(jnp.bfloat16)


def split_parts(matrix):
    high_part = matrix.astype(jnp.bfloat16)
    low_part = (matrix - high_part.astype(jnp.float32)).astype(jnp.bfloat16)
    return (high_part, low_part)


def pack_block(coords, mode_shapes):
    wide = coords.astype(jnp.float32)
    high = jnp.floor(wide * (1.0 / 256.0))
    low = wide - 256.0 * high
    pad = jnp.zeros((10, wide.shape[1]), jnp.float32)
    extra = jnp.concatenate([high, low, pad], axis=0).astype(jnp.bfloat16)
    return jnp.concatenate([mode_shapes, extra], axis=0)


def unpack_points(packed, mode_count):
    high = packed[..., mode_count:mode_count + 3, :].astype(jnp.float32)
    low = packed[..., mode_count + 3:mode_count + 6, :].astype(jnp.float32)
    return high * 256.0 + low


CHUNK = 64
SIN_TERMS = [(-1) ** k * math.pi ** (2 * k) / math.factorial(2 * k + 1) / wave_scale for k in range(6)]


def coherence_chunk(dx, dy, dz):
    squared = dx * dx + dy * dy + dz * dz
    safe = jnp.maximum(squared, 1e-30)
    root_inv = lax.rsqrt(safe)
    x = safe * root_inv * wave_scale
    n = jnp.floor(x + 0.5)
    f = x - n
    h = n * 0.5
    sign = 1.0 - 4.0 * (h - jnp.floor(h))
    f2 = f * f
    q = SIN_TERMS[4]
    for term in SIN_TERMS[3::-1]:
        q = q * f2 + term
    return (sign * f) * (q * root_inv)


def block_points(slot_ref, mode_count):
    tail = slot_ref[mode_count:mode_count + 16, :].astype(jnp.float32)
    return [tail[k:k + 1, :] * 256.0 + tail[k + 3:k + 4, :] for k in range(3)]


def accumulate_block(slot_ref, weight, rowpts_ref, out_ref, tile_ref, mode_count):
    bx, by, bz = block_points(slot_ref, mode_count)
    length = tile_ref.shape[0]

    def chunk(c, carry):
        r0 = pl.multiple_of(c * CHUNK, CHUNK)
        dx = rowpts_ref[0, pl.ds(r0, CHUNK), :] - bx
        dy = rowpts_ref[1, pl.ds(r0, CHUNK), :] - by
        dz = rowpts_ref[2, pl.ds(r0, CHUNK), :] - bz
        tile_ref[pl.ds(r0, CHUNK), :] = coherence_chunk(dx, dy, dz).astype(jnp.bfloat16)
        return carry

    lax.fori_loop(0, length // CHUNK, chunk, 0, unroll=4)
    shapes = slot_ref[0:mode_count, :] * weight.astype(jnp.bfloat16)
    product = lax.dot_general(
        tile_ref[...], shapes, (((1,), (1,)), ((), ())), preferred_element_type=jnp.float32
    )
    out_ref[...] += product


def shift_of(j, rows):
    odd = j % 2
    return odd * j + (1 - odd) * (rows - j)


def row_kernel(rows, cols, mode_count, packed_ref, out_ref, recv, colbuf, rowpts_ref, tile_ref, acc_ref,
               send_sems, recv_sems, col_send, col_recv):
    me = lax.axis_index("row")
    col = lax.axis_index("col")
    half = rows // 2
    nodes = packed_ref.shape[1]
    colbuf[...] = jnp.zeros_like(colbuf)
    barrier = pltpu.get_barrier_semaphore()
    for p in range(1, rows):
        pl.semaphore_signal(
            barrier, 1, device_id=(lax.rem(me + p, rows), col), device_id_type=pl.DeviceIdType.MESH
        )
    for p in range(1, cols):
        pl.semaphore_signal(
            barrier, 1, device_id=(me, lax.rem(col + p, cols)), device_id_type=pl.DeviceIdType.MESH
        )
    pl.semaphore_wait(barrier, rows - 1 + cols - 1)

    def col_copy(s, slot):
        return pltpu.make_async_remote_copy(
            src_ref=packed_ref,
            dst_ref=colbuf.at[slot],
            send_sem=col_send.at[s],
            recv_sem=col_recv.at[slot],
            device_id=(me, s),
            device_id_type=pl.DeviceIdType.MESH,
        )

    def transfer(k):
        target = lax.rem(me + rows - shift_of(k + 1, rows), rows)
        return pltpu.make_async_remote_copy(
            src_ref=packed_ref,
            dst_ref=recv.at[k],
            send_sem=send_sems.at[k],
            recv_sem=recv_sems.at[k],
            device_id=(target, col),
            device_id_type=pl.DeviceIdType.MESH,
        )

    for k in range(half):
        transfer(k).start()
    for p in range(1, cols):
        col_copy(lax.rem(col + p, cols), col).start()
    for s in range(cols):
        @pl.when(s != col)
        def _():
            col_copy(s, s).wait_recv()

    eye = (lax.broadcasted_iota(jnp.int32, (nodes, nodes), 0)
           == lax.broadcasted_iota(jnp.int32, (nodes, nodes), 1)).astype(jnp.bfloat16)
    own_tail = packed_ref[mode_count:mode_count + 16, :]
    for s in range(cols):
        tail = jnp.where(s == col, own_tail, colbuf[s, mode_count:mode_count + 16, :])
        moved = lax.dot_general(eye, tail, (((1,), (1,)), ((), ())), preferred_element_type=jnp.float32)
        for k in range(3):
            column = moved[:, k:k + 1] * 256.0 + moved[:, k + 3:k + 4]
            rowpts_ref[k, s * nodes:(s + 1) * nodes, :] = jnp.broadcast_to(column, (nodes, nodes))

    acc_ref[...] = jnp.zeros_like(acc_ref)
    accumulate_block(packed_ref, jnp.float32(0.5), rowpts_ref, acc_ref, tile_ref, mode_count)

    def step(k, carry):
        transfer(k).wait_recv()
        weight = jnp.where(k == half - 1, 0.5, 1.0).astype(jnp.float32)
        accumulate_block(recv.at[k], weight, rowpts_ref, acc_ref, tile_ref, mode_count)
        return carry

    lax.fori_loop(0, half, step, 0)

    own_shapes = packed_ref[0:mode_count, :]
    partial = jnp.zeros(out_ref.shape, jnp.float32)
    for s in range(cols):
        shapes = jnp.where(s == col, own_shapes, colbuf[s, 0:mode_count, :])
        part = acc_ref[s * nodes:(s + 1) * nodes, :]
        high = part.astype(jnp.bfloat16)
        low = (part - high.astype(jnp.float32)).astype(jnp.bfloat16)
        partial = partial + jnp.dot(shapes, high, preferred_element_type=jnp.float32)
        partial = partial + jnp.dot(shapes, low, preferred_element_type=jnp.float32)
    out_ref[...] = partial

    for k in range(half):
        transfer(k).wait_send()
    for s in range(cols):
        @pl.when(s != col)
        def _():
            col_copy(s, col).wait_send()


def row_exchange(packed, rows, cols, mode_count):
    nodes = packed.shape[1]
    length = cols * nodes
    half = rows // 2
    vmem = pltpu.MemorySpace.VMEM
    flops = 2 * (half + 1) * length * nodes * mode_count + 4 * length * mode_count * mode_count
    return pl.pallas_call(
        functools.partial(row_kernel, rows, cols, mode_count),
        out_shape=jax.ShapeDtypeStruct((mode_count, mode_count), jnp.float32),
        in_specs=[pl.BlockSpec(memory_space=vmem)],
        out_specs=pl.BlockSpec(memory_space=vmem),
        scratch_shapes=[
            pltpu.VMEM((half,) + packed.shape, packed.dtype),
            pltpu.VMEM((cols,) + packed.shape, packed.dtype),
            pltpu.VMEM((3, length, nodes), jnp.float32),
            pltpu.VMEM((length, nodes), jnp.bfloat16),
            pltpu.VMEM((length, mode_count), jnp.float32),
            pltpu.SemaphoreType.DMA((half,)),
            pltpu.SemaphoreType.DMA((half,)),
            pltpu.SemaphoreType.DMA((cols,)),
            pltpu.SemaphoreType.DMA((cols,)),
        ],
        compiler_params=pltpu.CompilerParams(
            collective_id=0, has_side_effects=True, vmem_limit_bytes=48 * 1024 * 1024
        ),
        cost_estimate=pl.CostEstimate(
            flops=flops, transcendentals=(half + 1) * length * nodes, bytes_accessed=4 * 1024 * 1024
        ),
    )(packed)

def gather_all(block, axis, count):
    spread = jnp.broadcast_to(block[None], (count,) + block.shape)
    return lax.all_to_all(spread, axis, 0, 0, tiled=True)


def ar_kernel(rows, cols, y_ref, out_ref, buf_a, buf_b, buf_g, buf_c, red_a, red_b, red_c,
              sa, ra, sb, rb, sg, rg, sc, rc):
    me_r = lax.axis_index("row")
    me_c = lax.axis_index("col")
    buf_a[...] = jnp.zeros_like(buf_a)
    buf_b[...] = jnp.zeros_like(buf_b)
    buf_g[...] = jnp.zeros_like(buf_g)
    buf_c[...] = jnp.zeros_like(buf_c)
    barrier = pltpu.get_barrier_semaphore()
    for p in range(1, cols):
        pl.semaphore_signal(
            barrier, 1, device_id=(me_r, lax.rem(me_c + p, cols)), device_id_type=pl.DeviceIdType.MESH
        )
    for p in range(1, rows):
        pl.semaphore_signal(
            barrier, 1, device_id=(lax.rem(me_r + p, rows), me_c), device_id_type=pl.DeviceIdType.MESH
        )
    pl.semaphore_wait(barrier, cols - 1 + rows - 1)

    def copy(src, dst, send, recv, sem_index, slot, peer):
        return pltpu.make_async_remote_copy(
            src_ref=src,
            dst_ref=dst,
            send_sem=send.at[sem_index],
            recv_sem=recv.at[slot],
            device_id=peer,
            device_id_type=pl.DeviceIdType.MESH,
        )

    def exchange(src_of, dst_of, send, recv, count, me, peer_of):
        for p in range(1, count):
            s = lax.rem(me + p, count)
            copy(src_of(s), dst_of(me), send, recv, s, me, peer_of(s)).start()
        for s in range(count):
            @pl.when(s != me)
            def _():
                copy(src_of(s), dst_of(s), send, recv, s, s, peer_of(s)).wait_recv()

    def finish(src_of, dst_of, send, recv, count, me, peer_of):
        for s in range(count):
            @pl.when(s != me)
            def _():
                copy(src_of(s), dst_of(me), send, recv, s, me, peer_of(s)).wait_send()

    col_peer = lambda s: (me_r, s)
    row_peer = lambda s: (s, me_c)
    col_a = (lambda s: y_ref.at[s], lambda s: buf_a.at[s], sa, ra, cols, me_c, col_peer)
    exchange(*col_a)
    chunk = y_ref[me_c]
    for s in range(cols):
        chunk = chunk + buf_a[s]
    red_a[...] = chunk
    row_b = (lambda s: red_a.at[pl.ds(s, 1)], lambda s: buf_b.at[pl.ds(s, 1)], sb, rb, rows, me_r, row_peer)
    exchange(*row_b)
    piece = red_a[pl.ds(me_r, 1), :] + jnp.sum(buf_b[...], axis=0, keepdims=True)
    red_b[...] = piece
    row_g = (lambda s: red_b, lambda s: buf_g.at[pl.ds(s, 1)], sg, rg, rows, me_r, row_peer)
    exchange(*row_g)
    lines = lax.broadcasted_iota(jnp.int32, chunk.shape, 0)
    total = jnp.where(lines == me_r, jnp.broadcast_to(piece, chunk.shape), buf_g[...])
    red_c[...] = total
    col_c = (lambda s: red_c, lambda s: buf_c.at[s], sc, rc, cols, me_c, col_peer)
    exchange(*col_c)
    for s in range(cols):
        out_ref[s] = jnp.where(s == me_c, total, buf_c[s])
    finish(*col_a)
    finish(*row_b)
    finish(*row_g)
    finish(*col_c)


def all_reduce(matrix, rows, cols):
    pieces = matrix.reshape(cols, rows, -1)
    shape = pieces.shape
    vmem = pltpu.MemorySpace.VMEM
    total = pl.pallas_call(
        functools.partial(ar_kernel, rows, cols),
        out_shape=jax.ShapeDtypeStruct(shape, jnp.float32),
        in_specs=[pl.BlockSpec(memory_space=vmem)],
        out_specs=pl.BlockSpec(memory_space=vmem),
        scratch_shapes=[
            pltpu.VMEM(shape, jnp.float32),
            pltpu.VMEM(shape[1:], jnp.float32),
            pltpu.VMEM(shape[1:], jnp.float32),
            pltpu.VMEM(shape, jnp.float32),
            pltpu.VMEM(shape[1:], jnp.float32),
            pltpu.VMEM((1, shape[2]), jnp.float32),
            pltpu.VMEM(shape[1:], jnp.float32),
            pltpu.SemaphoreType.DMA((cols,)),
            pltpu.SemaphoreType.DMA((cols,)),
            pltpu.SemaphoreType.DMA((rows,)),
            pltpu.SemaphoreType.DMA((rows,)),
            pltpu.SemaphoreType.DMA((rows,)),
            pltpu.SemaphoreType.DMA((rows,)),
            pltpu.SemaphoreType.DMA((cols,)),
            pltpu.SemaphoreType.DMA((cols,)),
        ],
        compiler_params=pltpu.CompilerParams(collective_id=1, has_side_effects=True),
    )(pieces)
    return total.reshape(matrix.shape)

def local(coords, mode_shapes, output_shapes, response_gain):
    rows = lax.axis_size("row")
    cols = lax.axis_size("col")
    mode_count, block_nodes = mode_shapes.shape
    packed = pack_block(coords, mode_shapes)
    partial = row_exchange(packed, rows, cols, mode_count)
    total = all_reduce(partial, rows, cols)
    modal_csd = total + total.T
    real_part = response_gain[0]
    imag_part = response_gain[1]
    weighted = (
        real_part[:, None] * real_part[None, :] + imag_part[:, None] * imag_part[None, :]
    ) * modal_csd
    weighted_high, weighted_low = split_parts(weighted)
    mapped = jnp.dot(output_shapes, weighted_high, preferred_element_type=jnp.float32)
    mapped = mapped + jnp.dot(output_shapes, weighted_low, preferred_element_type=jnp.float32)
    response_power = jnp.sum(mapped * output_shapes.astype(jnp.float32), axis=1)
    return (response_power, modal_csd)


def solution(mesh):
    in_specs = (P(None, ("row", "col")), P(None, ("row", "col")), P(("row", "col"), None), P())
    out_specs = (P(("row", "col")), P())
    return jax.shard_map(local, mesh=mesh, in_specs=in_specs, out_specs=out_specs, check_vma=False)
```

```python
import functools
import math

import jax
import jax.numpy as jnp
from jax import lax
from jax.experimental import pallas as pl
from jax.experimental.pallas import tpu as pltpu
from jax.sharding import PartitionSpec as P

wave_scale = 0.35 / 64.0


def coherence(left_points, right_points):
    difference = left_points[:, :, None] - right_points[:, None, :]
    squared = jnp.sum(difference * difference, axis=0)
    return jnp.sinc(wave_scale * jnp.sqrt(squared)).astype(jnp.bfloat16)


def split_parts(matrix):
    high_part = matrix.astype(jnp.bfloat16)
    low_part = (matrix - high_part.astype(jnp.float32)).astype(jnp.bfloat16)
    return (high_part, low_part)


def pack_block(coords, mode_shapes):
    wide = coords.astype(jnp.float32)
    high = jnp.floor(wide * (1.0 / 256.0))
    low = wide - 256.0 * high
    pad = jnp.zeros((10, wide.shape[1]), jnp.float32)
    extra = jnp.concatenate([high, low, pad], axis=0).astype(jnp.bfloat16)
    return jnp.concatenate([mode_shapes, extra], axis=0)


def unpack_points(packed, mode_count):
    high = packed[..., mode_count:mode_count + 3, :].astype(jnp.float32)
    low = packed[..., mode_count + 3:mode_count + 6, :].astype(jnp.float32)
    return high * 256.0 + low


CHUNK = 32
SIN_TERMS = [(-1) ** k * math.pi ** (2 * k) / math.factorial(2 * k + 1) / wave_scale for k in range(6)]


def coherence_chunk(dx, dy, dz):
    squared = dx * dx + dy * dy + dz * dz
    safe = jnp.maximum(squared, 1e-30)
    root_inv = lax.rsqrt(safe)
    x = safe * root_inv * wave_scale
    n = jnp.floor(x + 0.5)
    f = x - n
    h = n * 0.5
    sign = 1.0 - 4.0 * (h - jnp.floor(h))
    f2 = f * f
    q = SIN_TERMS[4]
    for term in SIN_TERMS[3::-1]:
        q = q * f2 + term
    return (sign * f) * (q * root_inv)


def block_points(slot_ref, mode_count):
    tail = slot_ref[mode_count:mode_count + 16, :].astype(jnp.float32)
    return [tail[k:k + 1, :] * 256.0 + tail[k + 3:k + 4, :] for k in range(3)]


def accumulate_block(slot_ref, weight, rowpts_ref, out_ref, tile_ref, mode_count):
    bx, by, bz = block_points(slot_ref, mode_count)
    length = tile_ref.shape[0]

    def chunk(c, carry):
        r0 = pl.multiple_of(c * CHUNK, CHUNK)
        dx = rowpts_ref[0, pl.ds(r0, CHUNK), :] - bx
        dy = rowpts_ref[1, pl.ds(r0, CHUNK), :] - by
        dz = rowpts_ref[2, pl.ds(r0, CHUNK), :] - bz
        tile_ref[pl.ds(r0, CHUNK), :] = coherence_chunk(dx, dy, dz).astype(jnp.bfloat16)
        return carry

    lax.fori_loop(0, length // CHUNK, chunk, 0, unroll=16)
    shapes = slot_ref[0:mode_count, :] * weight.astype(jnp.bfloat16)
    product = lax.dot_general(
        tile_ref[...], shapes, (((1,), (1,)), ((), ())), preferred_element_type=jnp.float32
    )
    out_ref[...] += product


def shift_of(j, rows):
    odd = j % 2
    return odd * j + (1 - odd) * (rows - j)


def row_kernel(rows, cols, mode_count, packed_ref, out_ref, recv, colbuf, rowpts_ref, tile_ref, acc_ref,
               send_sems, recv_sems, col_send, col_recv):
    me = lax.axis_index("row")
    col = lax.axis_index("col")
    half = rows // 2
    nodes = packed_ref.shape[1]
    colbuf[...] = jnp.zeros_like(colbuf)
    barrier = pltpu.get_barrier_semaphore()
    for p in range(1, rows):
        pl.semaphore_signal(
            barrier, 1, device_id=(lax.rem(me + p, rows), col), device_id_type=pl.DeviceIdType.MESH
        )
    for p in range(1, cols):
        pl.semaphore_signal(
            barrier, 1, device_id=(me, lax.rem(col + p, cols)), device_id_type=pl.DeviceIdType.MESH
        )
    pl.semaphore_wait(barrier, rows - 1 + cols - 1)

    def col_copy(s, slot):
        return pltpu.make_async_remote_copy(
            src_ref=packed_ref,
            dst_ref=colbuf.at[slot],
            send_sem=col_send.at[s],
            recv_sem=col_recv.at[slot],
            device_id=(me, s),
            device_id_type=pl.DeviceIdType.MESH,
        )

    def transfer(k):
        target = lax.rem(me + rows - shift_of(k + 1, rows), rows)
        return pltpu.make_async_remote_copy(
            src_ref=packed_ref,
            dst_ref=recv.at[k],
            send_sem=send_sems.at[k],
            recv_sem=recv_sems.at[k],
            device_id=(target, col),
            device_id_type=pl.DeviceIdType.MESH,
        )

    for k in range(half):
        transfer(k).start()
    for p in range(1, cols):
        col_copy(lax.rem(col + p, cols), col).start()
    for s in range(cols):
        @pl.when(s != col)
        def _():
            col_copy(s, s).wait_recv()

    eye = (lax.broadcasted_iota(jnp.int32, (nodes, nodes), 0)
           == lax.broadcasted_iota(jnp.int32, (nodes, nodes), 1)).astype(jnp.bfloat16)
    own_tail = packed_ref[mode_count:mode_count + 16, :]
    for s in range(cols):
        tail = jnp.where(s == col, own_tail, colbuf[s, mode_count:mode_count + 16, :])
        moved = lax.dot_general(eye, tail, (((1,), (1,)), ((), ())), preferred_element_type=jnp.float32)
        for k in range(3):
            column = moved[:, k:k + 1] * 256.0 + moved[:, k + 3:k + 4]
            rowpts_ref[k, s * nodes:(s + 1) * nodes, :] = jnp.broadcast_to(column, (nodes, nodes))

    acc_ref[...] = jnp.zeros_like(acc_ref)
    accumulate_block(packed_ref, jnp.float32(0.5), rowpts_ref, acc_ref, tile_ref, mode_count)

    def step(k, carry):
        transfer(k).wait_recv()
        weight = jnp.where(k == half - 1, 0.5, 1.0).astype(jnp.float32)
        accumulate_block(recv.at[k], weight, rowpts_ref, acc_ref, tile_ref, mode_count)
        return carry

    lax.fori_loop(0, half, step, 0)

    own_shapes = packed_ref[0:mode_count, :]
    partial = jnp.zeros(out_ref.shape, jnp.float32)
    for s in range(cols):
        shapes = jnp.where(s == col, own_shapes, colbuf[s, 0:mode_count, :])
        part = acc_ref[s * nodes:(s + 1) * nodes, :]
        high = part.astype(jnp.bfloat16)
        low = (part - high.astype(jnp.float32)).astype(jnp.bfloat16)
        partial = partial + jnp.dot(shapes, high, preferred_element_type=jnp.float32)
        partial = partial + jnp.dot(shapes, low, preferred_element_type=jnp.float32)
    out_ref[...] = partial

    for k in range(half):
        transfer(k).wait_send()
    for s in range(cols):
        @pl.when(s != col)
        def _():
            col_copy(s, col).wait_send()


def row_exchange(packed, rows, cols, mode_count):
    nodes = packed.shape[1]
    length = cols * nodes
    half = rows // 2
    vmem = pltpu.MemorySpace.VMEM
    flops = 2 * (half + 1) * length * nodes * mode_count + 4 * length * mode_count * mode_count
    return pl.pallas_call(
        functools.partial(row_kernel, rows, cols, mode_count),
        out_shape=jax.ShapeDtypeStruct((mode_count, mode_count), jnp.float32),
        in_specs=[pl.BlockSpec(memory_space=vmem)],
        out_specs=pl.BlockSpec(memory_space=vmem),
        scratch_shapes=[
            pltpu.VMEM((half,) + packed.shape, packed.dtype),
            pltpu.VMEM((cols,) + packed.shape, packed.dtype),
            pltpu.VMEM((3, length, nodes), jnp.float32),
            pltpu.VMEM((length, nodes), jnp.bfloat16),
            pltpu.VMEM((length, mode_count), jnp.float32),
            pltpu.SemaphoreType.DMA((half,)),
            pltpu.SemaphoreType.DMA((half,)),
            pltpu.SemaphoreType.DMA((cols,)),
            pltpu.SemaphoreType.DMA((cols,)),
        ],
        compiler_params=pltpu.CompilerParams(
            collective_id=0, has_side_effects=True, vmem_limit_bytes=48 * 1024 * 1024
        ),
        cost_estimate=pl.CostEstimate(
            flops=flops, transcendentals=(half + 1) * length * nodes, bytes_accessed=4 * 1024 * 1024
        ),
    )(packed)

def gather_all(block, axis, count):
    spread = jnp.broadcast_to(block[None], (count,) + block.shape)
    return lax.all_to_all(spread, axis, 0, 0, tiled=True)


def ar_kernel(rows, cols, y_ref, out_ref, buf_a, buf_b, buf_g, buf_c, red_a, red_b, red_c,
              sa, ra, sb, rb, sg, rg, sc, rc):
    me_r = lax.axis_index("row")
    me_c = lax.axis_index("col")
    buf_a[...] = jnp.zeros_like(buf_a)
    buf_b[...] = jnp.zeros_like(buf_b)
    buf_g[...] = jnp.zeros_like(buf_g)
    buf_c[...] = jnp.zeros_like(buf_c)
    barrier = pltpu.get_barrier_semaphore()
    for p in range(1, cols):
        pl.semaphore_signal(
            barrier, 1, device_id=(me_r, lax.rem(me_c + p, cols)), device_id_type=pl.DeviceIdType.MESH
        )
    for p in range(1, rows):
        pl.semaphore_signal(
            barrier, 1, device_id=(lax.rem(me_r + p, rows), me_c), device_id_type=pl.DeviceIdType.MESH
        )
    pl.semaphore_wait(barrier, cols - 1 + rows - 1)

    def copy(src, dst, send, recv, sem_index, slot, peer):
        return pltpu.make_async_remote_copy(
            src_ref=src,
            dst_ref=dst,
            send_sem=send.at[sem_index],
            recv_sem=recv.at[slot],
            device_id=peer,
            device_id_type=pl.DeviceIdType.MESH,
        )

    def exchange(src_of, dst_of, send, recv, count, me, peer_of):
        for p in range(1, count):
            s = lax.rem(me + p, count)
            copy(src_of(s), dst_of(me), send, recv, s, me, peer_of(s)).start()
        for s in range(count):
            @pl.when(s != me)
            def _():
                copy(src_of(s), dst_of(s), send, recv, s, s, peer_of(s)).wait_recv()

    def finish(src_of, dst_of, send, recv, count, me, peer_of):
        for s in range(count):
            @pl.when(s != me)
            def _():
                copy(src_of(s), dst_of(me), send, recv, s, me, peer_of(s)).wait_send()

    col_peer = lambda s: (me_r, s)
    row_peer = lambda s: (s, me_c)
    col_a = (lambda s: y_ref.at[s], lambda s: buf_a.at[s], sa, ra, cols, me_c, col_peer)
    exchange(*col_a)
    chunk = y_ref[me_c]
    for s in range(cols):
        chunk = chunk + buf_a[s]
    red_a[...] = chunk
    row_b = (lambda s: red_a.at[pl.ds(s, 1)], lambda s: buf_b.at[pl.ds(s, 1)], sb, rb, rows, me_r, row_peer)
    exchange(*row_b)
    piece = red_a[pl.ds(me_r, 1), :] + jnp.sum(buf_b[...], axis=0, keepdims=True)
    red_b[...] = piece
    row_g = (lambda s: red_b, lambda s: buf_g.at[pl.ds(s, 1)], sg, rg, rows, me_r, row_peer)
    exchange(*row_g)
    lines = lax.broadcasted_iota(jnp.int32, chunk.shape, 0)
    total = jnp.where(lines == me_r, jnp.broadcast_to(piece, chunk.shape), buf_g[...])
    red_c[...] = total
    col_c = (lambda s: red_c, lambda s: buf_c.at[s], sc, rc, cols, me_c, col_peer)
    exchange(*col_c)
    for s in range(cols):
        out_ref[s] = jnp.where(s == me_c, total, buf_c[s])
    finish(*col_a)
    finish(*row_b)
    finish(*row_g)
    finish(*col_c)


def all_reduce(matrix, rows, cols):
    pieces = matrix.reshape(cols, rows, -1)
    shape = pieces.shape
    vmem = pltpu.MemorySpace.VMEM
    total = pl.pallas_call(
        functools.partial(ar_kernel, rows, cols),
        out_shape=jax.ShapeDtypeStruct(shape, jnp.float32),
        in_specs=[pl.BlockSpec(memory_space=vmem)],
        out_specs=pl.BlockSpec(memory_space=vmem),
        scratch_shapes=[
            pltpu.VMEM(shape, jnp.float32),
            pltpu.VMEM(shape[1:], jnp.float32),
            pltpu.VMEM(shape[1:], jnp.float32),
            pltpu.VMEM(shape, jnp.float32),
            pltpu.VMEM(shape[1:], jnp.float32),
            pltpu.VMEM((1, shape[2]), jnp.float32),
            pltpu.VMEM(shape[1:], jnp.float32),
            pltpu.SemaphoreType.DMA((cols,)),
            pltpu.SemaphoreType.DMA((cols,)),
            pltpu.SemaphoreType.DMA((rows,)),
            pltpu.SemaphoreType.DMA((rows,)),
            pltpu.SemaphoreType.DMA((rows,)),
            pltpu.SemaphoreType.DMA((rows,)),
            pltpu.SemaphoreType.DMA((cols,)),
            pltpu.SemaphoreType.DMA((cols,)),
        ],
        compiler_params=pltpu.CompilerParams(collective_id=1, has_side_effects=True),
    )(pieces)
    return total.reshape(matrix.shape)

def local(coords, mode_shapes, output_shapes, response_gain):
    rows = lax.axis_size("row")
    cols = lax.axis_size("col")
    mode_count, block_nodes = mode_shapes.shape
    packed = pack_block(coords, mode_shapes)
    partial = row_exchange(packed, rows, cols, mode_count)
    total = all_reduce(partial, rows, cols)
    modal_csd = total + total.T
    real_part = response_gain[0]
    imag_part = response_gain[1]
    weighted = (
        real_part[:, None] * real_part[None, :] + imag_part[:, None] * imag_part[None, :]
    ) * modal_csd
    weighted_high, weighted_low = split_parts(weighted)
    mapped = jnp.dot(output_shapes, weighted_high, preferred_element_type=jnp.float32)
    mapped = mapped + jnp.dot(output_shapes, weighted_low, preferred_element_type=jnp.float32)
    response_power = jnp.sum(mapped * output_shapes.astype(jnp.float32), axis=1)
    return (response_power, modal_csd)


def solution(mesh):
    in_specs = (P(None, ("row", "col")), P(None, ("row", "col")), P(("row", "col"), None), P())
    out_specs = (P(("row", "col")), P())
    return jax.shard_map(local, mesh=mesh, in_specs=in_specs, out_specs=out_specs, check_vma=False)
```
